32 devices in a mesh: coarse: 8 (over z, y), fine: 4 (over x, core).
Axes of the slice: x: 2, y: 2, z: 4, core: 2. Of those that a mesh axis runs over, the one named last changes fastest.
Arguments:
- right_side: float32 [64, 32, 128], P('coarse', 'fine'), may hold values from -6 to 6
- coefficient_index: int32 [64, 32, 128], P('coarse', 'fine'), may hold values from 0 to 15
- material_coefficients: float32 [16], replicated, may hold values from 0.02 to 0.5
- block_cells: int32 [8, 4, 64, 128], P('coarse', 'fine'), may hold values from 0 to 8191, as said below
- block_inverses: float32 [8, 4, 64, 128, 128], P('coarse', 'fine'), as said below
- aggregate_map: int32 [64, 32, 128], P('coarse', 'fine'), may hold values from 0 to 15, as said below
- coarse_diagonal: float32 [8, 4, 16], P('coarse', 'fine'), may hold values from 0.1 to 8
Outputs:
- solution: float32 [64, 32, 128], P('coarse', 'fine')
- residual: float32 [64, 32, 128], P('coarse', 'fine')
- direction: float32 [64, 32, 128], P('coarse', 'fine')
The draws below stay inside these ranges and needn't reach their ends.
Inputs may be any that keep to these rules, and one draw needn't show every extreme that they name: `block_cells`: each device block's 64 x 128 entries list each of its local cell numbers exactly once. `block_inverses`: every 128 x 128 matrix is symmetric positive definite. A cell with third index j has aggregate_map equal to j // 8 - 1, j // 8 or j // 8 + 1.
All inputs are finite; a program needn't handle non-finite values.
Results may differ from the reference program's by a relative error of at most 0.00016.
Values sent between devices are 32-bit elements; how exact they have to be, the bound alone decides.
A program may use at most 64 MiB of HBM per device.

```python
import math
import jax
import jax.numpy as jnp
from jax import lax

AGG = 8
NY = 128
BS = 128
MATERIALS = 16
ITERS = 2
SWEEPS = 4
OWNERS = 8
MEMBERS = 4
NX = 64
NZ = 32
MY = 16
NBLK = 64


def draw_right_side(key, part):
    first = jax.random.fold_in(key, 0)
    xs = jnp.arange(NX, dtype=jnp.float32)[:, None, None]
    zs = jnp.arange(NZ, dtype=jnp.float32)[None, :, None]
    scale = 0.6 + 1.2 * (xs + zs) / (NX + NZ - 2)
    rough = jnp.clip(jax.random.normal(first, (NX, NZ, NY), jnp.float32), -3.3, 3.3)
    return rough * scale


def draw_aggregate_map(key, part):
    ys = jnp.arange(NY, dtype=jnp.int32)[None, None, :]
    moves = jax.random.randint(key, (NX, NZ, NY), -3, 4, dtype=jnp.int32)
    return jnp.clip(ys + moves, 0, NY - 1) // AGG


def draw_block_cells(key, part):
    keys = jax.random.split(key, OWNERS * MEMBERS)
    cells = AGG * AGG * NY

    def one_device(single):
        return jax.random.permutation(single, cells)
    orders = jax.vmap(one_device)(keys)
    return orders.astype(jnp.int32).reshape(OWNERS, MEMBERS, NBLK, BS)


def draw_block_inverses(key, part):
    spread, lowest, highest = (0.3, 0.3, 3.0)

    def one_owner(owner):
        base = jax.random.fold_in(key, owner)
        left, right = jax.random.split(base)
        noise = jax.random.normal(left, (MEMBERS, NBLK, BS, BS), jnp.float32) * (spread / math.sqrt(2.0 * BS))
        eye = jnp.eye(BS, dtype=jnp.float32)
        symmetric = (noise + jnp.swapaxes(noise, -1, -2)) * (1.0 - eye)
        scales = jnp.exp(jax.random.uniform(right, (MEMBERS, NBLK, BS), jnp.float32, math.log(lowest), math.log(highest)))
        root = jnp.sqrt(scales)
        return (eye + symmetric) * root[..., :, None] * root[..., None, :]
    return lax.map(one_owner, jnp.arange(OWNERS, dtype=jnp.int32))


def touch_ends(values, stream_key, least, top_value):
    longest = values.shape.index(max(values.shape))
    spots = []
    for shift in (0, 1):
        where = [jax.random.randint(jax.random.fold_in(stream_key, axis), (), 0, length) for axis, length in enumerate(values.shape)]
        where[longest] = (where[longest] + shift) % values.shape[longest]
        spots.append(tuple(where))
    return values.at[spots[0]].set(least).at[spots[1]].set(top_value)


def block_scale(rng, shape, shards, least, top_value):
    loudness = 1.0
    for position, blocks in shards:
        steps = jax.random.uniform(jax.random.fold_in(jax.random.fold_in(rng, 6), position), (blocks,), jnp.float32, least / len(shards), top_value / len(shards))
        loudness = loudness * jnp.repeat(jnp.exp(steps), shape[position] // blocks).reshape((-1,) + (1,) * (len(shape) - 1 - position))
    return loudness


def setup_inputs(seed: int = 0) -> dict:
    arg_keys = jax.random.split(jax.random.key(seed), 8)
    return {
        "right_side": draw_right_side(jax.random.fold_in(arg_keys[7], 71), 0),
        "coefficient_index": touch_ends(jax.random.randint(arg_keys[1], (NX, NZ, NY), 0, MATERIALS), jax.random.fold_in(arg_keys[1], 1), 0, MATERIALS - 1).astype(jnp.int32),
        "material_coefficients": jnp.clip(jnp.exp(jax.random.uniform(arg_keys[2], (MATERIALS,), jnp.float32, math.log(0.02), math.log(0.5))), 0.02, 0.5),
        "block_cells": draw_block_cells(jax.random.fold_in(arg_keys[7], 71), 0),
        "block_inverses": draw_block_inverses(jax.random.fold_in(arg_keys[7], 71), 0),
        "aggregate_map": draw_aggregate_map(jax.random.fold_in(arg_keys[7], 71), 0),
        "coarse_diagonal": jnp.clip(jnp.exp(math.log(8.0) - 4.3820266 * jax.random.uniform(arg_keys[6], (OWNERS, MEMBERS, MY), jnp.float32) ** block_scale(arg_keys[6], (OWNERS, MEMBERS, MY), ((0, 8), (1, 4)), -0.2, 0.2)), 0.1, 8.0),
    }


omega = 0.8
restrict_scale = 0.25


def neighbours():
    result = []
    for shift_x in (-1, 0, 1):
        for shift_z in (-1, 0, 1):
            for shift_y in (-1, 0, 1):
                reach = abs(shift_x) + abs(shift_z) + abs(shift_y)
                if reach > 0:
                    result.append((shift_x, shift_z, shift_y, 0.5 ** (reach - 1)))
    return result


def window(padded, shift_x, shift_z, shift_y, shape):
    return padded[1 + shift_x:1 + shift_x + shape[0], 1 + shift_z:1 + shift_z + shape[1], 1 + shift_y:1 + shift_y + shape[2]]


def fine_operate(field, kappa):
    padded = jnp.pad(field, 1)
    kappa_wide = jnp.pad(kappa, 1)
    total = jnp.zeros(field.shape, jnp.float32)
    for shift_x, shift_z, shift_y, weight in neighbours():
        near_field = window(padded, shift_x, shift_z, shift_y, field.shape)
        near_kappa = window(kappa_wide, shift_x, shift_z, shift_y, field.shape)
        total = total + (weight * 0.5) * (kappa + near_kappa) * (field - near_field)
    return total


def to_local(field):
    return field.reshape(OWNERS, AGG, MEMBERS, AGG, NY).transpose(0, 2, 1, 3, 4).reshape(OWNERS * MEMBERS, AGG * AGG * NY)


def from_local(flat):
    return flat.reshape(OWNERS, MEMBERS, AGG, AGG, NY).transpose(0, 2, 1, 3, 4).reshape(OWNERS * AGG, MEMBERS * AGG, NY)


def block_apply(residual, block_inverses, block_cells):
    local = to_local(residual)
    orders = block_cells.reshape(OWNERS * MEMBERS, NBLK, BS)
    matrices = block_inverses.reshape(OWNERS * MEMBERS, NBLK, BS, BS)

    def one_device(items):
        vector, order, matrix = items
        picked = vector[order]
        product = jnp.einsum("bij,bj->bi", matrix, picked, precision=lax.Precision.HIGHEST)
        return jnp.zeros(vector.shape, jnp.float32).at[order.reshape(-1)].set(product.reshape(-1))

    return from_local(lax.map(one_device, (local, orders, matrices)))


def segment_numbers(aggregate_map):
    base = jnp.arange(OWNERS * MEMBERS, dtype=jnp.int32) * MY
    return to_local(aggregate_map) + base[:, None]


def coarse_operate(guess, diagonal):
    padded = jnp.pad(guess, 1)
    beside = padded[2:, 1:-1, 1:-1] + padded[:-2, 1:-1, 1:-1]
    beside = beside + padded[1:-1, 2:, 1:-1] + padded[1:-1, :-2, 1:-1]
    beside = beside + padded[1:-1, 1:-1, 2:] + padded[1:-1, 1:-1, :-2]
    return (6.0 + diagonal) * guess - beside


def precondition(residual, block_inverses, block_cells, segments, coarse_diagonal):
    smoothed = block_apply(residual, block_inverses, block_cells)
    sums = jax.ops.segment_sum(to_local(residual).reshape(-1), segments.reshape(-1), num_segments=OWNERS * MEMBERS * MY)
    source = restrict_scale * sums.reshape(OWNERS, MEMBERS, MY)
    guess = jnp.zeros(source.shape, jnp.float32)
    for sweep in range(SWEEPS):
        guess = guess + omega * (source - coarse_operate(guess, coarse_diagonal)) / (6.0 + coarse_diagonal)
    correction = from_local(guess.reshape(-1)[segments])
    return smoothed + correction


def reference(right_side, coefficient_index, material_coefficients, block_cells, block_inverses, aggregate_map, coarse_diagonal):
    kappa = material_coefficients[coefficient_index]
    segments = segment_numbers(aggregate_map)
    solution = jnp.zeros(right_side.shape, jnp.float32)
    residual = right_side
    smoothed = precondition(residual, block_inverses, block_cells, segments, coarse_diagonal)
    current = jnp.sum(residual * smoothed)
    search = smoothed
    for step in range(ITERS):
        image = fine_operate(search, kappa)
        alpha = current / jnp.sum(search * image)
        solution = solution + alpha * search
        residual = residual - alpha * image
        smoothed = precondition(residual, block_inverses, block_cells, segments, coarse_diagonal)
        following = jnp.sum(residual * smoothed)
        search = smoothed + (following / current) * search
        current = following
    return solution, residual, search
```

```python
import functools

import jax
import jax.numpy as jnp
from jax import lax
from jax.experimental import pallas as pl
from jax.experimental.pallas import tpu as pltpu
from jax.sharding import PartitionSpec as P

ROUNDS = 3
SWEEPS = 4
omega = 0.8
restrict_scale = 0.25
MESH = pl.DeviceIdType.MESH
SUB = 8
LANES = 128
MAIN = 8
XLO, XHI, ZLO, ZHI, CORNER = 8, 9, 10, 11, 12
SLOTS = 13
AHEAD = 8
REACH = SWEEPS
DIRECTIONS = ((-1, 0), (1, 0), (0, -1), (0, 1), (-1, -1), (-1, 1), (1, -1), (1, 1))


def take(values, lanes):
    return jnp.take_along_axis(values, lanes, axis=1, mode="promise_in_bounds")


def full(row):
    return jnp.broadcast_to(row, (SUB, LANES))


def total_of(values):
    return jnp.sum(jnp.sum(values, axis=0, keepdims=True), axis=1, keepdims=True)


def kernel(
    owners, members, r_hbm, cidx_hbm, table_hbm, cells_hbm, inv_ref, amap_hbm, diag_hbm,
    x_out, r_out, p_out,
    r_ref, cidx_ref, table_ref, cells_ref, amap_ref, diag_ref, in_sems,
    mats, halves, rot, key_in, lane_in, key_out, lane_out, moved,
    first_ext, first_cols, first_corner_src, first_corners,
    w_ext, w_cols, w_corner_src, w_corners,
    b_ext, b_cols, b_corner_src, b_corners,
    kap, amaps, p_ext, u_ext, q_cur, v_cur, kt, small,
    row_src, rows,
    mat_sems, send_sems, recv_sems, row_send, row_recv,
):
    count = owners * members
    o = lax.axis_index("coarse")
    m = lax.axis_index("fine")
    me = o * members + m
    groups = cells_ref.shape[0]
    sub = lax.broadcasted_iota(jnp.int32, (SUB, LANES), 0)
    lane = lax.broadcasted_iota(jnp.int32, (SUB, LANES), 1)
    zero = jnp.zeros((SUB, LANES), jnp.float32)

    in_copies = [
        pltpu.make_async_copy(src, dst, in_sems.at[at])
        for at, (src, dst) in enumerate(
            (
                (cells_hbm, cells_ref),
                (r_hbm, r_ref),
                (amap_hbm, amap_ref),
                (cidx_hbm, cidx_ref),
                (table_hbm, table_ref),
                (diag_hbm, diag_ref),
            )
        )
    ]
    for copy in in_copies:
        copy.start()
    def mat_copy(u):
        part = pl.ds(u * SUB, SUB)
        return pltpu.make_async_copy(inv_ref.at[part], mats.at[part], mat_sems.at[u])

    for u in range(groups):
        mat_copy(u).start()

    for slot in range(MAIN, CORNER):
        for f in range(2):
            first_ext[slot, f] = zero
        w_ext[slot, 0] = zero
        b_ext[slot, 0] = zero
    for c in range(4):
        first_corners[c] = zero
        w_corners[c] = zero
        b_corners[c] = zero
    rows[...] = jnp.zeros(rows.shape, jnp.float32)

    barrier = pltpu.get_barrier_semaphore()
    reach_o = max(REACH, -(-(owners - 1) // 3))
    reach_m = max(REACH, -(-(members - 1) // 3))
    low_o, high_o = jnp.maximum(o - reach_o, 0), jnp.minimum(o + reach_o, owners - 1) + 1
    low_m, high_m = jnp.maximum(m - reach_m, 0), jnp.minimum(m + reach_m, members - 1) + 1
    near = (high_o - low_o) * (high_m - low_m) - 1

    def spans(size, reach):
        return {min(at + reach, size - 1) - max(at - reach, 0) + 1 for at in range(size)}

    near_counts = sorted(
        {a * b - 1 for a in spans(owners, reach_o) for b in spans(members, reach_m)}
    )

    def for_near(act):
        def one_owner(to_o, carry):
            def one(to_m, inner):
                @pl.when((to_o != o) | (to_m != m))
                def _():
                    act({"coarse": to_o, "fine": to_m})

                return inner

            return lax.fori_loop(low_m, high_m, one, carry)

        lax.fori_loop(low_o, high_o, one_owner, 0)

    def other(d):
        t = lax.rem(me + d, count)
        return {"coarse": lax.div(t, members), "fine": lax.rem(t, members)}

    for_near(
        lambda device: pl.semaphore_signal(barrier, inc=1, device_id=device, device_id_type=MESH)
    )

    in_copies[0].wait()

    def keys_of(source):
        row = lax.shift_right_logical(source, 7)
        turn = (jnp.bitwise_and(row, 7) - sub) & 7
        return jnp.bitwise_and(row, ~7) + turn, jnp.bitwise_and(source, 127)

    for g in range(groups):
        key, lanes = keys_of(cells_ref[g])
        key_in[g] = key
        lane_in[g] = lanes

    def load_turns(values):
        for g in range(len(values)):
            for turn in range(SUB):
                rot[g * SUB + turn] = (
                    values[g] if turn == 0 else pltpu.roll(values[g], SUB - turn, 0)
                )

    def permuted(key, lanes):
        parts = [zero, zero]
        for k in range(groups * SUB):
            parts[k % 2] = jnp.where(key == k, take(rot[k], lanes), parts[k % 2])
        return parts[0] + parts[1]

    tall = lax.broadcasted_iota(jnp.int32, (groups * SUB, LANES), 0)
    taller = lax.broadcasted_iota(jnp.int32, (LANES, LANES), 0)
    wide = lax.broadcasted_iota(jnp.int32, (groups * SUB, LANES), 1).astype(jnp.float32)

    def find_one(g, carry):
        block = cells_ref[g]
        for b in range(SUB):
            source = block[b : b + 1, :]
            hit = tall == jnp.broadcast_to(lax.shift_right_logical(source, 7), tall.shape)
            number = (g * SUB + b).astype(jnp.float32)
            left = jnp.concatenate(
                [jnp.where(hit, number, 0.0), jnp.where(hit, wide, 0.0)], axis=0
            ).astype(jnp.bfloat16)
            right = jnp.where(
                taller == jnp.broadcast_to(jnp.bitwise_and(source, 127), taller.shape), 1.0, 0.0
            ).astype(jnp.bfloat16)
            carry = carry + lax.dot_general(
                left, right, (((1,), (1,)), ((), ())), preferred_element_type=jnp.float32
            )
        return carry

    def find(turn, carry):
        return find_one(2 * turn + 1, find_one(2 * turn, carry))

    found = lax.fori_loop(
        0, groups // 2, find, jnp.zeros((2 * groups * SUB, LANES), jnp.float32)
    ).astype(jnp.int32)
    for g in range(groups):
        block = found[g * SUB : (g + 1) * SUB]
        place = found[(groups + g) * SUB : (groups + g + 1) * SUB]
        key, lanes = keys_of(block * LANES + place)
        key_out[g] = key
        lane_out[g] = lanes

    for copy in in_copies[1:]:
        copy.wait()
    small[...] = jnp.zeros(small.shape, jnp.float32)
    small[0, 0:1, 0 : table_ref.shape[1]] = table_ref[...]
    small[1, 0:1, 0 : diag_ref.shape[2]] = diag_ref[0]
    boxes = diag_ref.shape[2]
    table = full(small[0, 0:1, :])
    for x in range(MAIN):
        first_ext[x, 0] = take(table, cidx_ref[x])
        first_ext[x, 1] = (amap_ref[x] + 1).astype(jnp.float32)
        amaps[x] = amap_ref[x]

    def split(values):
        high = values.astype(jnp.bfloat16)
        low = (values - high.astype(jnp.float32)).astype(jnp.bfloat16)
        return high, low

    def block_apply(values, done_with_dot, first=False):
        load_turns(values)

        def some(turn, carry):
            dot, picked = carry
            if first:
                for at in range(AHEAD):
                    mat_copy(turn * AHEAD + at).wait()
            for at in range(AHEAD):
                u = turn * AHEAD + at
                if first:
                    for b in range(SUB):
                        high, low = split(mats[u * SUB + b])
                        halves[u * SUB + b, :, 0:LANES] = high
                        halves[u * SUB + b, :, LANES : 2 * LANES] = low
                ahead = lax.rem(u + 1, groups)
                upcoming = permuted(key_in[ahead], lane_in[ahead])
                left = jnp.concatenate(split(picked), axis=0)
                product = zero
                for b in range(SUB):
                    both = jnp.dot(left, halves[u * SUB + b], preferred_element_type=jnp.float32)
                    line = both[:SUB, :LANES] + (both[SUB:, :LANES] + both[:SUB, LANES:])
                    line = line + both[SUB:, LANES:]
                    product = jnp.where(sub == b, line, product)
                moved[u] = product
                dot = dot + picked * product
                picked = upcoming
            return dot, picked

        dot, _ = lax.fori_loop(
            0, groups // AHEAD, some, (zero, permuted(key_in[0], lane_in[0]))
        )
        if done_with_dot is not None:
            done_with_dot(total_of(dot))
        load_turns([moved[g] for g in range(groups)])

        def back(g, carry):
            for step in range(AHEAD):
                at = g * AHEAD + step
                moved[at] = permuted(key_out[at], lane_out[at])
            return carry

        lax.fori_loop(0, groups // AHEAD, back, 0)
        return [moved[g] for g in range(groups)]

    base = lax.shift_right_logical(lane, 3)

    def restrict(values):
        sums = []
        for move in (-1, 0, 1):
            total = zero
            for x in range(MAIN):
                total = total + jnp.where(amaps[x] - base == move, values[x], 0.0)
            sums.append(total)
        total = pltpu.roll(sums[0], LANES - SUB, 1) + sums[1] + pltpu.roll(sums[2], SUB, 1)
        total = full(jnp.sum(total, axis=0, keepdims=True))
        for step in (1, 2, 4):
            total = total + pltpu.roll(total, LANES - step, 1)
        return jnp.where(lane < boxes, restrict_scale * take(total, (lane * SUB) & 127), 0.0)

    def row_copy(index, src, dst, device):
        return pltpu.make_async_remote_copy(
            src_ref=src, dst_ref=dst, send_sem=row_send.at[index], recv_sem=row_recv.at[index],
            device_id=device, device_id_type=MESH,
        )

    def send_rows(index, row, everywhere=False):
        row_src[index] = row[0:1, :]
        rows[index, me] = row[0:1, :]
        if everywhere:

            def one(d, carry):
                row_copy(index, row_src.at[index], rows.at[index, me], other(d)).start()
                return carry

            lax.fori_loop(1, count, one, 0)
        else:
            for_near(
                lambda device: row_copy(
                    index, row_src.at[index], rows.at[index, me], device
                ).start()
            )

    def wait_rows(index, everywhere=False):
        def wait_for(number):
            part = rows.at[index, pl.ds(0, number)]
            both = row_copy(index, part, part, other(1))
            both.wait_send()
            both.wait_recv()

        if everywhere:
            wait_for(count - 1)
        else:
            for number in near_counts:
                pl.when(near == number)(functools.partial(wait_for, number))
        return rows[index].reshape(count, LANES)

    def scalar(row, number):
        at = 2 * boxes + number
        return row[:, at : at + 1]

    def with_scalar(row, number, value):
        return jnp.where(lane == 2 * boxes + number, full(value), row)

    def edge_rows(values, z):
        result = zero
        for x in range(MAIN):
            result = jnp.where(sub == x, full(values[x][z : z + 1, :]), result)
        return result

    def halo_copies(ring, ext, cols, corner_src, corners):
        copies = []
        for number, (do, dm) in enumerate(DIRECTIONS):
            if dm == 0:
                src = ext.at[MAIN - 1 if do == 1 else 0]
                dst = ext.at[XLO if do == 1 else XHI]
            elif do == 0:
                src = cols.at[1 if dm == 1 else 0]
                dst = ext.at[ZLO if dm == 1 else ZHI]
            else:
                at = 2 * (0 if do == 1 else 1) + (0 if dm == 1 else 1)
                src = corner_src.at[at]
                dst = corners.at[at]
            to_o, to_m = o + do, m + dm
            from_o, from_m = o - do, m - dm
            goes = (to_o >= 0) & (to_o < owners) & (to_m >= 0) & (to_m < members)
            comes = (from_o >= 0) & (from_o < owners) & (from_m >= 0) & (from_m < members)
            copies.append(
                (
                    goes,
                    comes,
                    pltpu.make_async_remote_copy(
                        src_ref=src, dst_ref=dst,
                        send_sem=send_sems.at[ring, number], recv_sem=recv_sems.at[ring, number],
                        device_id={"coarse": to_o, "fine": to_m}, device_id_type=MESH,
                    ),
                )
            )
        return copies

    def start_halo(ring, fields, ext, cols, corner_src, corners):
        packs = [zero, zero, zero, zero]
        for f, values in enumerate(fields):
            cols[0, f] = edge_rows(values, 0)
            cols[1, f] = edge_rows(values, SUB - 1)
            for side_x in range(2):
                for side_z in range(2):
                    at = 2 * side_x + side_z
                    x = MAIN - 1 if side_x == 0 else 0
                    z = SUB - 1 if side_z == 0 else 0
                    packs[at] = jnp.where(sub == f, full(values[x][z : z + 1, :]), packs[at])
        for at in range(4):
            corner_src[at] = packs[at]
        copies = halo_copies(ring, ext, cols, corner_src, corners)
        for goes, _, copy in copies:
            pl.when(goes)(copy.start)
        return copies

    def wait_halo(copies):
        for goes, comes, copy in copies:
            pl.when(goes)(copy.wait_send)
            pl.when(comes)(copy.wait_recv)

    def corner_rows(corners, f):
        result = zero
        for at in range(4):
            result = jnp.where(sub == at, full(corners[at][f : f + 1, :]), result)
        return result

    def shifted(values, low, high):
        before = jnp.where(sub == 0, full(low), pltpu.roll(values, 1, 0))
        after = jnp.where(sub == SUB - 1, full(high), pltpu.roll(values, SUB - 1, 0))
        return values + 0.5 * (before + after)

    def smear(v):
        planes = [v[XLO]] + [v[x] for x in range(MAIN)] + [v[XHI]]
        corner = v[CORNER]
        low = shifted(v[ZLO], corner[0:1, :], corner[2:3, :])
        high = shifted(v[ZHI], corner[1:2, :], corner[3:4, :])
        result = []
        for x in range(MAIN):
            mid = planes[x + 1] + 0.5 * (planes[x] + planes[x + 2])
            mid = shifted(mid, low[x : x + 1, :], high[x : x + 1, :])
            before = jnp.where(lane == 0, 0.0, pltpu.roll(mid, 1, 1))
            after = jnp.where(lane == LANES - 1, 0.0, pltpu.roll(mid, LANES - 1, 1))
            result.append(mid + 0.5 * (before + after))
        return result

    node = lax.broadcasted_iota(jnp.int32, (count, LANES), 0)
    node_lane = lax.broadcasted_iota(jnp.int32, (count, LANES), 1)
    member = lax.rem(node, members)

    def coarse_solve(source, inverse):
        guess = omega * source * inverse
        for sweep in range(SWEEPS - 1):
            beside = pltpu.roll(guess, 1, 1) + pltpu.roll(guess, LANES - 1, 1)
            beside = beside + jnp.where(member == 0, 0.0, pltpu.roll(guess, 1, 0))
            beside = beside + jnp.where(
                member == members - 1, 0.0, pltpu.roll(guess, count - 1, 0)
            )
            beside = beside + jnp.where(node < members, 0.0, pltpu.roll(guess, members, 0))
            beside = beside + jnp.where(
                node >= count - members, 0.0, pltpu.roll(guess, count - members, 0)
            )
            guess = (1.0 - omega) * guess + omega * (source + beside) * inverse
        return guess

    def only_boxes(values):
        return jnp.where(node_lane < boxes, values, 0.0)

    def dot_of(left, right):
        total = zero
        for x in range(MAIN):
            total = total + left[x] * right[x]
        return total_of(total)

    start = [r_ref[x] for x in range(MAIN)]
    spread = full(small[1, 0:1, :])
    spread = jnp.where(lane < boxes, 1.0 / jnp.where(lane < boxes, 6.0 + spread, 1.0), 0.0)
    spread = pltpu.roll(spread, boxes, 1)
    first_row = restrict(start) + spread
    pl.semaphore_wait(barrier, near)
    send_rows(0, first_row)
    kappas = [first_ext[x, 0] for x in range(MAIN)]
    maps = [first_ext[x, 1] for x in range(MAIN)]
    first_copies = start_halo(
        0, [kappas, maps], first_ext, first_cols, first_corner_src, first_corners
    )
    w = block_apply(start, None, True)
    for x in range(MAIN):
        w_ext[x, 0] = w[x]
    w_copies = start_halo(1, [w], w_ext, w_cols, w_corner_src, w_corners)
    gathered = wait_rows(0)
    inverse = only_boxes(pltpu.roll(gathered, LANES - boxes, 1))
    guess = coarse_solve(only_boxes(gathered), inverse)

    def guess_rows(guess):
        picks = {}
        for do in (-1, 0, 1):
            for dm in (-1, 0, 1):
                wanted = me + do * members + dm
                picks[(do, dm)] = full(
                    jnp.sum(jnp.where(node == wanted, guess, 0.0), axis=0, keepdims=True)
                )
        return picks

    def add_coarse(values, guess):
        picks = guess_rows(guess)
        result = []
        for x in range(MAIN):
            result.append(values[x] + take(picks[(0, 0)], amaps[x]))
        for slot, way in ((XLO, (-1, 0)), (XHI, (1, 0)), (ZLO, (0, -1)), (ZHI, (0, 1))):
            result.append(values[slot] + take(picks[way], amaps[slot]))
        corner = zero
        for at, way in enumerate(((-1, -1), (-1, 1), (1, -1), (1, 1))):
            corner = jnp.where(sub == at, take(picks[way], amaps[CORNER]), corner)
        result.append(values[CORNER] + corner)
        return result

    wait_halo(first_copies)
    for slot in range(SLOTS):
        if slot == CORNER:
            parts = [corner_rows(first_corners, f) for f in range(2)]
        else:
            parts = [first_ext[slot, f] for f in range(2)]
        kap[slot] = parts[0]
        if slot >= MAIN:
            amaps[slot] = (parts[1].astype(jnp.int32) + (LANES - 1)) & (LANES - 1)
    smeared = smear([kap[s] for s in range(SLOTS)])
    for x in range(MAIN):
        kt[x] = 8.0 * kap[x] + smeared[x]

    def arrived(copies, ext, corners):
        wait_halo(copies)
        return [ext[s, 0] for s in range(CORNER)] + [corner_rows(corners, 0)]

    def fine_operate(field, result):
        flat = smear(field)
        steep = smear([field[s] * kap[s] for s in range(SLOTS)])
        for x in range(MAIN):
            result[x] = field[x] * kt[x] - kap[x] * flat[x] - steep[x]

    z = add_coarse(arrived(w_copies, w_ext, w_corners), guess)
    for slot in range(SLOTS):
        p_ext[slot] = z[slot]
    fine_operate(z, q_cur)
    image = [q_cur[x] for x in range(MAIN)]
    send_rows(1, restrict(image))
    bq = block_apply(image, None)
    for x in range(MAIN):
        b_ext[x, 0] = bq[x]
    b_copies = start_halo(2, [bq], b_ext, b_cols, b_corner_src, b_corners)
    r_dot_p = dot_of(r_ref, p_ext)
    p_dot_q = dot_of(p_ext, q_cur)
    guess = coarse_solve(only_boxes(wait_rows(1)), inverse)
    u = add_coarse(arrived(b_copies, b_ext, b_corners), guess)
    for x in range(MAIN):
        u_ext[x] = u[x]
    fine_operate(u, v_cur)
    image = [v_cur[x] for x in range(MAIN)]
    row = restrict(image) + spread
    row = with_scalar(row, 0, r_dot_p)
    row = with_scalar(row, 1, p_dot_q)
    row = with_scalar(row, 2, dot_of(q_cur, u_ext))
    row = with_scalar(row, 3, dot_of(u_ext, v_cur))

    def last_send(dot):
        send_rows(2, with_scalar(row, 4, dot), True)

    bv = block_apply(image, last_send)
    gathered = wait_rows(2, True)
    sums = jnp.sum(gathered, axis=0, keepdims=True)
    inverse = only_boxes(pltpu.roll(gathered, LANES - boxes, 1))
    source = only_boxes(gathered)
    guess = coarse_solve(source, inverse)
    mu = [scalar(sums, number) for number in range(5)]
    mu[4] = mu[4] + total_of(source * guess) * (1.0 / restrict_scale)
    alpha0 = mu[0] / mu[1]
    norm1 = mu[0] - 2.0 * alpha0 * mu[1] + alpha0 * alpha0 * mu[2]
    grow = 1.0 + norm1 / mu[0]
    curve = grow * grow * mu[1] - 2.0 * grow * alpha0 * mu[2] + alpha0 * alpha0 * mu[3]
    alpha1 = norm1 / curve
    cross = grow * mu[1] - (1.0 + grow) * alpha0 * mu[2] + alpha0 * alpha0 * mu[3]
    square = grow * grow * mu[2] - 2.0 * grow * alpha0 * mu[3] + alpha0 * alpha0 * mu[4]
    norm2 = norm1 - 2.0 * alpha1 * cross + alpha1 * alpha1 * square
    beta1 = full(norm2 / norm1)
    alpha0, alpha1, grow = full(alpha0), full(alpha1), full(grow)
    own = full(jnp.sum(jnp.where(node == me, guess, 0.0), axis=0, keepdims=True))
    for x in range(MAIN):
        p0, q0, u0, v0 = p_ext[x], q_cur[x], u_ext[x], v_cur[x]
        t0 = bv[x] + take(own, amaps[x])
        p1 = grow * p0 - alpha0 * u0
        q1 = grow * q0 - alpha0 * v0
        x_out[x] = alpha0 * p0 + alpha1 * p1
        r_out[x] = r_ref[x] - alpha0 * q0 - alpha1 * q1
        z2 = p0 - alpha0 * u0 - alpha1 * (grow * u0 - alpha0 * t0)
        p_out[x] = z2 + beta1 * p1


def emit(x_ref, r_ref, p_ref, x_out, r_out, p_out, sems):
    pairs = ((x_ref, x_out), (r_ref, r_out), (p_ref, p_out))
    copies = [pltpu.make_async_copy(a, b, sems.at[i]) for i, (a, b) in enumerate(pairs)]
    for copy in copies:
        copy.start()
    for copy in copies:
        copy.wait()


def shards(
    owners, members, right_side, coefficient_index, material_coefficients, block_cells,
    block_inverses, aggregate_map, coarse_diagonal,
):
    blocks, side = block_cells.shape[2], block_cells.shape[3]
    assert right_side.shape == (SUB, SUB, LANES) and side == LANES and blocks == SUB * SUB
    count = owners * members
    groups = blocks // SUB
    field = jax.ShapeDtypeStruct(right_side.shape, jnp.float32)
    vmem = pl.BlockSpec(memory_space=pltpu.VMEM)
    f32, i32 = jnp.float32, jnp.int32
    tile = (SUB, LANES)
    hbm = pl.BlockSpec(memory_space=pltpu.HBM)
    results = pl.pallas_call(
        functools.partial(kernel, owners, members),
        out_shape=(field, field, field),
        in_specs=[hbm] * 7,
        out_specs=(vmem, vmem, vmem),
        scratch_shapes=[
            pltpu.VMEM(right_side.shape, f32),
            pltpu.VMEM(right_side.shape, i32),
            pltpu.VMEM((1,) + material_coefficients.shape, f32),
            pltpu.VMEM((groups,) + tile, i32),
            pltpu.VMEM(right_side.shape, i32),
            pltpu.VMEM(coarse_diagonal.shape, f32),
            pltpu.SemaphoreType.DMA((6,)),
            pltpu.VMEM((blocks, side, side), f32),
            pltpu.VMEM((blocks, side, 2 * side), jnp.bfloat16),
            pltpu.VMEM((blocks,) + tile, f32),
            pltpu.VMEM((groups,) + tile, i32),
            pltpu.VMEM((groups,) + tile, i32),
            pltpu.VMEM((groups,) + tile, i32),
            pltpu.VMEM((groups,) + tile, i32),
            pltpu.VMEM((groups,) + tile, f32),
            pltpu.VMEM((CORNER, 2) + tile, f32),
            pltpu.VMEM((2, 2) + tile, f32),
            pltpu.VMEM((4,) + tile, f32),
            pltpu.VMEM((4,) + tile, f32),
            pltpu.VMEM((CORNER, 1) + tile, f32),
            pltpu.VMEM((2, 1) + tile, f32),
            pltpu.VMEM((4,) + tile, f32),
            pltpu.VMEM((4,) + tile, f32),
            pltpu.VMEM((CORNER, 1) + tile, f32),
            pltpu.VMEM((2, 1) + tile, f32),
            pltpu.VMEM((4,) + tile, f32),
            pltpu.VMEM((4,) + tile, f32),
            pltpu.VMEM((SLOTS,) + tile, f32),
            pltpu.VMEM((SLOTS,) + tile, i32),
            pltpu.VMEM((SLOTS,) + tile, f32),
            pltpu.VMEM((MAIN,) + tile, f32),
            pltpu.VMEM((MAIN,) + tile, f32),
            pltpu.VMEM((MAIN,) + tile, f32),
            pltpu.VMEM((MAIN,) + tile, f32),
            pltpu.VMEM((2,) + tile, f32),
            pltpu.VMEM((ROUNDS, 1, LANES), f32),
            pltpu.VMEM((ROUNDS, count, 1, LANES), f32),
            pltpu.SemaphoreType.DMA((groups,)),
            pltpu.SemaphoreType.DMA((ROUNDS, len(DIRECTIONS))),
            pltpu.SemaphoreType.DMA((ROUNDS, len(DIRECTIONS))),
            pltpu.SemaphoreType.DMA((ROUNDS,)),
            pltpu.SemaphoreType.DMA((ROUNDS,)),
        ],
        compiler_params=pltpu.CompilerParams(
            collective_id=0, has_side_effects=True, vmem_limit_bytes=32 << 20
        ),
    )(
        *(pltpu.with_memory_space_constraint(a, pltpu.HBM) for a in (
        right_side,
        coefficient_index,
        material_coefficients.reshape(1, -1),
        block_cells.reshape(groups, SUB, LANES),
        block_inverses.reshape(blocks, side, side),
        aggregate_map,
        coarse_diagonal,
        ))
    )
    return pl.pallas_call(
        emit,
        out_shape=(field, field, field),
        in_specs=[vmem] * 3,
        out_specs=(hbm,) * 3,
        scratch_shapes=[pltpu.SemaphoreType.DMA((3,))],
        compiler_params=pltpu.CompilerParams(vmem_limit_bytes=1 << 20),
    )(*results)


def solution(mesh):
    three = P("coarse", "fine", None)
    return jax.shard_map(
        functools.partial(shards, mesh.shape["coarse"], mesh.shape["fine"]),
        mesh=mesh,
        in_specs=(
            three,
            three,
            P(),
            P("coarse", "fine", None, None),
            P("coarse", "fine", None, None, None),
            three,
            three,
        ),
        out_specs=(three, three, three),
        check_vma=False,
    )
```

```python
import functools

import jax
import jax.numpy as jnp
from jax import lax
from jax.experimental import pallas as pl
from jax.experimental.pallas import tpu as pltpu
from jax.sharding import PartitionSpec as P

RINGS = 3
ROUNDS = 4
UNROLLED = 64
SWEEPS = 4
omega = 0.8
restrict_scale = 0.25
MESH = pl.DeviceIdType.MESH
SUB = 8
LANES = 128
MAIN = 8
XLO, XHI, ZLO, ZHI, CORNER = 8, 9, 10, 11, 12
SLOTS = 13
REACH = SWEEPS
DIRECTIONS = ((-1, 0), (1, 0), (0, -1), (0, 1), (-1, -1), (-1, 1), (1, -1), (1, 1))


def take(values, lanes):
    return jnp.take_along_axis(values, lanes, axis=1, mode="promise_in_bounds")


def full(row):
    return jnp.broadcast_to(row, (SUB, LANES))


def total_of(values):
    return jnp.sum(jnp.sum(values, axis=0, keepdims=True), axis=1, keepdims=True)


def kernel(
    owners, members, r_hbm, cidx_hbm, table_hbm, cells_hbm, inv_ref, amap_hbm, diag_hbm,
    x_out, r_out, p_out,
    r_ref, cidx_ref, table_ref, cells_ref, amap_ref, diag_ref, in_sems,
    mats, halves, rot, key_in, lane_in, key_out, lane_out, moved,
    first_ext, first_cols, first_corner_src, first_corners,
    w_ext, w_cols, w_corner_src, w_corners,
    b_ext, b_cols, b_corner_src, b_corners,
    kap, amaps, p_ext, u_ext, q_cur, v_cur, kt, small,
    row_src, rows, picks,
    mat_sems, send_sems, recv_sems, row_send, row_recv,
):
    count = owners * members
    o = lax.axis_index("coarse")
    m = lax.axis_index("fine")
    me = o * members + m
    groups = cells_ref.shape[0]
    sub = lax.broadcasted_iota(jnp.int32, (SUB, LANES), 0)
    lane = lax.broadcasted_iota(jnp.int32, (SUB, LANES), 1)
    zero = jnp.zeros((SUB, LANES), jnp.float32)

    in_copies = [
        pltpu.make_async_copy(src, dst, in_sems.at[at])
        for at, (src, dst) in enumerate(
            (
                (cells_hbm, cells_ref),
                (r_hbm, r_ref),
                (amap_hbm, amap_ref),
                (cidx_hbm, cidx_ref),
                (table_hbm, table_ref),
                (diag_hbm, diag_ref),
            )
        )
    ]
    for copy in in_copies:
        copy.start()
    def mat_copy(u):
        part = pl.ds(u * SUB, SUB)
        return pltpu.make_async_copy(inv_ref.at[part], mats.at[part], mat_sems.at[u])

    for slot in range(MAIN, CORNER):
        for f in range(2):
            first_ext[slot, f] = zero
        w_ext[slot, 0] = zero
        b_ext[slot, 0] = zero
    for c in range(4):
        first_corners[c] = zero
        w_corners[c] = zero
        b_corners[c] = zero
    rows[...] = jnp.zeros(rows.shape, jnp.float32)

    barrier = pltpu.get_barrier_semaphore()
    reach_o = max(REACH, -(-(owners - 1) // 3))
    reach_m = max(REACH, -(-(members - 1) // 3))
    low_o, high_o = jnp.maximum(o - reach_o, 0), jnp.minimum(o + reach_o, owners - 1) + 1
    low_m, high_m = jnp.maximum(m - reach_m, 0), jnp.minimum(m + reach_m, members - 1) + 1
    near = (high_o - low_o) * (high_m - low_m) - 1

    def spans(size, reach):
        return {min(at + reach, size - 1) - max(at - reach, 0) + 1 for at in range(size)}

    near_counts = sorted(
        {a * b - 1 for a in spans(owners, reach_o) for b in spans(members, reach_m)}
    )

    def other(d):
        t = lax.rem(me + d, count)
        return {"coarse": lax.div(t, members), "fine": lax.rem(t, members)}

    def for_all(act):
        if count <= UNROLLED:
            for d in range(1, count):
                act(other(d))
        else:

            def one(d, carry):
                act(other(d))
                return carry

            lax.fori_loop(1, count, one, 0)

    def for_near(act):
        def one(device):
            to_o, to_m = device["coarse"], device["fine"]
            close = None
            if reach_o < owners - 1:
                close = (to_o >= low_o) & (to_o < high_o)
            if reach_m < members - 1:
                close_m = (to_m >= low_m) & (to_m < high_m)
                close = close_m if close is None else close & close_m
            if close is None:
                act(device)
            else:
                pl.when(close)(functools.partial(act, device))

        for_all(one)

    for_near(
        lambda device: pl.semaphore_signal(barrier, inc=1, device_id=device, device_id_type=MESH)
    )

    for u in range(groups):
        mat_copy(u).start()
    for copy in in_copies:
        copy.wait()

    def keys_of(source):
        row = lax.shift_right_logical(source, 7)
        turn = (jnp.bitwise_and(row, 7) - sub) & 7
        return jnp.bitwise_and(row, ~7) + turn, jnp.bitwise_and(source, 127)

    for g in range(groups):
        key, lanes = keys_of(cells_ref[g])
        key_in[g] = key
        lane_in[g] = lanes

    def load_turns(values):
        for g in range(len(values)):
            for turn in range(SUB):
                rot[g * SUB + turn] = (
                    values[g] if turn == 0 else pltpu.roll(values[g], SUB - turn, 0)
                )

    def permuted(key, lanes):
        parts = [zero, zero]
        for k in range(groups * SUB):
            parts[k % 2] = jnp.where(key == k, take(rot[k], lanes), parts[k % 2])
        return parts[0] + parts[1]

    both_lanes = 2 * LANES
    tall = lax.broadcasted_iota(jnp.int32, (groups * SUB, both_lanes), 0)
    taller = lax.broadcasted_iota(jnp.int32, (LANES, both_lanes), 0)
    place = lax.broadcasted_iota(jnp.int32, (groups * SUB, both_lanes), 1)
    second = jnp.where(place >= LANES, 1.0, 0.0)

    def narrow(values):
        return values.astype(jnp.float32).astype(jnp.bfloat16)

    tall, taller, place = narrow(tall), narrow(taller), narrow(place & (LANES - 1))
    one, nothing = jnp.bfloat16(1), jnp.bfloat16(0)
    found = jnp.zeros((2 * groups * SUB, LANES), jnp.float32)
    for g in range(groups):
        block = cells_ref[g]
        for b in range(0, SUB, 2):
            source = jnp.concatenate([block[b : b + 1, :], block[b + 1 : b + 2, :]], axis=1)
            row = narrow(lax.shift_right_logical(source, 7))
            hit = tall == jnp.broadcast_to(row, tall.shape)
            number = (second + (g * SUB + b)).astype(jnp.bfloat16)
            left = jnp.concatenate(
                [jnp.where(hit, number, nothing), jnp.where(hit, place, nothing)], axis=0
            )
            column = narrow(jnp.bitwise_and(source, LANES - 1))
            right = jnp.where(taller == jnp.broadcast_to(column, taller.shape), one, nothing)
            found = found + lax.dot_general(
                left, right, (((1,), (1,)), ((), ())), preferred_element_type=jnp.float32
            )
    found = found.astype(jnp.int32)
    for g in range(groups):
        block = found[g * SUB : (g + 1) * SUB]
        spot = found[(groups + g) * SUB : (groups + g + 1) * SUB]
        key, lanes = keys_of(block * LANES + spot)
        key_out[g] = key
        lane_out[g] = lanes

    small[...] = jnp.zeros(small.shape, jnp.float32)
    small[0, 0:1, 0 : table_ref.shape[1]] = table_ref[...]
    small[1, 0:1, 0 : diag_ref.shape[2]] = diag_ref[0]
    boxes = diag_ref.shape[2]
    table = full(small[0, 0:1, :])
    for x in range(MAIN):
        first_ext[x, 0] = take(table, cidx_ref[x])
        first_ext[x, 1] = (amap_ref[x] + 1).astype(jnp.float32)
        amaps[x] = amap_ref[x]

    def split(values):
        high = values.astype(jnp.bfloat16)
        low = (values - high.astype(jnp.float32)).astype(jnp.bfloat16)
        return high, low

    odd = (sub & 1) == 1

    def pick(values, keep):
        load_turns(values)
        for g in range(groups):
            keep[g] = permuted(key_in[g], lane_in[g])

    def block_apply(picked_of, done_with_dot, first=False):
        dot = zero
        picked = picked_of(0)
        for u in range(groups):
            if first:
                mat_copy(u).wait()
                for b in range(SUB):
                    high, low = split(mats[u * SUB + b])
                    pair, part = (u * SUB + b) // 2, pl.ds((b % 2) * LANES, LANES)
                    halves[pair, part, 0:LANES] = high
                    halves[pair, part, LANES : 2 * LANES] = low
            upcoming = picked_of(u + 1) if u + 1 < groups else None
            sides = []
            for keep_odd in (False, True):
                side = jnp.where(odd == keep_odd, picked, 0.0)
                sides.append(jnp.concatenate(split(side), axis=0))
            left = jnp.concatenate(sides, axis=1)
            product = zero
            for j in range(SUB // 2):
                both = jnp.dot(
                    left, halves[u * SUB // 2 + j], preferred_element_type=jnp.float32
                )
                line = both[:SUB, :LANES] + (both[SUB:, :LANES] + both[:SUB, LANES:])
                line = line + both[SUB:, LANES:]
                product = jnp.where(lax.shift_right_logical(sub, 1) == j, line, product)
            moved[u] = product
            if done_with_dot is not None:
                dot = dot + picked * product
            picked = upcoming
        if done_with_dot is not None:
            done_with_dot(total_of(dot))
        load_turns([moved[g] for g in range(groups)])
        for g in range(groups):
            moved[g] = permuted(key_out[g], lane_out[g])
        return [moved[g] for g in range(groups)]

    def solve(values, done_with_dot=None):
        load_turns(values)
        return block_apply(lambda g: permuted(key_in[g], lane_in[g]), done_with_dot)

    base = lax.shift_right_logical(lane, 3)

    def restrict(values):
        sums = []
        for move in (-1, 0, 1):
            total = zero
            for x in range(MAIN):
                total = total + jnp.where(amaps[x] - base == move, values[x], 0.0)
            sums.append(total)
        total = pltpu.roll(sums[0], LANES - SUB, 1) + sums[1] + pltpu.roll(sums[2], SUB, 1)
        total = full(jnp.sum(total, axis=0, keepdims=True))
        for step in (1, 2, 4):
            total = total + pltpu.roll(total, LANES - step, 1)
        return jnp.where(lane < boxes, restrict_scale * take(total, (lane * SUB) & 127), 0.0)

    def row_copy(index, src, dst, device):
        return pltpu.make_async_remote_copy(
            src_ref=src, dst_ref=dst, send_sem=row_send.at[index], recv_sem=row_recv.at[index],
            device_id=device, device_id_type=MESH,
        )

    def send_rows(index, row, everywhere=False):
        row_src[index] = row[0:1, :]
        rows[index, me] = row[0:1, :]
        (for_all if everywhere else for_near)(
            lambda device: row_copy(index, row_src.at[index], rows.at[index, me], device).start()
        )

    def wait_rows(index, everywhere=False):
        def wait_for(number):
            part = rows.at[index, pl.ds(0, number)]
            both = row_copy(index, part, part, other(1))
            both.wait_send()
            both.wait_recv()

        if everywhere:
            wait_for(count - 1)
        else:
            for number in near_counts:
                pl.when(near == number)(functools.partial(wait_for, number))
        return rows[index].reshape(count, LANES)

    def scalar(row, number):
        at = 2 * boxes + number
        return row[:, at : at + 1]

    def with_scalar(row, number, value):
        return jnp.where(lane == 2 * boxes + number, full(value), row)

    def edge_rows(values, z):
        result = zero
        for x in range(MAIN):
            result = jnp.where(sub == x, full(values[x][z : z + 1, :]), result)
        return result

    def halo_copies(ring, ext, cols, corner_src, corners):
        copies = []
        for do, dm in DIRECTIONS:
            if dm == 0:
                src = ext.at[MAIN - 1 if do == 1 else 0]
                dst = ext.at[XLO if do == 1 else XHI]
            elif do == 0:
                src = cols.at[1 if dm == 1 else 0]
                dst = ext.at[ZLO if dm == 1 else ZHI]
            else:
                at = 2 * (0 if do == 1 else 1) + (0 if dm == 1 else 1)
                src = corner_src.at[at]
                dst = corners.at[at]
            to_o, to_m = o + do, m + dm
            goes = (to_o >= 0) & (to_o < owners) & (to_m >= 0) & (to_m < members)
            copies.append(
                (
                    goes,
                    pltpu.make_async_remote_copy(
                        src_ref=src, dst_ref=dst,
                        send_sem=send_sems.at[ring], recv_sem=recv_sems.at[ring],
                        device_id={"coarse": to_o, "fine": to_m}, device_id_type=MESH,
                    ),
                )
            )
        return copies

    def start_halo(ring, fields, ext, cols, corner_src, corners):
        packs = [zero, zero, zero, zero]
        for f, values in enumerate(fields):
            cols[0, f] = edge_rows(values, 0)
            cols[1, f] = edge_rows(values, SUB - 1)
            for side_x in range(2):
                for side_z in range(2):
                    at = 2 * side_x + side_z
                    x = MAIN - 1 if side_x == 0 else 0
                    z = SUB - 1 if side_z == 0 else 0
                    packs[at] = jnp.where(sub == f, full(values[x][z : z + 1, :]), packs[at])
        for at in range(4):
            corner_src[at] = packs[at]
        copies = halo_copies(ring, ext, cols, corner_src, corners)
        for goes, copy in copies:
            pl.when(goes)(copy.start)

    beside_o = (o > 0).astype(jnp.int32) + (o < owners - 1).astype(jnp.int32)
    beside_m = (m > 0).astype(jnp.int32) + (m < members - 1).astype(jnp.int32)

    def wait_halo(ring, fields):
        for number_o in range(3):
            for number_m in range(3):
                tiles = fields * (number_o + number_m) + number_o * number_m
                if tiles == 0:
                    continue

                @pl.when((beside_o == number_o) & (beside_m == number_m))
                def _(tiles=tiles):
                    part = rot.at[pl.ds(0, tiles)]
                    both = pltpu.make_async_remote_copy(
                        src_ref=part, dst_ref=part,
                        send_sem=send_sems.at[ring], recv_sem=recv_sems.at[ring],
                        device_id=other(1), device_id_type=MESH,
                    )
                    both.wait_send()
                    both.wait_recv()

    def corner_rows(corners, f):
        result = zero
        for at in range(4):
            result = jnp.where(sub == at, full(corners[at][f : f + 1, :]), result)
        return result

    def shifted(values, low, high):
        before = jnp.where(sub == 0, full(low), pltpu.roll(values, 1, 0))
        after = jnp.where(sub == SUB - 1, full(high), pltpu.roll(values, SUB - 1, 0))
        return values + 0.5 * (before + after)

    def smear(v):
        planes = [v[XLO]] + [v[x] for x in range(MAIN)] + [v[XHI]]
        corner = v[CORNER]
        low = shifted(v[ZLO], corner[0:1, :], corner[2:3, :])
        high = shifted(v[ZHI], corner[1:2, :], corner[3:4, :])
        result = []
        for x in range(MAIN):
            mid = planes[x + 1] + 0.5 * (planes[x] + planes[x + 2])
            mid = shifted(mid, low[x : x + 1, :], high[x : x + 1, :])
            before = jnp.where(lane == 0, 0.0, pltpu.roll(mid, 1, 1))
            after = jnp.where(lane == LANES - 1, 0.0, pltpu.roll(mid, LANES - 1, 1))
            result.append(mid + 0.5 * (before + after))
        return result

    node = lax.broadcasted_iota(jnp.int32, (count, LANES), 0)
    node_lane = lax.broadcasted_iota(jnp.int32, (count, LANES), 1)
    member = lax.rem(node, members)

    def coarse_solve(source, inverse):
        guess = omega * source * inverse
        for sweep in range(SWEEPS - 1):
            beside = pltpu.roll(guess, 1, 1) + pltpu.roll(guess, LANES - 1, 1)
            beside = beside + jnp.where(member == 0, 0.0, pltpu.roll(guess, 1, 0))
            beside = beside + jnp.where(
                member == members - 1, 0.0, pltpu.roll(guess, count - 1, 0)
            )
            beside = beside + jnp.where(node < members, 0.0, pltpu.roll(guess, members, 0))
            beside = beside + jnp.where(
                node >= count - members, 0.0, pltpu.roll(guess, count - members, 0)
            )
            guess = (1.0 - omega) * guess + omega * (source + beside) * inverse
        return guess

    def only_boxes(values):
        return jnp.where(node_lane < boxes, values, 0.0)

    def dot_of(left, right):
        total = zero
        for x in range(MAIN):
            total = total + left[x] * right[x]
        return total_of(total)

    start = [r_ref[x] for x in range(MAIN)]
    spread = full(small[1, 0:1, :])
    spread = jnp.where(lane < boxes, 1.0 / jnp.where(lane < boxes, 6.0 + spread, 1.0), 0.0)
    spread = pltpu.roll(spread, boxes, 1)
    first_row = restrict(start) + spread
    pick(start, picks)
    pl.semaphore_wait(barrier, near)
    send_rows(0, first_row)
    kappas = [first_ext[x, 0] for x in range(MAIN)]
    maps = [first_ext[x, 1] for x in range(MAIN)]
    start_halo(
        0, [kappas, maps], first_ext, first_cols, first_corner_src, first_corners
    )
    w = block_apply(lambda g: picks[g], None, True)
    for x in range(MAIN):
        w_ext[x, 0] = w[x]
    start_halo(1, [w], w_ext, w_cols, w_corner_src, w_corners)
    gathered = wait_rows(0)
    inverse = only_boxes(pltpu.roll(gathered, LANES - boxes, 1))
    guess = coarse_solve(only_boxes(gathered), inverse)

    def guess_rows(guess):
        picks = {}
        for do in (-1, 0, 1):
            for dm in (-1, 0, 1):
                wanted = me + do * members + dm
                picks[(do, dm)] = full(
                    jnp.sum(jnp.where(node == wanted, guess, 0.0), axis=0, keepdims=True)
                )
        return picks

    def add_coarse(values, guess):
        picks = guess_rows(guess)
        result = []
        for x in range(MAIN):
            result.append(values[x] + take(picks[(0, 0)], amaps[x]))
        for slot, way in ((XLO, (-1, 0)), (XHI, (1, 0)), (ZLO, (0, -1)), (ZHI, (0, 1))):
            result.append(values[slot] + take(picks[way], amaps[slot]))
        corner = zero
        for at, way in enumerate(((-1, -1), (-1, 1), (1, -1), (1, 1))):
            corner = jnp.where(sub == at, take(picks[way], amaps[CORNER]), corner)
        result.append(values[CORNER] + corner)
        return result

    wait_halo(0, 2)
    for slot in range(SLOTS):
        if slot == CORNER:
            parts = [corner_rows(first_corners, f) for f in range(2)]
        else:
            parts = [first_ext[slot, f] for f in range(2)]
        kap[slot] = parts[0]
        if slot >= MAIN:
            amaps[slot] = (parts[1].astype(jnp.int32) + (LANES - 1)) & (LANES - 1)
    smeared = smear([kap[s] for s in range(SLOTS)])
    for x in range(MAIN):
        kt[x] = 8.0 * kap[x] + smeared[x]

    def arrived(ring, ext, corners):
        wait_halo(ring, 1)
        return [ext[s, 0] for s in range(CORNER)] + [corner_rows(corners, 0)]

    def fine_operate(field, result):
        flat = smear(field)
        steep = smear([field[s] * kap[s] for s in range(SLOTS)])
        for x in range(MAIN):
            result[x] = field[x] * kt[x] - kap[x] * flat[x] - steep[x]

    z = add_coarse(arrived(1, w_ext, w_corners), guess)
    for slot in range(SLOTS):
        p_ext[slot] = z[slot]
    fine_operate(z, q_cur)
    image = [q_cur[x] for x in range(MAIN)]
    send_rows(1, restrict(image))
    bq = solve(image)
    for x in range(MAIN):
        b_ext[x, 0] = bq[x]
    start_halo(2, [bq], b_ext, b_cols, b_corner_src, b_corners)
    r_dot_p = dot_of(r_ref, p_ext)
    p_dot_q = dot_of(p_ext, q_cur)
    guess = coarse_solve(only_boxes(wait_rows(1)), inverse)
    u = add_coarse(arrived(2, b_ext, b_corners), guess)
    for x in range(MAIN):
        u_ext[x] = u[x]
    fine_operate(u, v_cur)
    image = [v_cur[x] for x in range(MAIN)]
    row = restrict(image) + spread
    row = with_scalar(row, 0, r_dot_p)
    row = with_scalar(row, 1, p_dot_q)
    row = with_scalar(row, 2, dot_of(q_cur, u_ext))
    row = with_scalar(row, 3, dot_of(u_ext, v_cur))
    send_rows(2, row, True)
    bv = solve(image, lambda dot: send_rows(3, full(dot), True))
    gathered = wait_rows(2, True)
    sums = jnp.sum(gathered, axis=0, keepdims=True)
    inverse = only_boxes(pltpu.roll(gathered, LANES - boxes, 1))
    source = only_boxes(gathered)
    guess = coarse_solve(source, inverse)
    coarse_part = full(total_of(source * guess) * (1.0 / restrict_scale))
    mu = [full(scalar(sums, number)) for number in range(4)]
    turn = 1.0 / mu[1]
    alpha0 = mu[0] * turn
    grow = alpha0 * mu[2] * turn
    curve = 1.0 / (alpha0 * alpha0 * mu[3] - grow * grow * mu[1])
    alpha1 = mu[0] * (grow - 1.0) * curve
    part = grow * grow * mu[2] - 2.0 * grow * alpha0 * mu[3] + alpha0 * alpha0 * coarse_part
    scale = alpha1 * curve
    own = full(jnp.sum(jnp.where(node == me, guess, 0.0), axis=0, keepdims=True))
    ahead, onward = [], []
    for x in range(MAIN):
        p0, q0, u0, v0 = p_ext[x], q_cur[x], u_ext[x], v_cur[x]
        t0 = bv[x] + take(own, amaps[x])
        p1 = grow * p0 - alpha0 * u0
        q1 = grow * q0 - alpha0 * v0
        x_out[x] = alpha0 * p0 + alpha1 * p1
        r_out[x] = r_ref[x] - alpha0 * q0 - alpha1 * q1
        ahead.append(p0 - alpha0 * u0 - alpha1 * (grow * u0 - alpha0 * t0))
        onward.append(p1)
    last = full(jnp.sum(wait_rows(3, True), axis=0, keepdims=True))
    beta1 = scale * (part + alpha0 * alpha0 * last) - 1.0
    for x in range(MAIN):
        p_out[x] = ahead[x] + beta1 * onward[x]


def emit(x_ref, r_ref, p_ref, x_out, r_out, p_out, sems):
    pairs = ((x_ref, x_out), (r_ref, r_out), (p_ref, p_out))
    copies = [pltpu.make_async_copy(a, b, sems.at[i]) for i, (a, b) in enumerate(pairs)]
    for copy in copies:
        copy.start()
    for copy in copies:
        copy.wait()


def shards(
    owners, members, right_side, coefficient_index, material_coefficients, block_cells,
    block_inverses, aggregate_map, coarse_diagonal,
):
    blocks, side = block_cells.shape[2], block_cells.shape[3]
    assert right_side.shape == (SUB, SUB, LANES) and side == LANES and blocks == SUB * SUB
    count = owners * members
    groups = blocks // SUB
    field = jax.ShapeDtypeStruct(right_side.shape, jnp.float32)
    vmem = pl.BlockSpec(memory_space=pltpu.VMEM)
    f32, i32 = jnp.float32, jnp.int32
    tile = (SUB, LANES)
    hbm = pl.BlockSpec(memory_space=pltpu.HBM)
    results = pl.pallas_call(
        functools.partial(kernel, owners, members),
        out_shape=(field, field, field),
        in_specs=[hbm] * 7,
        out_specs=(vmem, vmem, vmem),
        scratch_shapes=[
            pltpu.VMEM(right_side.shape, f32),
            pltpu.VMEM(right_side.shape, i32),
            pltpu.VMEM((1,) + material_coefficients.shape, f32),
            pltpu.VMEM((groups,) + tile, i32),
            pltpu.VMEM(right_side.shape, i32),
            pltpu.VMEM(coarse_diagonal.shape, f32),
            pltpu.SemaphoreType.DMA((6,)),
            pltpu.VMEM((blocks, side, side), f32),
            pltpu.VMEM((blocks // 2, 2 * side, 2 * side), jnp.bfloat16),
            pltpu.VMEM((blocks,) + tile, f32),
            pltpu.VMEM((groups,) + tile, i32),
            pltpu.VMEM((groups,) + tile, i32),
            pltpu.VMEM((groups,) + tile, i32),
            pltpu.VMEM((groups,) + tile, i32),
            pltpu.VMEM((groups,) + tile, f32),
            pltpu.VMEM((CORNER, 2) + tile, f32),
            pltpu.VMEM((2, 2) + tile, f32),
            pltpu.VMEM((4,) + tile, f32),
            pltpu.VMEM((4,) + tile, f32),
            pltpu.VMEM((CORNER, 1) + tile, f32),
            pltpu.VMEM((2, 1) + tile, f32),
            pltpu.VMEM((4,) + tile, f32),
            pltpu.VMEM((4,) + tile, f32),
            pltpu.VMEM((CORNER, 1) + tile, f32),
            pltpu.VMEM((2, 1) + tile, f32),
            pltpu.VMEM((4,) + tile, f32),
            pltpu.VMEM((4,) + tile, f32),
            pltpu.VMEM((SLOTS,) + tile, f32),
            pltpu.VMEM((SLOTS,) + tile, i32),
            pltpu.VMEM((SLOTS,) + tile, f32),
            pltpu.VMEM((MAIN,) + tile, f32),
            pltpu.VMEM((MAIN,) + tile, f32),
            pltpu.VMEM((MAIN,) + tile, f32),
            pltpu.VMEM((MAIN,) + tile, f32),
            pltpu.VMEM((2,) + tile, f32),
            pltpu.VMEM((ROUNDS, 1, LANES), f32),
            pltpu.VMEM((ROUNDS, count, 1, LANES), f32),
            pltpu.VMEM((groups,) + tile, f32),
            pltpu.SemaphoreType.DMA((groups,)),
            pltpu.SemaphoreType.DMA((RINGS,)),
            pltpu.SemaphoreType.DMA((RINGS,)),
            pltpu.SemaphoreType.DMA((ROUNDS,)),
            pltpu.SemaphoreType.DMA((ROUNDS,)),
        ],
        compiler_params=pltpu.CompilerParams(
            collective_id=0, has_side_effects=True, vmem_limit_bytes=32 << 20
        ),
    )(
        *(pltpu.with_memory_space_constraint(a, pltpu.HBM) for a in (
        right_side,
        coefficient_index,
        material_coefficients.reshape(1, -1),
        block_cells.reshape(groups, SUB, LANES),
        block_inverses.reshape(blocks, side, side),
        aggregate_map,
        coarse_diagonal,
        ))
    )
    return pl.pallas_call(
        emit,
        out_shape=(field, field, field),
        in_specs=[vmem] * 3,
        out_specs=(hbm,) * 3,
        scratch_shapes=[pltpu.SemaphoreType.DMA((3,))],
        compiler_params=pltpu.CompilerParams(vmem_limit_bytes=1 << 20),
    )(*results)


def solution(mesh):
    three = P("coarse", "fine", None)
    return jax.shard_map(
        functools.partial(shards, mesh.shape["coarse"], mesh.shape["fine"]),
        mesh=mesh,
        in_specs=(
            three,
            three,
            P(),
            P("coarse", "fine", None, None),
            P("coarse", "fine", None, None, None),
            three,
            three,
        ),
        out_specs=(three, three, three),
        check_vma=False,
    )
```

```python
import functools

import jax
import jax.numpy as jnp
from jax import lax
from jax.experimental import pallas as pl
from jax.experimental.pallas import tpu as pltpu
from jax.sharding import PartitionSpec as P

RINGS = 3
ROUNDS = 4
UNROLLED = 64
SWEEPS = 4
omega = 0.8
restrict_scale = 0.25
MESH = pl.DeviceIdType.MESH
SUB = 8
LANES = 128
MAIN = 8
XLO, XHI, ZLO, ZHI, CORNER = 8, 9, 10, 11, 12
SLOTS = 13
REACH = SWEEPS
DIRECTIONS = ((-1, 0), (1, 0), (0, -1), (0, 1), (-1, -1), (-1, 1), (1, -1), (1, 1))


def take(values, lanes):
    return jnp.take_along_axis(values, lanes, axis=1, mode="promise_in_bounds")


def full(row):
    return jnp.broadcast_to(row, (SUB, LANES))


def total_of(values):
    return jnp.sum(jnp.sum(values, axis=0, keepdims=True), axis=1, keepdims=True)


def kernel(
    owners, members, r_hbm, cidx_hbm, table_hbm, cells_hbm, inv_ref, amap_hbm, diag_hbm,
    x_out, r_out, p_out,
    r_ref, cidx_ref, table_ref, cells_ref, amap_ref, diag_ref, in_sems,
    mats, halves, rot, key_in, lane_in, key_out, lane_out, moved,
    first_ext, first_cols, first_corner_src, first_corners,
    w_ext, w_cols, w_corner_src, w_corners,
    b_ext, b_cols, b_corner_src, b_corners,
    kap, amaps, p_ext, u_ext, q_cur, v_cur, kt, small,
    row_src, rows, picks,
    mat_sems, send_sems, recv_sems, row_send, row_recv,
):
    count = owners * members
    o = lax.axis_index("coarse")
    m = lax.axis_index("fine")
    me = o * members + m
    groups = cells_ref.shape[0]
    sub = lax.broadcasted_iota(jnp.int32, (SUB, LANES), 0)
    lane = lax.broadcasted_iota(jnp.int32, (SUB, LANES), 1)
    zero = jnp.zeros((SUB, LANES), jnp.float32)

    in_copies = [
        pltpu.make_async_copy(src, dst, in_sems.at[at])
        for at, (src, dst) in enumerate(
            (
                (cells_hbm, cells_ref),
                (r_hbm, r_ref),
                (amap_hbm, amap_ref),
                (cidx_hbm, cidx_ref),
                (table_hbm, table_ref),
                (diag_hbm, diag_ref),
            )
        )
    ]
    for copy in in_copies:
        copy.start()
    def mat_copy(u):
        part = pl.ds(u * SUB, SUB)
        return pltpu.make_async_copy(inv_ref.at[part], mats.at[part], mat_sems.at[u])

    for slot in range(MAIN, CORNER):
        for f in range(2):
            first_ext[slot, f] = zero
        w_ext[slot, 0] = zero
        b_ext[slot, 0] = zero
    for c in range(4):
        first_corners[c] = zero
        w_corners[c] = zero
        b_corners[c] = zero
    rows[...] = jnp.zeros(rows.shape, jnp.float32)

    barrier = pltpu.get_barrier_semaphore()
    reach_o = max(REACH, -(-(owners - 1) // 3))
    reach_m = max(REACH, -(-(members - 1) // 3))
    low_o, high_o = jnp.maximum(o - reach_o, 0), jnp.minimum(o + reach_o, owners - 1) + 1
    low_m, high_m = jnp.maximum(m - reach_m, 0), jnp.minimum(m + reach_m, members - 1) + 1
    near = (high_o - low_o) * (high_m - low_m) - 1

    def spans(size, reach):
        return {min(at + reach, size - 1) - max(at - reach, 0) + 1 for at in range(size)}

    near_counts = sorted(
        {a * b - 1 for a in spans(owners, reach_o) for b in spans(members, reach_m)}
    )

    def other(d):
        t = lax.rem(me + d, count)
        return {"coarse": lax.div(t, members), "fine": lax.rem(t, members)}

    def for_all(act):
        if count <= UNROLLED:
            for d in range(1, count):
                act(other(d))
        else:

            def one(d, carry):
                act(other(d))
                return carry

            lax.fori_loop(1, count, one, 0)

    def for_near(act):
        def one(device):
            to_o, to_m = device["coarse"], device["fine"]
            close = None
            if reach_o < owners - 1:
                close = (to_o >= low_o) & (to_o < high_o)
            if reach_m < members - 1:
                close_m = (to_m >= low_m) & (to_m < high_m)
                close = close_m if close is None else close & close_m
            if close is None:
                act(device)
            else:
                pl.when(close)(functools.partial(act, device))

        for_all(one)

    for_near(
        lambda device: pl.semaphore_signal(barrier, inc=1, device_id=device, device_id_type=MESH)
    )

    for u in range(groups):
        mat_copy(u).start()
    for copy in in_copies:
        copy.wait()

    def keys_of(source):
        row = lax.shift_right_logical(source, 7)
        turn = (jnp.bitwise_and(row, 7) - sub) & 7
        return jnp.bitwise_and(row, ~7) + turn, jnp.bitwise_and(source, 127)

    for g in range(groups):
        key, lanes = keys_of(cells_ref[g])
        key_in[g] = key
        lane_in[g] = lanes

    def load_turns(values):
        for g in range(len(values)):
            for turn in range(SUB):
                rot[g * SUB + turn] = (
                    values[g] if turn == 0 else pltpu.roll(values[g], SUB - turn, 0)
                )

    def permuted(key, lanes):
        parts = [zero, zero]
        for k in range(groups * SUB):
            parts[k % 2] = jnp.where(key == k, take(rot[k], lanes), parts[k % 2])
        return parts[0] + parts[1]

    both_lanes = 2 * LANES
    tall = lax.broadcasted_iota(jnp.int32, (groups * SUB, both_lanes), 0)
    taller = lax.broadcasted_iota(jnp.int32, (LANES, both_lanes), 0)
    place = lax.broadcasted_iota(jnp.int32, (groups * SUB, both_lanes), 1)
    second = jnp.where(place >= LANES, 1.0, 0.0)

    def narrow(values):
        return values.astype(jnp.float32).astype(jnp.bfloat16)

    tall, taller, place = narrow(tall), narrow(taller), narrow(place & (LANES - 1))
    one, nothing = jnp.bfloat16(1), jnp.bfloat16(0)
    found = jnp.zeros((2 * groups * SUB, LANES), jnp.float32)
    for g in range(groups):
        block = cells_ref[g]
        for b in range(0, SUB, 2):
            source = jnp.concatenate([block[b : b + 1, :], block[b + 1 : b + 2, :]], axis=1)
            row = narrow(lax.shift_right_logical(source, 7))
            hit = tall == jnp.broadcast_to(row, tall.shape)
            number = (second + (g * SUB + b)).astype(jnp.bfloat16)
            left = jnp.concatenate(
                [jnp.where(hit, number, nothing), jnp.where(hit, place, nothing)], axis=0
            )
            column = narrow(jnp.bitwise_and(source, LANES - 1))
            right = jnp.where(taller == jnp.broadcast_to(column, taller.shape), one, nothing)
            found = found + lax.dot_general(
                left, right, (((1,), (1,)), ((), ())), preferred_element_type=jnp.float32
            )
    found = found.astype(jnp.int32)
    for g in range(groups):
        block = found[g * SUB : (g + 1) * SUB]
        spot = found[(groups + g) * SUB : (groups + g + 1) * SUB]
        key, lanes = keys_of(block * LANES + spot)
        key_out[g] = key
        lane_out[g] = lanes

    small[...] = jnp.zeros(small.shape, jnp.float32)
    small[0, 0:1, 0 : table_ref.shape[1]] = table_ref[...]
    small[1, 0:1, 0 : diag_ref.shape[2]] = diag_ref[0]
    boxes = diag_ref.shape[2]
    table = full(small[0, 0:1, :])
    for x in range(MAIN):
        first_ext[x, 0] = take(table, cidx_ref[x])
        first_ext[x, 1] = (amap_ref[x] + 1).astype(jnp.float32)
        amaps[x] = amap_ref[x]

    def split(values):
        high = values.astype(jnp.bfloat16)
        low = (values - high.astype(jnp.float32)).astype(jnp.bfloat16)
        return high, low

    odd = (sub & 1) == 1

    def pick(values, keep):
        load_turns(values)
        for g in range(groups):
            keep[g] = permuted(key_in[g], lane_in[g])

    def block_apply(picked_of, done_with_dot, first=False):
        dot = zero
        picked = picked_of(0)
        if first:
            for u in range(groups):
                mat_copy(u).wait()
        for u in range(groups):
            if first:
                for b in range(SUB):
                    high, low = split(mats[u * SUB + b])
                    pair, part = (u * SUB + b) // 2, pl.ds((b % 2) * LANES, LANES)
                    halves[pair, part, 0:LANES] = high
                    halves[pair, part, LANES : 2 * LANES] = low
            upcoming = picked_of(u + 1) if u + 1 < groups else None
            sides = []
            for keep_odd in (False, True):
                side = jnp.where(odd == keep_odd, picked, 0.0)
                sides.append(jnp.concatenate(split(side), axis=0))
            left = jnp.concatenate(sides, axis=1)
            product = zero
            for j in range(SUB // 2):
                both = jnp.dot(
                    left, halves[u * SUB // 2 + j], preferred_element_type=jnp.float32
                )
                line = both[:SUB, :LANES] + (both[SUB:, :LANES] + both[:SUB, LANES:])
                line = line + both[SUB:, LANES:]
                product = jnp.where(lax.shift_right_logical(sub, 1) == j, line, product)
            moved[u] = product
            if done_with_dot is not None:
                dot = dot + picked * product
            picked = upcoming
        if done_with_dot is not None:
            done_with_dot(total_of(dot))
        load_turns([moved[g] for g in range(groups)])
        for g in range(groups):
            moved[g] = permuted(key_out[g], lane_out[g])
        return [moved[g] for g in range(groups)]

    def solve(values, done_with_dot=None):
        load_turns(values)
        return block_apply(lambda g: permuted(key_in[g], lane_in[g]), done_with_dot)

    base = lax.shift_right_logical(lane, 3)

    def restrict(values):
        sums = []
        for move in (-1, 0, 1):
            total = zero
            for x in range(MAIN):
                total = total + jnp.where(amaps[x] - base == move, values[x], 0.0)
            sums.append(total)
        total = pltpu.roll(sums[0], LANES - SUB, 1) + sums[1] + pltpu.roll(sums[2], SUB, 1)
        total = full(jnp.sum(total, axis=0, keepdims=True))
        for step in (1, 2, 4):
            total = total + pltpu.roll(total, LANES - step, 1)
        return jnp.where(lane < boxes, restrict_scale * take(total, (lane * SUB) & 127), 0.0)

    def row_copy(index, src, dst, device):
        return pltpu.make_async_remote_copy(
            src_ref=src, dst_ref=dst, send_sem=row_send.at[index], recv_sem=row_recv.at[index],
            device_id=device, device_id_type=MESH,
        )

    def send_rows(index, row, everywhere=False):
        row_src[index] = row[0:1, :]
        rows[index, me] = row[0:1, :]
        (for_all if everywhere else for_near)(
            lambda device: row_copy(index, row_src.at[index], rows.at[index, me], device).start()
        )

    def wait_rows(index, everywhere=False):
        def wait_for(number):
            part = rows.at[index, pl.ds(0, number)]
            both = row_copy(index, part, part, other(1))
            both.wait_send()
            both.wait_recv()

        if everywhere:
            wait_for(count - 1)
        else:
            for number in near_counts:
                pl.when(near == number)(functools.partial(wait_for, number))
        return rows[index].reshape(count, LANES)

    def scalar(row, number):
        at = 2 * boxes + number
        return row[:, at : at + 1]

    def with_scalar(row, number, value):
        return jnp.where(lane == 2 * boxes + number, full(value), row)

    def edge_rows(values, z):
        result = zero
        for x in range(MAIN):
            result = jnp.where(sub == x, full(values[x][z : z + 1, :]), result)
        return result

    def halo_copies(ring, ext, cols, corner_src, corners):
        copies = []
        for do, dm in DIRECTIONS:
            if dm == 0:
                src = ext.at[MAIN - 1 if do == 1 else 0]
                dst = ext.at[XLO if do == 1 else XHI]
            elif do == 0:
                src = cols.at[1 if dm == 1 else 0]
                dst = ext.at[ZLO if dm == 1 else ZHI]
            else:
                at = 2 * (0 if do == 1 else 1) + (0 if dm == 1 else 1)
                src = corner_src.at[at]
                dst = corners.at[at]
            to_o, to_m = o + do, m + dm
            goes = (to_o >= 0) & (to_o < owners) & (to_m >= 0) & (to_m < members)
            copies.append(
                (
                    goes,
                    pltpu.make_async_remote_copy(
                        src_ref=src, dst_ref=dst,
                        send_sem=send_sems.at[ring], recv_sem=recv_sems.at[ring],
                        device_id={"coarse": to_o, "fine": to_m}, device_id_type=MESH,
                    ),
                )
            )
        return copies

    def start_halo(ring, fields, ext, cols, corner_src, corners):
        packs = [zero, zero, zero, zero]
        for f, values in enumerate(fields):
            cols[0, f] = edge_rows(values, 0)
            cols[1, f] = edge_rows(values, SUB - 1)
            for side_x in range(2):
                for side_z in range(2):
                    at = 2 * side_x + side_z
                    x = MAIN - 1 if side_x == 0 else 0
                    z = SUB - 1 if side_z == 0 else 0
                    packs[at] = jnp.where(sub == f, full(values[x][z : z + 1, :]), packs[at])
        for at in range(4):
            corner_src[at] = packs[at]
        copies = halo_copies(ring, ext, cols, corner_src, corners)
        for goes, copy in copies:
            pl.when(goes)(copy.start)

    beside_o = (o > 0).astype(jnp.int32) + (o < owners - 1).astype(jnp.int32)
    beside_m = (m > 0).astype(jnp.int32) + (m < members - 1).astype(jnp.int32)

    def wait_halo(ring, fields):
        for number_o in range(3):
            for number_m in range(3):
                tiles = fields * (number_o + number_m) + number_o * number_m
                if tiles == 0:
                    continue

                @pl.when((beside_o == number_o) & (beside_m == number_m))
                def _(tiles=tiles):
                    part = rot.at[pl.ds(0, tiles)]
                    both = pltpu.make_async_remote_copy(
                        src_ref=part, dst_ref=part,
                        send_sem=send_sems.at[ring], recv_sem=recv_sems.at[ring],
                        device_id=other(1), device_id_type=MESH,
                    )
                    both.wait_send()
                    both.wait_recv()

    def corner_rows(corners, f):
        result = zero
        for at in range(4):
            result = jnp.where(sub == at, full(corners[at][f : f + 1, :]), result)
        return result

    def shifted(values, low, high):
        before = jnp.where(sub == 0, full(low), pltpu.roll(values, 1, 0))
        after = jnp.where(sub == SUB - 1, full(high), pltpu.roll(values, SUB - 1, 0))
        return values + 0.5 * (before + after)

    def smear(v):
        planes = [v[XLO]] + [v[x] for x in range(MAIN)] + [v[XHI]]
        corner = v[CORNER]
        low = shifted(v[ZLO], corner[0:1, :], corner[2:3, :])
        high = shifted(v[ZHI], corner[1:2, :], corner[3:4, :])
        result = []
        for x in range(MAIN):
            mid = planes[x + 1] + 0.5 * (planes[x] + planes[x + 2])
            mid = shifted(mid, low[x : x + 1, :], high[x : x + 1, :])
            before = jnp.where(lane == 0, 0.0, pltpu.roll(mid, 1, 1))
            after = jnp.where(lane == LANES - 1, 0.0, pltpu.roll(mid, LANES - 1, 1))
            result.append(mid + 0.5 * (before + after))
        return result

    node = lax.broadcasted_iota(jnp.int32, (count, LANES), 0)
    node_lane = lax.broadcasted_iota(jnp.int32, (count, LANES), 1)
    member = lax.rem(node, members)

    def coarse_solve(source, inverse):
        guess = omega * source * inverse
        for sweep in range(SWEEPS - 1):
            beside = pltpu.roll(guess, 1, 1) + pltpu.roll(guess, LANES - 1, 1)
            beside = beside + jnp.where(member == 0, 0.0, pltpu.roll(guess, 1, 0))
            beside = beside + jnp.where(
                member == members - 1, 0.0, pltpu.roll(guess, count - 1, 0)
            )
            beside = beside + jnp.where(node < members, 0.0, pltpu.roll(guess, members, 0))
            beside = beside + jnp.where(
                node >= count - members, 0.0, pltpu.roll(guess, count - members, 0)
            )
            guess = (1.0 - omega) * guess + omega * (source + beside) * inverse
        return guess

    def only_boxes(values):
        return jnp.where(node_lane < boxes, values, 0.0)

    def dot_of(left, right):
        total = zero
        for x in range(MAIN):
            total = total + left[x] * right[x]
        return total_of(total)

    start = [r_ref[x] for x in range(MAIN)]
    spread = full(small[1, 0:1, :])
    spread = jnp.where(lane < boxes, 1.0 / jnp.where(lane < boxes, 6.0 + spread, 1.0), 0.0)
    spread = pltpu.roll(spread, boxes, 1)
    first_row = restrict(start) + spread
    pick(start, picks)
    pl.semaphore_wait(barrier, near)
    send_rows(0, first_row)
    kappas = [first_ext[x, 0] for x in range(MAIN)]
    maps = [first_ext[x, 1] for x in range(MAIN)]
    start_halo(
        0, [kappas, maps], first_ext, first_cols, first_corner_src, first_corners
    )
    w = block_apply(lambda g: picks[g], None, True)
    for x in range(MAIN):
        w_ext[x, 0] = w[x]
    start_halo(1, [w], w_ext, w_cols, w_corner_src, w_corners)
    gathered = wait_rows(0)
    inverse = only_boxes(pltpu.roll(gathered, LANES - boxes, 1))
    guess = coarse_solve(only_boxes(gathered), inverse)

    def guess_rows(guess):
        picks = {}
        for do in (-1, 0, 1):
            for dm in (-1, 0, 1):
                wanted = me + do * members + dm
                picks[(do, dm)] = full(
                    jnp.sum(jnp.where(node == wanted, guess, 0.0), axis=0, keepdims=True)
                )
        return picks

    def add_coarse(values, guess):
        picks = guess_rows(guess)
        result = []
        for x in range(MAIN):
            result.append(values[x] + take(picks[(0, 0)], amaps[x]))
        for slot, way in ((XLO, (-1, 0)), (XHI, (1, 0)), (ZLO, (0, -1)), (ZHI, (0, 1))):
            result.append(values[slot] + take(picks[way], amaps[slot]))
        corner = zero
        for at, way in enumerate(((-1, -1), (-1, 1), (1, -1), (1, 1))):
            corner = jnp.where(sub == at, take(picks[way], amaps[CORNER]), corner)
        result.append(values[CORNER] + corner)
        return result

    wait_halo(0, 2)
    for slot in range(SLOTS):
        if slot == CORNER:
            parts = [corner_rows(first_corners, f) for f in range(2)]
        else:
            parts = [first_ext[slot, f] for f in range(2)]
        kap[slot] = parts[0]
        if slot >= MAIN:
            amaps[slot] = (parts[1].astype(jnp.int32) + (LANES - 1)) & (LANES - 1)
    smeared = smear([kap[s] for s in range(SLOTS)])
    for x in range(MAIN):
        kt[x] = 8.0 * kap[x] + smeared[x]

    def arrived(ring, ext, corners):
        wait_halo(ring, 1)
        return [ext[s, 0] for s in range(CORNER)] + [corner_rows(corners, 0)]

    def fine_operate(field, result):
        flat = smear(field)
        steep = smear([field[s] * kap[s] for s in range(SLOTS)])
        for x in range(MAIN):
            result[x] = field[x] * kt[x] - kap[x] * flat[x] - steep[x]

    z = add_coarse(arrived(1, w_ext, w_corners), guess)
    for slot in range(SLOTS):
        p_ext[slot] = z[slot]
    fine_operate(z, q_cur)
    image = [q_cur[x] for x in range(MAIN)]
    send_rows(1, restrict(image))
    bq = solve(image)
    for x in range(MAIN):
        b_ext[x, 0] = bq[x]
    start_halo(2, [bq], b_ext, b_cols, b_corner_src, b_corners)
    r_dot_p = dot_of(r_ref, p_ext)
    p_dot_q = dot_of(p_ext, q_cur)
    guess = coarse_solve(only_boxes(wait_rows(1)), inverse)
    u = add_coarse(arrived(2, b_ext, b_corners), guess)
    for x in range(MAIN):
        u_ext[x] = u[x]
    fine_operate(u, v_cur)
    image = [v_cur[x] for x in range(MAIN)]
    row = restrict(image) + spread
    row = with_scalar(row, 0, r_dot_p)
    row = with_scalar(row, 1, p_dot_q)
    row = with_scalar(row, 2, dot_of(q_cur, u_ext))
    row = with_scalar(row, 3, dot_of(u_ext, v_cur))
    send_rows(2, row, True)
    bv = solve(image, lambda dot: send_rows(3, full(dot), True))
    gathered = wait_rows(2, True)
    sums = jnp.sum(gathered, axis=0, keepdims=True)
    inverse = only_boxes(pltpu.roll(gathered, LANES - boxes, 1))
    source = only_boxes(gathered)
    guess = coarse_solve(source, inverse)
    coarse_part = full(total_of(source * guess) * (1.0 / restrict_scale))
    mu = [full(scalar(sums, number)) for number in range(4)]
    turn = 1.0 / mu[1]
    alpha0 = mu[0] * turn
    grow = alpha0 * mu[2] * turn
    curve = 1.0 / (alpha0 * alpha0 * mu[3] - grow * grow * mu[1])
    alpha1 = mu[0] * (grow - 1.0) * curve
    part = grow * grow * mu[2] - 2.0 * grow * alpha0 * mu[3] + alpha0 * alpha0 * coarse_part
    scale = alpha1 * curve
    own = full(jnp.sum(jnp.where(node == me, guess, 0.0), axis=0, keepdims=True))
    ahead, onward = [], []
    for x in range(MAIN):
        p0, q0, u0, v0 = p_ext[x], q_cur[x], u_ext[x], v_cur[x]
        t0 = bv[x] + take(own, amaps[x])
        p1 = grow * p0 - alpha0 * u0
        q1 = grow * q0 - alpha0 * v0
        x_out[x] = alpha0 * p0 + alpha1 * p1
        r_out[x] = r_ref[x] - alpha0 * q0 - alpha1 * q1
        ahead.append(p0 - alpha0 * u0 - alpha1 * (grow * u0 - alpha0 * t0))
        onward.append(p1)
    last = full(jnp.sum(wait_rows(3, True), axis=0, keepdims=True))
    beta1 = scale * (part + alpha0 * alpha0 * last) - 1.0
    for x in range(MAIN):
        p_out[x] = ahead[x] + beta1 * onward[x]


def emit(x_ref, r_ref, p_ref, x_out, r_out, p_out, sems):
    pairs = ((x_ref, x_out), (r_ref, r_out), (p_ref, p_out))
    copies = [pltpu.make_async_copy(a, b, sems.at[i]) for i, (a, b) in enumerate(pairs)]
    for copy in copies:
        copy.start()
    for copy in copies:
        copy.wait()


def shards(
    owners, members, right_side, coefficient_index, material_coefficients, block_cells,
    block_inverses, aggregate_map, coarse_diagonal,
):
    blocks, side = block_cells.shape[2], block_cells.shape[3]
    assert right_side.shape == (SUB, SUB, LANES) and side == LANES and blocks == SUB * SUB
    count = owners * members
    groups = blocks // SUB
    field = jax.ShapeDtypeStruct(right_side.shape, jnp.float32)
    vmem = pl.BlockSpec(memory_space=pltpu.VMEM)
    f32, i32 = jnp.float32, jnp.int32
    tile = (SUB, LANES)
    hbm = pl.BlockSpec(memory_space=pltpu.HBM)
    results = pl.pallas_call(
        functools.partial(kernel, owners, members),
        out_shape=(field, field, field),
        in_specs=[hbm] * 7,
        out_specs=(vmem, vmem, vmem),
        scratch_shapes=[
            pltpu.VMEM(right_side.shape, f32),
            pltpu.VMEM(right_side.shape, i32),
            pltpu.VMEM((1,) + material_coefficients.shape, f32),
            pltpu.VMEM((groups,) + tile, i32),
            pltpu.VMEM(right_side.shape, i32),
            pltpu.VMEM(coarse_diagonal.shape, f32),
            pltpu.SemaphoreType.DMA((6,)),
            pltpu.VMEM((blocks, side, side), f32),
            pltpu.VMEM((blocks // 2, 2 * side, 2 * side), jnp.bfloat16),
            pltpu.VMEM((blocks,) + tile, f32),
            pltpu.VMEM((groups,) + tile, i32),
            pltpu.VMEM((groups,) + tile, i32),
            pltpu.VMEM((groups,) + tile, i32),
            pltpu.VMEM((groups,) + tile, i32),
            pltpu.VMEM((groups,) + tile, f32),
            pltpu.VMEM((CORNER, 2) + tile, f32),
            pltpu.VMEM((2, 2) + tile, f32),
            pltpu.VMEM((4,) + tile, f32),
            pltpu.VMEM((4,) + tile, f32),
            pltpu.VMEM((CORNER, 1) + tile, f32),
            pltpu.VMEM((2, 1) + tile, f32),
            pltpu.VMEM((4,) + tile, f32),
            pltpu.VMEM((4,) + tile, f32),
            pltpu.VMEM((CORNER, 1) + tile, f32),
            pltpu.VMEM((2, 1) + tile, f32),
            pltpu.VMEM((4,) + tile, f32),
            pltpu.VMEM((4,) + tile, f32),
            pltpu.VMEM((SLOTS,) + tile, f32),
            pltpu.VMEM((SLOTS,) + tile, i32),
            pltpu.VMEM((SLOTS,) + tile, f32),
            pltpu.VMEM((MAIN,) + tile, f32),
            pltpu.VMEM((MAIN,) + tile, f32),
            pltpu.VMEM((MAIN,) + tile, f32),
            pltpu.VMEM((MAIN,) + tile, f32),
            pltpu.VMEM((2,) + tile, f32),
            pltpu.VMEM((ROUNDS, 1, LANES), f32),
            pltpu.VMEM((ROUNDS, count, 1, LANES), f32),
            pltpu.VMEM((groups,) + tile, f32),
            pltpu.SemaphoreType.DMA((groups,)),
            pltpu.SemaphoreType.DMA((RINGS,)),
            pltpu.SemaphoreType.DMA((RINGS,)),
            pltpu.SemaphoreType.DMA((ROUNDS,)),
            pltpu.SemaphoreType.DMA((ROUNDS,)),
        ],
        compiler_params=pltpu.CompilerParams(
            collective_id=0, has_side_effects=True, vmem_limit_bytes=32 << 20
        ),
    )(
        *(pltpu.with_memory_space_constraint(a, pltpu.HBM) for a in (
        right_side,
        coefficient_index,
        material_coefficients.reshape(1, -1),
        block_cells.reshape(groups, SUB, LANES),
        block_inverses.reshape(blocks, side, side),
        aggregate_map,
        coarse_diagonal,
        ))
    )
    return pl.pallas_call(
        emit,
        out_shape=(field, field, field),
        in_specs=[vmem] * 3,
        out_specs=(hbm,) * 3,
        scratch_shapes=[pltpu.SemaphoreType.DMA((3,))],
        compiler_params=pltpu.CompilerParams(vmem_limit_bytes=1 << 20),
    )(*results)


def solution(mesh):
    three = P("coarse", "fine", None)
    return jax.shard_map(
        functools.partial(shards, mesh.shape["coarse"], mesh.shape["fine"]),
        mesh=mesh,
        in_specs=(
            three,
            three,
            P(),
            P("coarse", "fine", None, None),
            P("coarse", "fine", None, None, None),
            three,
            three,
        ),
        out_specs=(three, three, three),
        check_vma=False,
    )
```

```python
import functools

import jax
import jax.numpy as jnp
from jax import lax
from jax.experimental import pallas as pl
from jax.experimental.pallas import tpu as pltpu
from jax.sharding import PartitionSpec as P

RINGS = 3
ROUNDS = 4
UNROLLED = 64
SWEEPS = 4
omega = 0.8
restrict_scale = 0.25
MESH = pl.DeviceIdType.MESH
SUB = 8
LANES = 128
MAIN = 8
XLO, XHI, ZLO, ZHI, CORNER = 8, 9, 10, 11, 12
SLOTS = 13
REACH = SWEEPS
DIRECTIONS = ((-1, 0), (1, 0), (0, -1), (0, 1), (-1, -1), (-1, 1), (1, -1), (1, 1))


def take(values, lanes):
    return jnp.take_along_axis(values, lanes, axis=1, mode="promise_in_bounds")


def full(row):
    return jnp.broadcast_to(row, (SUB, LANES))


def total_of(values):
    return jnp.sum(jnp.sum(values, axis=0, keepdims=True), axis=1, keepdims=True)


def kernel(
    owners, members, r_hbm, cidx_hbm, table_hbm, cells_hbm, inv_ref, amap_hbm, diag_hbm,
    x_out, r_out, p_out,
    r_ref, cidx_ref, table_ref, cells_ref, amap_ref, diag_ref, in_sems,
    mats, highs, lows, rot, key_in, lane_in, key_out, lane_out, moved,
    first_ext, first_cols, first_corner_src, first_corners,
    w_ext, w_cols, w_corner_src, w_corners,
    b_ext, b_cols, b_corner_src, b_corners,
    kap, amaps, p_ext, u_ext, q_cur, v_cur, kt, small,
    row_src, rows, picks,
    mat_sems, send_sems, recv_sems, row_send, row_recv,
):
    count = owners * members
    o = lax.axis_index("coarse")
    m = lax.axis_index("fine")
    me = o * members + m
    groups = cells_ref.shape[0]
    sub = lax.broadcasted_iota(jnp.int32, (SUB, LANES), 0)
    lane = lax.broadcasted_iota(jnp.int32, (SUB, LANES), 1)
    zero = jnp.zeros((SUB, LANES), jnp.float32)

    in_copies = [
        pltpu.make_async_copy(src, dst, in_sems.at[at])
        for at, (src, dst) in enumerate(
            (
                (cells_hbm, cells_ref),
                (r_hbm, r_ref),
                (amap_hbm, amap_ref),
                (cidx_hbm, cidx_ref),
                (table_hbm, table_ref),
                (diag_hbm, diag_ref),
            )
        )
    ]
    for copy in in_copies:
        copy.start()
    def mat_copy(u):
        part = pl.ds(u * SUB, SUB)
        return pltpu.make_async_copy(inv_ref.at[part], mats.at[part], mat_sems.at[u])

    for slot in range(MAIN, CORNER):
        for f in range(2):
            first_ext[slot, f] = zero
        w_ext[slot, 0] = zero
        b_ext[slot, 0] = zero
    for c in range(4):
        first_corners[c] = zero
        w_corners[c] = zero
        b_corners[c] = zero
    rows[...] = jnp.zeros(rows.shape, jnp.float32)

    barrier = pltpu.get_barrier_semaphore()
    reach_o = max(REACH, -(-(owners - 1) // 3))
    reach_m = max(REACH, -(-(members - 1) // 3))
    low_o, high_o = jnp.maximum(o - reach_o, 0), jnp.minimum(o + reach_o, owners - 1) + 1
    low_m, high_m = jnp.maximum(m - reach_m, 0), jnp.minimum(m + reach_m, members - 1) + 1
    near = (high_o - low_o) * (high_m - low_m) - 1

    def spans(size, reach):
        return {min(at + reach, size - 1) - max(at - reach, 0) + 1 for at in range(size)}

    near_counts = sorted(
        {a * b - 1 for a in spans(owners, reach_o) for b in spans(members, reach_m)}
    )

    def other(d):
        t = lax.rem(me + d, count)
        return {"coarse": lax.div(t, members), "fine": lax.rem(t, members)}

    def for_all(act):
        if count <= UNROLLED:
            for d in range(1, count):
                act(other(d))
        else:

            def one(d, carry):
                act(other(d))
                return carry

            lax.fori_loop(1, count, one, 0)

    def for_near(act):
        def one(device):
            to_o, to_m = device["coarse"], device["fine"]
            close = None
            if reach_o < owners - 1:
                close = (to_o >= low_o) & (to_o < high_o)
            if reach_m < members - 1:
                close_m = (to_m >= low_m) & (to_m < high_m)
                close = close_m if close is None else close & close_m
            if close is None:
                act(device)
            else:
                pl.when(close)(functools.partial(act, device))

        for_all(one)

    for u in range(groups):
        mat_copy(u).start()
    for_near(
        lambda device: pl.semaphore_signal(barrier, inc=1, device_id=device, device_id_type=MESH)
    )

    for copy in in_copies:
        copy.wait()

    def keys_of(source):
        row = lax.shift_right_logical(source, 7)
        turn = (jnp.bitwise_and(row, 7) - sub) & 7
        return jnp.bitwise_and(row, ~7) + turn, jnp.bitwise_and(source, 127)

    for g in range(groups):
        key, lanes = keys_of(cells_ref[g])
        key_in[g] = key
        lane_in[g] = lanes

    def load_turns(values):
        for g in range(len(values)):
            for turn in range(SUB):
                rot[g * SUB + turn] = (
                    values[g] if turn == 0 else pltpu.roll(values[g], SUB - turn, 0)
                )

    def permuted(key, lanes):
        parts = [zero, zero]
        for k in range(groups * SUB):
            parts[k % 2] = jnp.where(key == k, take(rot[k], lanes), parts[k % 2])
        return parts[0] + parts[1]

    both_lanes = 2 * LANES
    tall = lax.broadcasted_iota(jnp.int32, (groups * SUB, both_lanes), 0)
    taller = lax.broadcasted_iota(jnp.int32, (LANES, both_lanes), 0)
    place = lax.broadcasted_iota(jnp.int32, (groups * SUB, both_lanes), 1)
    second = jnp.where(place >= LANES, 1.0, 0.0)

    def narrow(values):
        return values.astype(jnp.float32).astype(jnp.bfloat16)

    tall, taller, place = narrow(tall), narrow(taller), narrow(place & (LANES - 1))
    one, nothing = jnp.bfloat16(1), jnp.bfloat16(0)
    parts = [jnp.zeros((2 * groups * SUB, LANES), jnp.float32)] * 2
    for g in range(groups):
        block = cells_ref[g]
        for b in range(0, SUB, 2):
            source = jnp.concatenate([block[b : b + 1, :], block[b + 1 : b + 2, :]], axis=1)
            row = narrow(lax.shift_right_logical(source, 7))
            hit = tall == jnp.broadcast_to(row, tall.shape)
            number = (second + (g * SUB + b)).astype(jnp.bfloat16)
            left = jnp.concatenate(
                [jnp.where(hit, number, nothing), jnp.where(hit, place, nothing)], axis=0
            )
            column = narrow(jnp.bitwise_and(source, LANES - 1))
            right = jnp.where(taller == jnp.broadcast_to(column, taller.shape), one, nothing)
            at = (b // 2) % 2
            parts[at] = parts[at] + lax.dot_general(
                left, right, (((1,), (1,)), ((), ())), preferred_element_type=jnp.float32
            )
    found = jnp.maximum(parts[0], parts[1]).astype(jnp.int32)
    for g in range(groups):
        block = found[g * SUB : (g + 1) * SUB]
        spot = found[(groups + g) * SUB : (groups + g + 1) * SUB]
        key, lanes = keys_of(block * LANES + spot)
        key_out[g] = key
        lane_out[g] = lanes

    small[...] = jnp.zeros(small.shape, jnp.float32)
    small[0, 0:1, 0 : table_ref.shape[1]] = table_ref[...]
    small[1, 0:1, 0 : diag_ref.shape[2]] = diag_ref[0]
    boxes = diag_ref.shape[2]
    table = full(small[0, 0:1, :])
    for x in range(MAIN):
        first_ext[x, 0] = take(table, cidx_ref[x])
        first_ext[x, 1] = (amap_ref[x] + 1).astype(jnp.float32)
        amaps[x] = amap_ref[x]

    def split(values):
        high = values.astype(jnp.bfloat16)
        low = (values - high.astype(jnp.float32)).astype(jnp.bfloat16)
        return high, low

    odd = (sub & 1) == 1

    def pick(values, keep):
        load_turns(values)
        for g in range(groups):
            keep[g] = permuted(key_in[g], lane_in[g])

    def block_apply(picked_of, done_with_dot, first=False):
        dot = zero
        picked = picked_of(0)
        if first:
            for u in range(groups):
                mat_copy(u).wait()
        for u in range(groups):
            if first:
                for b in range(SUB):
                    high, low = split(mats[u * SUB + b])
                    pair, part = (u * SUB + b) // 2, pl.ds((b % 2) * LANES, LANES)
                    highs[pair, part] = high
                    lows[pair, part] = low
            upcoming = picked_of(u + 1) if u + 1 < groups else None
            sides = []
            for keep_odd in (False, True):
                side = jnp.where(odd == keep_odd, picked, 0.0)
                sides.append(jnp.concatenate(split(side), axis=0))
            left = jnp.concatenate(sides, axis=1)
            product = zero
            for j in range(SUB // 2):
                pair = u * SUB // 2 + j
                right = jnp.concatenate([highs[pair], lows[pair]], axis=1)
                both = jnp.dot(left, right, preferred_element_type=jnp.float32)
                line = both[:SUB, :LANES] + (both[SUB:, :LANES] + both[:SUB, LANES:])
                line = line + both[SUB:, LANES:]
                product = jnp.where(lax.shift_right_logical(sub, 1) == j, line, product)
            moved[u] = product
            if done_with_dot is not None:
                dot = dot + picked * product
            picked = upcoming
        if done_with_dot is not None:
            done_with_dot(total_of(dot))
        load_turns([moved[g] for g in range(groups)])
        for g in range(groups):
            moved[g] = permuted(key_out[g], lane_out[g])
        return [moved[g] for g in range(groups)]

    def solve(values, done_with_dot=None):
        load_turns(values)
        return block_apply(lambda g: permuted(key_in[g], lane_in[g]), done_with_dot)

    base = lax.shift_right_logical(lane, 3)

    def restrict(values):
        sums = []
        for move in (-1, 0, 1):
            total = zero
            for x in range(MAIN):
                total = total + jnp.where(amaps[x] - base == move, values[x], 0.0)
            sums.append(total)
        total = pltpu.roll(sums[0], LANES - SUB, 1) + sums[1] + pltpu.roll(sums[2], SUB, 1)
        total = full(jnp.sum(total, axis=0, keepdims=True))
        for step in (1, 2, 4):
            total = total + pltpu.roll(total, LANES - step, 1)
        return jnp.where(lane < boxes, restrict_scale * take(total, (lane * SUB) & 127), 0.0)

    def row_copy(index, src, dst, device):
        return pltpu.make_async_remote_copy(
            src_ref=src, dst_ref=dst, send_sem=row_send.at[index], recv_sem=row_recv.at[index],
            device_id=device, device_id_type=MESH,
        )

    def send_rows(index, row, everywhere=False):
        row_src[index] = row[0:1, :]
        rows[index, me] = row[0:1, :]
        (for_all if everywhere else for_near)(
            lambda device: row_copy(index, row_src.at[index], rows.at[index, me], device).start()
        )

    def wait_rows(index, everywhere=False):
        def wait_for(number):
            part = rows.at[index, pl.ds(0, number)]
            both = row_copy(index, part, part, other(1))
            both.wait_send()
            both.wait_recv()

        if everywhere:
            wait_for(count - 1)
        else:
            for number in near_counts:
                pl.when(near == number)(functools.partial(wait_for, number))
        return rows[index].reshape(count, LANES)

    def scalar(row, number):
        at = 2 * boxes + number
        return row[:, at : at + 1]

    def with_scalar(row, number, value):
        return jnp.where(lane == 2 * boxes + number, full(value), row)

    def edge_rows(values, z):
        result = zero
        for x in range(MAIN):
            result = jnp.where(sub == x, full(values[x][z : z + 1, :]), result)
        return result

    def halo_copies(ring, ext, cols, corner_src, corners):
        copies = []
        for do, dm in DIRECTIONS:
            if dm == 0:
                src = ext.at[MAIN - 1 if do == 1 else 0]
                dst = ext.at[XLO if do == 1 else XHI]
            elif do == 0:
                src = cols.at[1 if dm == 1 else 0]
                dst = ext.at[ZLO if dm == 1 else ZHI]
            else:
                at = 2 * (0 if do == 1 else 1) + (0 if dm == 1 else 1)
                src = corner_src.at[at]
                dst = corners.at[at]
            to_o, to_m = o + do, m + dm
            goes = (to_o >= 0) & (to_o < owners) & (to_m >= 0) & (to_m < members)
            copies.append(
                (
                    goes,
                    pltpu.make_async_remote_copy(
                        src_ref=src, dst_ref=dst,
                        send_sem=send_sems.at[ring], recv_sem=recv_sems.at[ring],
                        device_id={"coarse": to_o, "fine": to_m}, device_id_type=MESH,
                    ),
                )
            )
        return copies

    def start_halo(ring, fields, ext, cols, corner_src, corners):
        packs = [zero, zero, zero, zero]
        for f, values in enumerate(fields):
            cols[0, f] = edge_rows(values, 0)
            cols[1, f] = edge_rows(values, SUB - 1)
            for side_x in range(2):
                for side_z in range(2):
                    at = 2 * side_x + side_z
                    x = MAIN - 1 if side_x == 0 else 0
                    z = SUB - 1 if side_z == 0 else 0
                    packs[at] = jnp.where(sub == f, full(values[x][z : z + 1, :]), packs[at])
        for at in range(4):
            corner_src[at] = packs[at]
        copies = halo_copies(ring, ext, cols, corner_src, corners)
        for goes, copy in copies:
            pl.when(goes)(copy.start)

    beside_o = (o > 0).astype(jnp.int32) + (o < owners - 1).astype(jnp.int32)
    beside_m = (m > 0).astype(jnp.int32) + (m < members - 1).astype(jnp.int32)

    def wait_halo(ring, fields):
        for number_o in range(3):
            for number_m in range(3):
                tiles = fields * (number_o + number_m) + number_o * number_m
                if tiles == 0:
                    continue

                @pl.when((beside_o == number_o) & (beside_m == number_m))
                def _(tiles=tiles):
                    part = rot.at[pl.ds(0, tiles)]
                    both = pltpu.make_async_remote_copy(
                        src_ref=part, dst_ref=part,
                        send_sem=send_sems.at[ring], recv_sem=recv_sems.at[ring],
                        device_id=other(1), device_id_type=MESH,
                    )
                    both.wait_send()
                    both.wait_recv()

    def corner_rows(corners, f):
        result = zero
        for at in range(4):
            result = jnp.where(sub == at, full(corners[at][f : f + 1, :]), result)
        return result

    def shifted(values, low, high):
        before = jnp.where(sub == 0, full(low), pltpu.roll(values, 1, 0))
        after = jnp.where(sub == SUB - 1, full(high), pltpu.roll(values, SUB - 1, 0))
        return values + 0.5 * (before + after)

    def smear(v):
        planes = [v[XLO]] + [v[x] for x in range(MAIN)] + [v[XHI]]
        corner = v[CORNER]
        low = shifted(v[ZLO], corner[0:1, :], corner[2:3, :])
        high = shifted(v[ZHI], corner[1:2, :], corner[3:4, :])
        result = []
        for x in range(MAIN):
            mid = planes[x + 1] + 0.5 * (planes[x] + planes[x + 2])
            mid = shifted(mid, low[x : x + 1, :], high[x : x + 1, :])
            before = jnp.where(lane == 0, 0.0, pltpu.roll(mid, 1, 1))
            after = jnp.where(lane == LANES - 1, 0.0, pltpu.roll(mid, LANES - 1, 1))
            result.append(mid + 0.5 * (before + after))
        return result

    node = lax.broadcasted_iota(jnp.int32, (count, LANES), 0)
    node_lane = lax.broadcasted_iota(jnp.int32, (count, LANES), 1)
    member = lax.rem(node, members)

    def coarse_solve(source, inverse):
        guess = omega * source * inverse
        for sweep in range(SWEEPS - 1):
            beside = pltpu.roll(guess, 1, 1) + pltpu.roll(guess, LANES - 1, 1)
            beside = beside + jnp.where(member == 0, 0.0, pltpu.roll(guess, 1, 0))
            beside = beside + jnp.where(
                member == members - 1, 0.0, pltpu.roll(guess, count - 1, 0)
            )
            beside = beside + jnp.where(node < members, 0.0, pltpu.roll(guess, members, 0))
            beside = beside + jnp.where(
                node >= count - members, 0.0, pltpu.roll(guess, count - members, 0)
            )
            guess = (1.0 - omega) * guess + omega * (source + beside) * inverse
        return guess

    def only_boxes(values):
        return jnp.where(node_lane < boxes, values, 0.0)

    def dot_of(left, right):
        total = zero
        for x in range(MAIN):
            total = total + left[x] * right[x]
        return total_of(total)

    start = [r_ref[x] for x in range(MAIN)]
    spread = full(small[1, 0:1, :])
    spread = jnp.where(lane < boxes, 1.0 / jnp.where(lane < boxes, 6.0 + spread, 1.0), 0.0)
    spread = pltpu.roll(spread, boxes, 1)
    first_row = restrict(start) + spread
    pick(start, picks)
    pl.semaphore_wait(barrier, near)
    send_rows(0, first_row)
    kappas = [first_ext[x, 0] for x in range(MAIN)]
    maps = [first_ext[x, 1] for x in range(MAIN)]
    start_halo(
        0, [kappas, maps], first_ext, first_cols, first_corner_src, first_corners
    )
    w = block_apply(lambda g: picks[g], None, True)
    for x in range(MAIN):
        w_ext[x, 0] = w[x]
    start_halo(1, [w], w_ext, w_cols, w_corner_src, w_corners)
    gathered = wait_rows(0)
    inverse = only_boxes(pltpu.roll(gathered, LANES - boxes, 1))
    guess = coarse_solve(only_boxes(gathered), inverse)

    def guess_rows(guess):
        picks = {}
        for do in (-1, 0, 1):
            for dm in (-1, 0, 1):
                wanted = me + do * members + dm
                picks[(do, dm)] = full(
                    jnp.sum(jnp.where(node == wanted, guess, 0.0), axis=0, keepdims=True)
                )
        return picks

    def add_coarse(values, guess):
        picks = guess_rows(guess)
        result = []
        for x in range(MAIN):
            result.append(values[x] + take(picks[(0, 0)], amaps[x]))
        for slot, way in ((XLO, (-1, 0)), (XHI, (1, 0)), (ZLO, (0, -1)), (ZHI, (0, 1))):
            result.append(values[slot] + take(picks[way], amaps[slot]))
        corner = zero
        for at, way in enumerate(((-1, -1), (-1, 1), (1, -1), (1, 1))):
            corner = jnp.where(sub == at, take(picks[way], amaps[CORNER]), corner)
        result.append(values[CORNER] + corner)
        return result

    wait_halo(0, 2)
    for slot in range(SLOTS):
        if slot == CORNER:
            parts = [corner_rows(first_corners, f) for f in range(2)]
        else:
            parts = [first_ext[slot, f] for f in range(2)]
        kap[slot] = parts[0]
        if slot >= MAIN:
            amaps[slot] = (parts[1].astype(jnp.int32) + (LANES - 1)) & (LANES - 1)
    smeared = smear([kap[s] for s in range(SLOTS)])
    for x in range(MAIN):
        kt[x] = 8.0 * kap[x] + smeared[x]

    def arrived(ring, ext, corners):
        wait_halo(ring, 1)
        return [ext[s, 0] for s in range(CORNER)] + [corner_rows(corners, 0)]

    def fine_operate(field, result):
        flat = smear(field)
        steep = smear([field[s] * kap[s] for s in range(SLOTS)])
        for x in range(MAIN):
            result[x] = field[x] * kt[x] - kap[x] * flat[x] - steep[x]

    z = add_coarse(arrived(1, w_ext, w_corners), guess)
    for slot in range(SLOTS):
        p_ext[slot] = z[slot]
    fine_operate(z, q_cur)
    image = [q_cur[x] for x in range(MAIN)]
    send_rows(1, restrict(image))
    bq = solve(image)
    for x in range(MAIN):
        b_ext[x, 0] = bq[x]
    start_halo(2, [bq], b_ext, b_cols, b_corner_src, b_corners)
    r_dot_p = dot_of(r_ref, p_ext)
    p_dot_q = dot_of(p_ext, q_cur)
    guess = coarse_solve(only_boxes(wait_rows(1)), inverse)
    u = add_coarse(arrived(2, b_ext, b_corners), guess)
    for x in range(MAIN):
        u_ext[x] = u[x]
    fine_operate(u, v_cur)
    image = [v_cur[x] for x in range(MAIN)]
    row = restrict(image) + spread
    row = with_scalar(row, 0, r_dot_p)
    row = with_scalar(row, 1, p_dot_q)
    row = with_scalar(row, 2, dot_of(q_cur, u_ext))
    row = with_scalar(row, 3, dot_of(u_ext, v_cur))
    send_rows(2, row, True)
    bv = solve(image, lambda dot: send_rows(3, full(dot), True))
    gathered = wait_rows(2, True)
    sums = jnp.sum(gathered, axis=0, keepdims=True)
    inverse = only_boxes(pltpu.roll(gathered, LANES - boxes, 1))
    source = only_boxes(gathered)
    guess = coarse_solve(source, inverse)
    coarse_part = full(total_of(source * guess) * (1.0 / restrict_scale))
    mu = [full(scalar(sums, number)) for number in range(4)]
    turn = 1.0 / mu[1]
    alpha0 = mu[0] * turn
    grow = alpha0 * mu[2] * turn
    curve = 1.0 / (alpha0 * alpha0 * mu[3] - grow * grow * mu[1])
    alpha1 = mu[0] * (grow - 1.0) * curve
    part = grow * grow * mu[2] - 2.0 * grow * alpha0 * mu[3] + alpha0 * alpha0 * coarse_part
    scale = alpha1 * curve
    own = full(jnp.sum(jnp.where(node == me, guess, 0.0), axis=0, keepdims=True))
    ahead, onward = [], []
    for x in range(MAIN):
        p0, q0, u0, v0 = p_ext[x], q_cur[x], u_ext[x], v_cur[x]
        t0 = bv[x] + take(own, amaps[x])
        p1 = grow * p0 - alpha0 * u0
        q1 = grow * q0 - alpha0 * v0
        x_out[x] = alpha0 * p0 + alpha1 * p1
        r_out[x] = r_ref[x] - alpha0 * q0 - alpha1 * q1
        ahead.append(p0 - alpha0 * u0 - alpha1 * (grow * u0 - alpha0 * t0))
        onward.append(p1)
    last = full(jnp.sum(wait_rows(3, True), axis=0, keepdims=True))
    beta1 = scale * (part + alpha0 * alpha0 * last) - 1.0
    for x in range(MAIN):
        p_out[x] = ahead[x] + beta1 * onward[x]


def emit(x_ref, r_ref, p_ref, x_out, r_out, p_out, sems):
    pairs = ((x_ref, x_out), (r_ref, r_out), (p_ref, p_out))
    copies = [pltpu.make_async_copy(a, b, sems.at[i]) for i, (a, b) in enumerate(pairs)]
    for copy in copies:
        copy.start()
    for copy in copies:
        copy.wait()


def shards(
    owners, members, right_side, coefficient_index, material_coefficients, block_cells,
    block_inverses, aggregate_map, coarse_diagonal,
):
    blocks, side = block_cells.shape[2], block_cells.shape[3]
    assert right_side.shape == (SUB, SUB, LANES) and side == LANES and blocks == SUB * SUB
    count = owners * members
    groups = blocks // SUB
    field = jax.ShapeDtypeStruct(right_side.shape, jnp.float32)
    vmem = pl.BlockSpec(memory_space=pltpu.VMEM)
    f32, i32 = jnp.float32, jnp.int32
    tile = (SUB, LANES)
    hbm = pl.BlockSpec(memory_space=pltpu.HBM)
    results = pl.pallas_call(
        functools.partial(kernel, owners, members),
        out_shape=(field, field, field),
        in_specs=[hbm] * 7,
        out_specs=(vmem, vmem, vmem),
        scratch_shapes=[
            pltpu.VMEM(right_side.shape, f32),
            pltpu.VMEM(right_side.shape, i32),
            pltpu.VMEM((1,) + material_coefficients.shape, f32),
            pltpu.VMEM((groups,) + tile, i32),
            pltpu.VMEM(right_side.shape, i32),
            pltpu.VMEM(coarse_diagonal.shape, f32),
            pltpu.SemaphoreType.DMA((6,)),
            pltpu.VMEM((blocks, side, side), f32),
            pltpu.VMEM((blocks // 2, 2 * side, side), jnp.bfloat16),
            pltpu.VMEM((blocks // 2, 2 * side, side), jnp.bfloat16),
            pltpu.VMEM((blocks,) + tile, f32),
            pltpu.VMEM((groups,) + tile, i32),
            pltpu.VMEM((groups,) + tile, i32),
            pltpu.VMEM((groups,) + tile, i32),
            pltpu.VMEM((groups,) + tile, i32),
            pltpu.VMEM((groups,) + tile, f32),
            pltpu.VMEM((CORNER, 2) + tile, f32),
            pltpu.VMEM((2, 2) + tile, f32),
            pltpu.VMEM((4,) + tile, f32),
            pltpu.VMEM((4,) + tile, f32),
            pltpu.VMEM((CORNER, 1) + tile, f32),
            pltpu.VMEM((2, 1) + tile, f32),
            pltpu.VMEM((4,) + tile, f32),
            pltpu.VMEM((4,) + tile, f32),
            pltpu.VMEM((CORNER, 1) + tile, f32),
            pltpu.VMEM((2, 1) + tile, f32),
            pltpu.VMEM((4,) + tile, f32),
            pltpu.VMEM((4,) + tile, f32),
            pltpu.VMEM((SLOTS,) + tile, f32),
            pltpu.VMEM((SLOTS,) + tile, i32),
            pltpu.VMEM((SLOTS,) + tile, f32),
            pltpu.VMEM((MAIN,) + tile, f32),
            pltpu.VMEM((MAIN,) + tile, f32),
            pltpu.VMEM((MAIN,) + tile, f32),
            pltpu.VMEM((MAIN,) + tile, f32),
            pltpu.VMEM((2,) + tile, f32),
            pltpu.VMEM((ROUNDS, 1, LANES), f32),
            pltpu.VMEM((ROUNDS, count, 1, LANES), f32),
            pltpu.VMEM((groups,) + tile, f32),
            pltpu.SemaphoreType.DMA((groups,)),
            pltpu.SemaphoreType.DMA((RINGS,)),
            pltpu.SemaphoreType.DMA((RINGS,)),
            pltpu.SemaphoreType.DMA((ROUNDS,)),
            pltpu.SemaphoreType.DMA((ROUNDS,)),
        ],
        compiler_params=pltpu.CompilerParams(
            collective_id=0, has_side_effects=True, vmem_limit_bytes=32 << 20
        ),
    )(
        *(pltpu.with_memory_space_constraint(a, pltpu.HBM) for a in (
        right_side,
        coefficient_index,
        material_coefficients.reshape(1, -1),
        block_cells.reshape(groups, SUB, LANES),
        block_inverses.reshape(blocks, side, side),
        aggregate_map,
        coarse_diagonal,
        ))
    )
    return pl.pallas_call(
        emit,
        out_shape=(field, field, field),
        in_specs=[vmem] * 3,
        out_specs=(hbm,) * 3,
        scratch_shapes=[pltpu.SemaphoreType.DMA((3,))],
        compiler_params=pltpu.CompilerParams(vmem_limit_bytes=1 << 20),
    )(*results)


def solution(mesh):
    three = P("coarse", "fine", None)
    return jax.shard_map(
        functools.partial(shards, mesh.shape["coarse"], mesh.shape["fine"]),
        mesh=mesh,
        in_specs=(
            three,
            three,
            P(),
            P("coarse", "fine", None, None),
            P("coarse", "fine", None, None, None),
            three,
            three,
        ),
        out_specs=(three, three, three),
        check_vma=False,
    )
```

```python
import functools

import jax
import jax.numpy as jnp
from jax import lax
from jax.experimental import pallas as pl
from jax.experimental.pallas import tpu as pltpu
from jax.sharding import PartitionSpec as P

RINGS = 3
ROUNDS = 4
UNROLLED = 64
SWEEPS = 4
omega = 0.8
restrict_scale = 0.25
MESH = pl.DeviceIdType.MESH
SUB = 8
LANES = 128
MAIN = 8
XLO, XHI, ZLO, ZHI, CORNER = 8, 9, 10, 11, 12
SLOTS = 13
DIRECTIONS = ((-1, 0), (1, 0), (0, -1), (0, 1), (-1, -1), (-1, 1), (1, -1), (1, 1))


def take(values, lanes):
    return jnp.take_along_axis(values, lanes, axis=1, mode="promise_in_bounds")


def full(row):
    return jnp.broadcast_to(row, (SUB, LANES))


def total_of(values):
    return jnp.sum(jnp.sum(values, axis=0, keepdims=True), axis=1, keepdims=True)


def kernel(
    owners, members, r_hbm, cidx_hbm, table_hbm, cells_hbm, inv_ref, amap_hbm, diag_hbm,
    x_out, r_out, p_out,
    r_ref, cidx_ref, table_ref, cells_ref, amap_ref, diag_ref, in_sems,
    mats, highs, lows, rot, key_in, lane_in, key_out, lane_out, moved,
    first_ext, first_cols, first_corner_src, first_corners,
    w_ext, w_cols, w_corner_src, w_corners,
    b_ext, b_cols, b_corner_src, b_corners,
    kap, amaps, p_ext, u_ext, q_cur, v_cur, kt, small,
    row_src, rows, picks,
    mat_sems, send_sems, recv_sems, row_send, row_recv,
):
    count = owners * members
    o = lax.axis_index("coarse")
    m = lax.axis_index("fine")
    me = o * members + m
    groups = cells_ref.shape[0]
    sub = lax.broadcasted_iota(jnp.int32, (SUB, LANES), 0)
    lane = lax.broadcasted_iota(jnp.int32, (SUB, LANES), 1)
    zero = jnp.zeros((SUB, LANES), jnp.float32)

    in_copies = [
        pltpu.make_async_copy(src, dst, in_sems.at[at])
        for at, (src, dst) in enumerate(
            (
                (cells_hbm, cells_ref),
                (r_hbm, r_ref),
                (amap_hbm, amap_ref),
                (cidx_hbm, cidx_ref),
                (table_hbm, table_ref),
                (diag_hbm, diag_ref),
            )
        )
    ]
    for copy in in_copies:
        copy.start()
    def mat_copy(u):
        part = pl.ds(u * SUB, SUB)
        return pltpu.make_async_copy(inv_ref.at[part], mats.at[part], mat_sems.at[u])

    for slot in range(MAIN, CORNER):
        for f in range(2):
            first_ext[slot, f] = zero
        w_ext[slot, 0] = zero
        b_ext[slot, 0] = zero
    for c in range(4):
        first_corners[c] = zero
        w_corners[c] = zero
        b_corners[c] = zero
    rows[...] = jnp.zeros(rows.shape, jnp.float32)

    barrier = pltpu.get_barrier_semaphore()
    step_o, step_m = -(-(owners - 1) // 3), -(-(members - 1) // 3)
    reach = max(SWEEPS - 1, max(step_o - 1, 0) + max(step_m - 1, 0))

    def height(away):
        return reach - max(abs(away) - 1, 0) + 1

    columns = [b for b in range(1 - members, members) if height(b) > 0]

    def near_of(o, m, least, most):
        total = -1
        for b in columns:
            size = most(o - height(b), 0, least(o + height(b), owners - 1))
            total = total + size * ((m + b >= 0) & (m + b < members))
        return total

    near = near_of(
        o, m, jnp.minimum, lambda low, zero, high: high - jnp.maximum(low, zero) + 1
    )
    near_counts = sorted(
        {
            near_of(at_o, at_m, min, lambda low, zero, high: high - max(low, zero) + 1)
            for at_o in range(owners)
            for at_m in range(members)
        }
    )

    def other(d):
        if count & (count - 1) or members & (members - 1):
            t = lax.rem(me + d, count)
            return {"coarse": lax.div(t, members), "fine": lax.rem(t, members)}
        t = (me + d) & (count - 1)
        return {
            "coarse": lax.shift_right_logical(t, members.bit_length() - 1),
            "fine": t & (members - 1),
        }

    def for_all(act):
        if count <= UNROLLED:
            for d in range(1, count):
                act(other(d))
        else:

            def one(d, carry):
                act(other(d))
                return carry

            lax.fori_loop(1, count, one, 0)

    inside_m = {b: (m + b >= 0) & (m + b < members) for b in columns}

    def greet_near(midway):
        highest = min(reach + 1, owners - 1)
        for a in range(-highest, highest + 1):
            if a == 0:
                midway()
            inside_o = (o + a >= 0) & (o + a < owners)
            for b in columns:
                if (a or b) and abs(a) <= height(b):

                    @pl.when(inside_o & inside_m[b])
                    def _(a=a, b=b):
                        pl.semaphore_signal(
                            barrier, inc=1, device_id={"coarse": o + a, "fine": m + b},
                            device_id_type=MESH,
                        )

    def for_near(act):
        def one(device):
            away_o, away_m = jnp.abs(device["coarse"] - o), jnp.abs(device["fine"] - m)
            steps = jnp.maximum(away_o - 1, 0) + jnp.maximum(away_m - 1, 0)
            pl.when(steps <= reach)(functools.partial(act, device))

        for_all(one)

    def load_matrices():
        for u in range(groups):
            mat_copy(u).start()

    greet_near(load_matrices)
    for copy in in_copies:
        copy.wait()

    def keys_of(source):
        row = lax.shift_right_logical(source, 7)
        turn = (jnp.bitwise_and(row, 7) - sub) & 7
        return jnp.bitwise_and(row, ~7) + turn, jnp.bitwise_and(source, 127)

    for g in range(groups):
        key, lanes = keys_of(cells_ref[g])
        key_in[g] = key
        lane_in[g] = lanes

    def load_turns(values):
        for g in range(len(values)):
            for turn in range(SUB):
                rot[g * SUB + turn] = (
                    values[g] if turn == 0 else pltpu.roll(values[g], SUB - turn, 0)
                )

    def permuted(key, lanes):
        parts = [zero, zero]
        for k in range(groups * SUB):
            parts[k % 2] = jnp.where(key == k, take(rot[k], lanes), parts[k % 2])
        return parts[0] + parts[1]

    both_lanes = 2 * LANES
    tall = lax.broadcasted_iota(jnp.int32, (groups * SUB, both_lanes), 0)
    taller = lax.broadcasted_iota(jnp.int32, (LANES, both_lanes), 0)
    place = lax.broadcasted_iota(jnp.int32, (groups * SUB, both_lanes), 1)
    second = jnp.where(place >= LANES, 1.0, 0.0)

    def narrow(values):
        return values.astype(jnp.float32).astype(jnp.bfloat16)

    tall, taller, place = narrow(tall), narrow(taller), narrow(place & (LANES - 1))
    one, nothing = jnp.bfloat16(1), jnp.bfloat16(0)
    parts = [jnp.zeros((2 * groups * SUB, LANES), jnp.float32)] * 2
    for g in range(groups):
        block = cells_ref[g]
        for b in range(0, SUB, 2):
            source = jnp.concatenate([block[b : b + 1, :], block[b + 1 : b + 2, :]], axis=1)
            row = narrow(lax.shift_right_logical(source, 7))
            hit = tall == jnp.broadcast_to(row, tall.shape)
            number = (second + (g * SUB + b)).astype(jnp.bfloat16)
            left = jnp.concatenate(
                [jnp.where(hit, number, nothing), jnp.where(hit, place, nothing)], axis=0
            )
            column = narrow(jnp.bitwise_and(source, LANES - 1))
            right = jnp.where(taller == jnp.broadcast_to(column, taller.shape), one, nothing)
            at = (b // 2) % 2
            parts[at] = parts[at] + lax.dot_general(
                left, right, (((1,), (1,)), ((), ())), preferred_element_type=jnp.float32
            )
    found = jnp.maximum(parts[0], parts[1]).astype(jnp.int32)
    for g in range(groups):
        block = found[g * SUB : (g + 1) * SUB]
        spot = found[(groups + g) * SUB : (groups + g + 1) * SUB]
        key, lanes = keys_of(block * LANES + spot)
        key_out[g] = key
        lane_out[g] = lanes

    small[...] = jnp.zeros(small.shape, jnp.float32)
    small[0, 0:1, 0 : table_ref.shape[1]] = table_ref[...]
    small[1, 0:1, 0 : diag_ref.shape[2]] = diag_ref[0]
    boxes = diag_ref.shape[2]
    table = full(small[0, 0:1, :])
    for x in range(MAIN):
        first_ext[x, 0] = take(table, cidx_ref[x])
        first_ext[x, 1] = (amap_ref[x] + 1).astype(jnp.float32)
        amaps[x] = amap_ref[x]

    def split(values):
        high = values.astype(jnp.bfloat16)
        low = (values - high.astype(jnp.float32)).astype(jnp.bfloat16)
        return high, low

    odd = (sub & 1) == 1

    def pick(values, keep):
        load_turns(values)
        for g in range(groups):
            keep[g] = permuted(key_in[g], lane_in[g])

    def block_apply(picked_of, done_with_dot, first=False, hook_at=None, hook=None):
        dot = zero
        picked = picked_of(0)
        for u in range(groups):
            if first and u % (groups // 2) == 0:
                for at in range(u, u + groups // 2):
                    mat_copy(at).wait()
            if first:
                for b in range(SUB):
                    high, low = split(mats[u * SUB + b])
                    pair, part = (u * SUB + b) // 2, pl.ds((b % 2) * LANES, LANES)
                    highs[pair, part] = high
                    lows[pair, part] = low
            upcoming = picked_of(u + 1) if u + 1 < groups else None
            if u == hook_at:
                hook()
            sides = []
            for keep_odd in (False, True):
                side = jnp.where(odd == keep_odd, picked, 0.0)
                sides.append(jnp.concatenate(split(side), axis=0))
            left = jnp.concatenate(sides, axis=1)
            product = zero
            for j in range(SUB // 2):
                pair = u * SUB // 2 + j
                right = jnp.concatenate([highs[pair], lows[pair]], axis=1)
                both = jnp.dot(left, right, preferred_element_type=jnp.float32)
                line = both[:SUB, :LANES] + (both[SUB:, :LANES] + both[:SUB, LANES:])
                line = line + both[SUB:, LANES:]
                product = jnp.where(lax.shift_right_logical(sub, 1) == j, line, product)
            moved[u] = product
            if done_with_dot is not None:
                dot = dot + picked * product
            picked = upcoming
        if done_with_dot is not None:
            done_with_dot(total_of(dot))
        load_turns([moved[g] for g in range(groups)])
        for g in range(groups):
            moved[g] = permuted(key_out[g], lane_out[g])
        return [moved[g] for g in range(groups)]

    def solve(values, done_with_dot, hook_at, hook):
        load_turns(values)
        return block_apply(
            lambda g: permuted(key_in[g], lane_in[g]), done_with_dot, False, hook_at, hook
        )

    base = lax.shift_right_logical(lane, 3)

    def restrict(values):
        sums = []
        for move in (-1, 0, 1):
            total = zero
            for x in range(MAIN):
                total = total + jnp.where(amaps[x] - base == move, values[x], 0.0)
            sums.append(total)
        total = pltpu.roll(sums[0], LANES - SUB, 1) + sums[1] + pltpu.roll(sums[2], SUB, 1)
        total = full(jnp.sum(total, axis=0, keepdims=True))
        for step in (1, 2, 4):
            total = total + pltpu.roll(total, LANES - step, 1)
        return jnp.where(lane < boxes, restrict_scale * take(total, (lane * SUB) & 127), 0.0)

    def row_copy(index, src, dst, device):
        return pltpu.make_async_remote_copy(
            src_ref=src, dst_ref=dst, send_sem=row_send.at[index], recv_sem=row_recv.at[index],
            device_id=device, device_id_type=MESH,
        )

    def put_row(index, row):
        row_src[index] = row[0:1, :]
        rows[index, me] = row[0:1, :]

    def send_rows(index, everywhere=False):
        (for_all if everywhere else for_near)(
            lambda device: row_copy(index, row_src.at[index], rows.at[index, me], device).start()
        )

    def wait_rows(index, everywhere=False):
        def wait_for(number):
            part = rows.at[index, pl.ds(0, number)]
            both = row_copy(index, part, part, other(1))
            both.wait_send()
            both.wait_recv()

        if everywhere:
            wait_for(count - 1)
        else:
            for number in near_counts:
                pl.when(near == number)(functools.partial(wait_for, number))
        return rows[index].reshape(count, LANES)

    def scalar(row, number):
        at = 2 * boxes + number
        return row[:, at : at + 1]

    def with_scalar(row, number, value):
        return jnp.where(lane == 2 * boxes + number, full(value), row)

    def edge_rows(values, z):
        result = zero
        for x in range(MAIN):
            result = jnp.where(sub == x, full(values[x][z : z + 1, :]), result)
        return result

    def halo_copies(ring, ext, cols, corner_src, corners):
        copies = []
        for do, dm in DIRECTIONS:
            if dm == 0:
                src = ext.at[MAIN - 1 if do == 1 else 0]
                dst = ext.at[XLO if do == 1 else XHI]
            elif do == 0:
                src = cols.at[1 if dm == 1 else 0]
                dst = ext.at[ZLO if dm == 1 else ZHI]
            else:
                at = 2 * (0 if do == 1 else 1) + (0 if dm == 1 else 1)
                src = corner_src.at[at]
                dst = corners.at[at]
            to_o, to_m = o + do, m + dm
            goes = (to_o >= 0) & (to_o < owners) & (to_m >= 0) & (to_m < members)
            copies.append(
                (
                    goes,
                    pltpu.make_async_remote_copy(
                        src_ref=src, dst_ref=dst,
                        send_sem=send_sems.at[ring], recv_sem=recv_sems.at[ring],
                        device_id={"coarse": to_o, "fine": to_m}, device_id_type=MESH,
                    ),
                )
            )
        return copies

    def pack_halo(fields, cols, corner_src):
        packs = [zero, zero, zero, zero]
        for f, values in enumerate(fields):
            cols[0, f] = edge_rows(values, 0)
            cols[1, f] = edge_rows(values, SUB - 1)
            for side_x in range(2):
                for side_z in range(2):
                    at = 2 * side_x + side_z
                    x = MAIN - 1 if side_x == 0 else 0
                    z = SUB - 1 if side_z == 0 else 0
                    packs[at] = jnp.where(sub == f, full(values[x][z : z + 1, :]), packs[at])
        for at in range(4):
            corner_src[at] = packs[at]

    def send_halo(ring, ext, cols, corner_src, corners):
        copies = halo_copies(ring, ext, cols, corner_src, corners)
        for goes, copy in copies:
            pl.when(goes)(copy.start)

    beside_o = (o > 0).astype(jnp.int32) + (o < owners - 1).astype(jnp.int32)
    beside_m = (m > 0).astype(jnp.int32) + (m < members - 1).astype(jnp.int32)

    def wait_halo(ring, fields):
        for number_o in range(3):
            for number_m in range(3):
                tiles = fields * (number_o + number_m) + number_o * number_m
                if tiles == 0:
                    continue

                @pl.when((beside_o == number_o) & (beside_m == number_m))
                def _(tiles=tiles):
                    part = rot.at[pl.ds(0, tiles)]
                    both = pltpu.make_async_remote_copy(
                        src_ref=part, dst_ref=part,
                        send_sem=send_sems.at[ring], recv_sem=recv_sems.at[ring],
                        device_id=other(1), device_id_type=MESH,
                    )
                    both.wait_send()
                    both.wait_recv()

    def corner_rows(corners, f):
        result = zero
        for at in range(4):
            result = jnp.where(sub == at, full(corners[at][f : f + 1, :]), result)
        return result

    def shifted(values, low, high):
        before = jnp.where(sub == 0, full(low), pltpu.roll(values, 1, 0))
        after = jnp.where(sub == SUB - 1, full(high), pltpu.roll(values, SUB - 1, 0))
        return values + 0.5 * (before + after)

    def smear(v):
        planes = [v[XLO]] + [v[x] for x in range(MAIN)] + [v[XHI]]
        corner = v[CORNER]
        low = shifted(v[ZLO], corner[0:1, :], corner[2:3, :])
        high = shifted(v[ZHI], corner[1:2, :], corner[3:4, :])
        result = []
        for x in range(MAIN):
            mid = planes[x + 1] + 0.5 * (planes[x] + planes[x + 2])
            mid = shifted(mid, low[x : x + 1, :], high[x : x + 1, :])
            before = jnp.where(lane == 0, 0.0, pltpu.roll(mid, 1, 1))
            after = jnp.where(lane == LANES - 1, 0.0, pltpu.roll(mid, LANES - 1, 1))
            result.append(mid + 0.5 * (before + after))
        return result

    node = lax.broadcasted_iota(jnp.int32, (count, LANES), 0)
    node_lane = lax.broadcasted_iota(jnp.int32, (count, LANES), 1)
    member = lax.rem(node, members)

    def coarse_solve(source, inverse):
        guess = omega * source * inverse
        for sweep in range(SWEEPS - 1):
            beside = pltpu.roll(guess, 1, 1) + pltpu.roll(guess, LANES - 1, 1)
            beside = beside + jnp.where(member == 0, 0.0, pltpu.roll(guess, 1, 0))
            beside = beside + jnp.where(
                member == members - 1, 0.0, pltpu.roll(guess, count - 1, 0)
            )
            beside = beside + jnp.where(node < members, 0.0, pltpu.roll(guess, members, 0))
            beside = beside + jnp.where(
                node >= count - members, 0.0, pltpu.roll(guess, count - members, 0)
            )
            guess = (1.0 - omega) * guess + omega * (source + beside) * inverse
        return guess

    def only_boxes(values):
        return jnp.where(node_lane < boxes, values, 0.0)

    def dot_of(left, right):
        total = zero
        for x in range(MAIN):
            total = total + left[x] * right[x]
        return total_of(total)

    start = [r_ref[x] for x in range(MAIN)]
    spread = full(small[1, 0:1, :])
    spread = jnp.where(lane < boxes, 1.0 / jnp.where(lane < boxes, 6.0 + spread, 1.0), 0.0)
    spread = pltpu.roll(spread, boxes, 1)
    first_row = restrict(start) + spread
    pick(start, picks)
    put_row(0, first_row)
    kappas = [first_ext[x, 0] for x in range(MAIN)]
    maps = [first_ext[x, 1] for x in range(MAIN)]
    pack_halo([kappas, maps], first_cols, first_corner_src)

    def open_up():
        pl.semaphore_wait(barrier, near)
        send_rows(0)
        send_halo(0, first_ext, first_cols, first_corner_src, first_corners)

    late = (o >= owners - max(1, owners // 4)) & (m >= members // 2)
    pl.when(late)(open_up)
    w = block_apply(lambda g: picks[g], None, True)
    for x in range(MAIN):
        w_ext[x, 0] = w[x]
    pack_halo([w], w_cols, w_corner_src)
    pl.when(jnp.logical_not(late))(open_up)
    send_halo(1, w_ext, w_cols, w_corner_src, w_corners)
    wait_halo(0, 2)
    for slot in range(SLOTS):
        if slot == CORNER:
            parts = [corner_rows(first_corners, f) for f in range(2)]
        else:
            parts = [first_ext[slot, f] for f in range(2)]
        kap[slot] = parts[0]
        if slot >= MAIN:
            amaps[slot] = (parts[1].astype(jnp.int32) + (LANES - 1)) & (LANES - 1)
    smeared = smear([kap[s] for s in range(SLOTS)])
    for x in range(MAIN):
        kt[x] = 8.0 * kap[x] + smeared[x]

    gathered = wait_rows(0)
    inverse = only_boxes(pltpu.roll(gathered, LANES - boxes, 1))
    guess = coarse_solve(only_boxes(gathered), inverse)

    def guess_rows(guess):
        picks = {}
        for do in (-1, 0, 1):
            for dm in (-1, 0, 1):
                wanted = me + do * members + dm
                picks[(do, dm)] = full(
                    jnp.sum(jnp.where(node == wanted, guess, 0.0), axis=0, keepdims=True)
                )
        return picks

    def coarse_parts(guess):
        picks_of = guess_rows(guess)
        result = []
        for x in range(MAIN):
            result.append(take(picks_of[(0, 0)], amaps[x]))
        for slot, way in ((XLO, (-1, 0)), (XHI, (1, 0)), (ZLO, (0, -1)), (ZHI, (0, 1))):
            result.append(take(picks_of[way], amaps[slot]))
        corner = zero
        for at, way in enumerate(((-1, -1), (-1, 1), (1, -1), (1, 1))):
            corner = jnp.where(sub == at, take(picks_of[way], amaps[CORNER]), corner)
        result.append(corner)
        return result

    def arrived(ring, ext, corners):
        wait_halo(ring, 1)
        return [ext[s, 0] for s in range(CORNER)] + [corner_rows(corners, 0)]

    def fine_operate(field, result):
        flat = smear(field)
        steep = smear([field[s] * kap[s] for s in range(SLOTS)])
        for x in range(MAIN):
            result[x] = field[x] * kt[x] - kap[x] * flat[x] - steep[x]

    coarse = coarse_parts(guess)
    z = [a + b for a, b in zip(arrived(1, w_ext, w_corners), coarse)]
    for slot in range(SLOTS):
        p_ext[slot] = z[slot]
    fine_operate(z, q_cur)
    image = [q_cur[x] for x in range(MAIN)]
    image_row = restrict(image)

    def send_image():
        put_row(1, image_row)
        send_rows(1)

    bq = solve(image, None, 0, send_image)
    for x in range(MAIN):
        b_ext[x, 0] = bq[x]
    pack_halo([bq], b_cols, b_corner_src)
    send_halo(2, b_ext, b_cols, b_corner_src, b_corners)
    r_dot_p = dot_of(r_ref, p_ext)
    p_dot_q = dot_of(p_ext, q_cur)
    coarse = coarse_parts(coarse_solve(only_boxes(wait_rows(1)), inverse))
    u = [a + b for a, b in zip(arrived(2, b_ext, b_corners), coarse)]
    for x in range(MAIN):
        u_ext[x] = u[x]
    fine_operate(u, v_cur)
    image = [v_cur[x] for x in range(MAIN)]
    row = restrict(image) + spread
    row = with_scalar(row, 0, r_dot_p)
    row = with_scalar(row, 1, p_dot_q)
    row = with_scalar(row, 2, dot_of(q_cur, u_ext))
    row = with_scalar(row, 3, dot_of(u_ext, v_cur))

    def send_moments():
        put_row(2, row)
        send_rows(2, True)

    def send_last(dot):
        put_row(3, full(dot))
        send_rows(3, True)

    bv = solve(image, send_last, groups // 2 - 1, send_moments)
    gathered = wait_rows(2, True)
    sums = jnp.sum(gathered, axis=0, keepdims=True)
    inverse = only_boxes(pltpu.roll(gathered, LANES - boxes, 1))
    source = only_boxes(gathered)
    guess = coarse_solve(source, inverse)
    coarse_part = full(total_of(source * guess) * (1.0 / restrict_scale))
    mu = [full(scalar(sums, number)) for number in range(4)]
    turn = 1.0 / mu[1]
    alpha0 = mu[0] * turn
    grow = alpha0 * mu[2] * turn
    curve = 1.0 / (alpha0 * alpha0 * mu[3] - grow * grow * mu[1])
    alpha1 = mu[0] * (grow - 1.0) * curve
    part = grow * grow * mu[2] - 2.0 * grow * alpha0 * mu[3] + alpha0 * alpha0 * coarse_part
    scale = alpha1 * curve
    own = full(jnp.sum(jnp.where(node == me, guess, 0.0), axis=0, keepdims=True))
    ahead, onward = [], []
    for x in range(MAIN):
        p0, q0, u0, v0 = p_ext[x], q_cur[x], u_ext[x], v_cur[x]
        t0 = bv[x] + take(own, amaps[x])
        p1 = grow * p0 - alpha0 * u0
        q1 = grow * q0 - alpha0 * v0
        x_out[x] = alpha0 * p0 + alpha1 * p1
        r_out[x] = r_ref[x] - alpha0 * q0 - alpha1 * q1
        ahead.append(p0 - alpha0 * u0 - alpha1 * (grow * u0 - alpha0 * t0))
        onward.append(p1)
    last = full(jnp.sum(wait_rows(3, True), axis=0, keepdims=True))
    beta1 = scale * (part + alpha0 * alpha0 * last) - 1.0
    for x in range(MAIN):
        p_out[x] = ahead[x] + beta1 * onward[x]


def emit(x_ref, r_ref, p_ref, x_out, r_out, p_out, sems):
    pairs = ((x_ref, x_out), (r_ref, r_out), (p_ref, p_out))
    copies = [pltpu.make_async_copy(a, b, sems.at[i]) for i, (a, b) in enumerate(pairs)]
    for copy in copies:
        copy.start()
    for copy in copies:
        copy.wait()


def shards(
    owners, members, right_side, coefficient_index, material_coefficients, block_cells,
    block_inverses, aggregate_map, coarse_diagonal,
):
    blocks, side = block_cells.shape[2], block_cells.shape[3]
    assert right_side.shape == (SUB, SUB, LANES) and side == LANES and blocks == SUB * SUB
    count = owners * members
    groups = blocks // SUB
    field = jax.ShapeDtypeStruct(right_side.shape, jnp.float32)
    vmem = pl.BlockSpec(memory_space=pltpu.VMEM)
    f32, i32 = jnp.float32, jnp.int32
    tile = (SUB, LANES)
    hbm = pl.BlockSpec(memory_space=pltpu.HBM)
    results = pl.pallas_call(
        functools.partial(kernel, owners, members),
        out_shape=(field, field, field),
        in_specs=[hbm] * 7,
        out_specs=(vmem, vmem, vmem),
        scratch_shapes=[
            pltpu.VMEM(right_side.shape, f32),
            pltpu.VMEM(right_side.shape, i32),
            pltpu.VMEM((1,) + material_coefficients.shape, f32),
            pltpu.VMEM((groups,) + tile, i32),
            pltpu.VMEM(right_side.shape, i32),
            pltpu.VMEM(coarse_diagonal.shape, f32),
            pltpu.SemaphoreType.DMA((6,)),
            pltpu.VMEM((blocks, side, side), f32),
            pltpu.VMEM((blocks // 2, 2 * side, side), jnp.bfloat16),
            pltpu.VMEM((blocks // 2, 2 * side, side), jnp.bfloat16),
            pltpu.VMEM((blocks,) + tile, f32),
            pltpu.VMEM((groups,) + tile, i32),
            pltpu.VMEM((groups,) + tile, i32),
            pltpu.VMEM((groups,) + tile, i32),
            pltpu.VMEM((groups,) + tile, i32),
            pltpu.VMEM((groups,) + tile, f32),
            pltpu.VMEM((CORNER, 2) + tile, f32),
            pltpu.VMEM((2, 2) + tile, f32),
            pltpu.VMEM((4,) + tile, f32),
            pltpu.VMEM((4,) + tile, f32),
            pltpu.VMEM((CORNER, 1) + tile, f32),
            pltpu.VMEM((2, 1) + tile, f32),
            pltpu.VMEM((4,) + tile, f32),
            pltpu.VMEM((4,) + tile, f32),
            pltpu.VMEM((CORNER, 1) + tile, f32),
            pltpu.VMEM((2, 1) + tile, f32),
            pltpu.VMEM((4,) + tile, f32),
            pltpu.VMEM((4,) + tile, f32),
            pltpu.VMEM((SLOTS,) + tile, f32),
            pltpu.VMEM((SLOTS,) + tile, i32),
            pltpu.VMEM((SLOTS,) + tile, f32),
            pltpu.VMEM((MAIN,) + tile, f32),
            pltpu.VMEM((MAIN,) + tile, f32),
            pltpu.VMEM((MAIN,) + tile, f32),
            pltpu.VMEM((MAIN,) + tile, f32),
            pltpu.VMEM((2,) + tile, f32),
            pltpu.VMEM((ROUNDS, 1, LANES), f32),
            pltpu.VMEM((ROUNDS, count, 1, LANES), f32),
            pltpu.VMEM((groups,) + tile, f32),
            pltpu.SemaphoreType.DMA((groups,)),
            pltpu.SemaphoreType.DMA((RINGS,)),
            pltpu.SemaphoreType.DMA((RINGS,)),
            pltpu.SemaphoreType.DMA((ROUNDS,)),
            pltpu.SemaphoreType.DMA((ROUNDS,)),
        ],
        compiler_params=pltpu.CompilerParams(
            collective_id=0, has_side_effects=True, vmem_limit_bytes=32 << 20
        ),
    )(
        *(pltpu.with_memory_space_constraint(a, pltpu.HBM) for a in (
        right_side,
        coefficient_index,
        material_coefficients.reshape(1, -1),
        block_cells.reshape(groups, SUB, LANES),
        block_inverses.reshape(blocks, side, side),
        aggregate_map,
        coarse_diagonal,
        ))
    )
    return pl.pallas_call(
        emit,
        out_shape=(field, field, field),
        in_specs=[vmem] * 3,
        out_specs=(hbm,) * 3,
        scratch_shapes=[pltpu.SemaphoreType.DMA((3,))],
        compiler_params=pltpu.CompilerParams(vmem_limit_bytes=1 << 20),
    )(*results)


def solution(mesh):
    three = P("coarse", "fine", None)
    return jax.shard_map(
        functools.partial(shards, mesh.shape["coarse"], mesh.shape["fine"]),
        mesh=mesh,
        in_specs=(
            three,
            three,
            P(),
            P("coarse", "fine", None, None),
            P("coarse", "fine", None, None, None),
            three,
            three,
        ),
        out_specs=(three, three, three),
        check_vma=False,
    )
```

```python
import functools

import jax
import jax.numpy as jnp
from jax import lax
from jax.experimental import pallas as pl
from jax.experimental.pallas import tpu as pltpu
from jax.sharding import PartitionSpec as P

RINGS = 3
ROUNDS = 4
UNROLLED = 64
WORD = 32
SWEEPS = 4
omega = 0.8
restrict_scale = 0.25
MESH = pl.DeviceIdType.MESH
SUB = 8
LANES = 128
MAIN = 8
XLO, XHI, ZLO, ZHI, CORNER = 8, 9, 10, 11, 12
SLOTS = 13
DIRECTIONS = ((-1, 0), (1, 0), (0, -1), (0, 1), (-1, -1), (-1, 1), (1, -1), (1, 1))


def take(values, lanes):
    return jnp.take_along_axis(values, lanes, axis=1, mode="promise_in_bounds")


def full(row):
    return jnp.broadcast_to(row, (SUB, LANES))


def total_of(values):
    return jnp.sum(jnp.sum(values, axis=0, keepdims=True), axis=1, keepdims=True)


def kernel(
    owners, members, r_hbm, cidx_hbm, table_hbm, cells_hbm, inv_ref, amap_hbm, diag_hbm,
    x_out, r_out, p_out,
    r_ref, cidx_ref, table_ref, cells_ref, amap_ref, diag_ref, in_sems,
    mats, highs, lows, rot, key_in, lane_in, key_out, lane_out, moved,
    first_ext, first_cols, first_corner_src, first_corners,
    w_ext, w_cols, w_corner_src, w_corners,
    b_ext, b_cols, b_corner_src, b_corners,
    kap, amaps, p_ext, u_ext, q_cur, v_cur, kt, small,
    row_src, rows, picks,
    mat_sems, send_sems, recv_sems, row_send, row_recv,
):
    count = owners * members
    o = lax.axis_index("coarse")
    m = lax.axis_index("fine")
    me = o * members + m
    groups = cells_ref.shape[0]
    sub = lax.broadcasted_iota(jnp.int32, (SUB, LANES), 0)
    lane = lax.broadcasted_iota(jnp.int32, (SUB, LANES), 1)
    zero = jnp.zeros((SUB, LANES), jnp.float32)

    in_copies = [
        pltpu.make_async_copy(src, dst, in_sems.at[at])
        for at, (src, dst) in enumerate(
            (
                (cells_hbm, cells_ref),
                (r_hbm, r_ref),
                (amap_hbm, amap_ref),
                (cidx_hbm, cidx_ref),
                (table_hbm, table_ref),
                (diag_hbm, diag_ref),
            )
        )
    ]
    for copy in in_copies:
        copy.start()
    def mat_copy(u):
        part = pl.ds(u * SUB, SUB)
        return pltpu.make_async_copy(inv_ref.at[part], mats.at[part], mat_sems.at[u])

    for slot in range(MAIN, CORNER):
        for f in range(2):
            first_ext[slot, f] = zero
        w_ext[slot, 0] = zero
        b_ext[slot, 0] = zero
    for c in range(4):
        first_corners[c] = zero
        w_corners[c] = zero
        b_corners[c] = zero
    rows[...] = jnp.zeros(rows.shape, jnp.float32)

    barrier = pltpu.get_barrier_semaphore()
    step_o, step_m = -(-(owners - 1) // 3), -(-(members - 1) // 3)
    reach = max(SWEEPS - 1, max(step_o - 1, 0) + max(step_m - 1, 0))

    def height(away):
        return reach - max(abs(away) - 1, 0) + 1

    columns = [b for b in range(1 - members, members) if height(b) > 0]

    def near_of(o, m, least, most):
        total = -1
        for b in columns:
            size = most(o - height(b), 0, least(o + height(b), owners - 1))
            total = total + size * ((m + b >= 0) & (m + b < members))
        return total

    near = near_of(
        o, m, jnp.minimum, lambda low, zero, high: high - jnp.maximum(low, zero) + 1
    )
    near_counts = sorted(
        {
            near_of(at_o, at_m, min, lambda low, zero, high: high - max(low, zero) + 1)
            for at_o in range(owners)
            for at_m in range(members)
        }
    )

    def other(d):
        if count & (count - 1) or members & (members - 1):
            t = lax.rem(me + d, count)
            return {"coarse": lax.div(t, members), "fine": lax.rem(t, members)}
        t = (me + d) & (count - 1)
        return {
            "coarse": lax.shift_right_logical(t, members.bit_length() - 1),
            "fine": t & (members - 1),
        }

    def for_all(act):
        if count <= UNROLLED:
            for d in range(1, count):
                act(other(d))
        else:

            def one(d, carry):
                act(other(d))
                return carry

            lax.fori_loop(1, count, one, 0)

    inside_m = {b: (m + b >= 0) & (m + b < members) for b in columns}

    def greet_near(midway):
        highest = min(reach + 1, owners - 1)
        for a in range(-highest, highest + 1):
            if a == 0:
                midway()
            inside_o = (o + a >= 0) & (o + a < owners)
            for b in columns:
                if (a or b) and abs(a) <= height(b):

                    @pl.when(inside_o & inside_m[b])
                    def _(a=a, b=b):
                        pl.semaphore_signal(
                            barrier, inc=1, device_id={"coarse": o + a, "fine": m + b},
                            device_id_type=MESH,
                        )

    def is_near(device):
        away_o, away_m = jnp.abs(device["coarse"] - o), jnp.abs(device["fine"] - m)
        return jnp.maximum(away_o - 1, 0) + jnp.maximum(away_m - 1, 0) <= reach

    def for_near(act):
        if count <= WORD:
            for d in range(1, count):
                pl.when((mask & (1 << (d - 1))) != 0)(functools.partial(act, other(d)))
        else:
            for_all(lambda device: pl.when(is_near(device))(functools.partial(act, device)))

    def load_matrices():
        for u in range(groups):
            mat_copy(u).start()

    greet_near(load_matrices)
    mask = jnp.int32(0)
    if count <= WORD:
        for d in range(1, count):
            mask = mask | (is_near(other(d)).astype(jnp.int32) << (d - 1))

    for copy in in_copies:
        copy.wait()

    def keys_of(source):
        row = lax.shift_right_logical(source, 7)
        turn = (jnp.bitwise_and(row, 7) - sub) & 7
        return jnp.bitwise_and(row, ~7) + turn, jnp.bitwise_and(source, 127)

    for g in range(groups):
        key, lanes = keys_of(cells_ref[g])
        key_in[g] = key
        lane_in[g] = lanes

    def load_turns(values):
        for g in range(len(values)):
            for turn in range(SUB):
                rot[g * SUB + turn] = (
                    values[g] if turn == 0 else pltpu.roll(values[g], SUB - turn, 0)
                )

    def permuted(key, lanes):
        parts = [zero, zero]
        for k in range(groups * SUB):
            parts[k % 2] = jnp.where(key == k, take(rot[k], lanes), parts[k % 2])
        return parts[0] + parts[1]

    both_lanes = 2 * LANES
    tall = lax.broadcasted_iota(jnp.int32, (groups * SUB, both_lanes), 0)
    taller = lax.broadcasted_iota(jnp.int32, (LANES, both_lanes), 0)
    place = lax.broadcasted_iota(jnp.int32, (groups * SUB, both_lanes), 1)
    second = jnp.where(place >= LANES, 1.0, 0.0)

    def narrow(values):
        return values.astype(jnp.float32).astype(jnp.bfloat16)

    tall, taller, place = narrow(tall), narrow(taller), narrow(place & (LANES - 1))
    one, nothing = jnp.bfloat16(1), jnp.bfloat16(0)
    parts = [jnp.zeros((2 * groups * SUB, LANES), jnp.float32)] * 2
    for g in range(groups):
        block = cells_ref[g]
        for b in range(0, SUB, 2):
            source = jnp.concatenate([block[b : b + 1, :], block[b + 1 : b + 2, :]], axis=1)
            row = narrow(lax.shift_right_logical(source, 7))
            hit = tall == jnp.broadcast_to(row, tall.shape)
            number = (second + (g * SUB + b)).astype(jnp.bfloat16)
            left = jnp.concatenate(
                [jnp.where(hit, number, nothing), jnp.where(hit, place, nothing)], axis=0
            )
            column = narrow(jnp.bitwise_and(source, LANES - 1))
            right = jnp.where(taller == jnp.broadcast_to(column, taller.shape), one, nothing)
            at = (b // 2) % 2
            parts[at] = parts[at] + lax.dot_general(
                left, right, (((1,), (1,)), ((), ())), preferred_element_type=jnp.float32
            )
    found = jnp.maximum(parts[0], parts[1]).astype(jnp.int32)
    for g in range(groups):
        block = found[g * SUB : (g + 1) * SUB]
        spot = found[(groups + g) * SUB : (groups + g + 1) * SUB]
        key, lanes = keys_of(block * LANES + spot)
        key_out[g] = key
        lane_out[g] = lanes

    small[...] = jnp.zeros(small.shape, jnp.float32)
    small[0, 0:1, 0 : table_ref.shape[1]] = table_ref[...]
    small[1, 0:1, 0 : diag_ref.shape[2]] = diag_ref[0]
    boxes = diag_ref.shape[2]
    table = full(small[0, 0:1, :])
    for x in range(MAIN):
        first_ext[x, 0] = take(table, cidx_ref[x])
        first_ext[x, 1] = (amap_ref[x] + 1).astype(jnp.float32)
        amaps[x] = amap_ref[x]

    def split(values):
        high = values.astype(jnp.bfloat16)
        low = (values - high.astype(jnp.float32)).astype(jnp.bfloat16)
        return high, low

    odd = (sub & 1) == 1

    def pick(values, keep):
        load_turns(values)
        for g in range(groups):
            keep[g] = permuted(key_in[g], lane_in[g])

    def block_apply(picked_of, done_with_dot, first=False, hook_at=None, hook=None):
        dot = zero
        picked = picked_of(0)
        for u in range(groups):
            if first and u % (groups // 2) == 0:
                for at in range(u, u + groups // 2):
                    mat_copy(at).wait()
            if first:
                for b in range(SUB):
                    high, low = split(mats[u * SUB + b])
                    pair, part = (u * SUB + b) // 2, pl.ds((b % 2) * LANES, LANES)
                    highs[pair, part] = high
                    lows[pair, part] = low
            upcoming = picked_of(u + 1) if u + 1 < groups else None
            if u == hook_at:
                hook()
            sides = []
            for keep_odd in (False, True):
                side = jnp.where(odd == keep_odd, picked, 0.0)
                sides.append(jnp.concatenate(split(side), axis=0))
            left = jnp.concatenate(sides, axis=1)
            product = zero
            for j in range(SUB // 2):
                pair = u * SUB // 2 + j
                right = jnp.concatenate([highs[pair], lows[pair]], axis=1)
                both = jnp.dot(left, right, preferred_element_type=jnp.float32)
                line = both[:SUB, :LANES] + (both[SUB:, :LANES] + both[:SUB, LANES:])
                line = line + both[SUB:, LANES:]
                product = jnp.where(lax.shift_right_logical(sub, 1) == j, line, product)
            moved[u] = product
            if done_with_dot is not None:
                dot = dot + picked * product
            picked = upcoming
        if done_with_dot is not None:
            done_with_dot(total_of(dot))
        load_turns([moved[g] for g in range(groups)])
        for g in range(groups):
            moved[g] = permuted(key_out[g], lane_out[g])
        return [moved[g] for g in range(groups)]

    def solve(values, done_with_dot, hook_at, hook):
        load_turns(values)
        return block_apply(
            lambda g: permuted(key_in[g], lane_in[g]), done_with_dot, False, hook_at, hook
        )

    base = lax.shift_right_logical(lane, 3)

    def restrict(values):
        sums = []
        for move in (-1, 0, 1):
            total = zero
            for x in range(MAIN):
                total = total + jnp.where(amaps[x] - base == move, values[x], 0.0)
            sums.append(total)
        total = pltpu.roll(sums[0], LANES - SUB, 1) + sums[1] + pltpu.roll(sums[2], SUB, 1)
        total = full(jnp.sum(total, axis=0, keepdims=True))
        for step in (1, 2, 4):
            total = total + pltpu.roll(total, LANES - step, 1)
        return jnp.where(lane < boxes, restrict_scale * take(total, (lane * SUB) & 127), 0.0)

    def row_copy(index, src, dst, device):
        return pltpu.make_async_remote_copy(
            src_ref=src, dst_ref=dst, send_sem=row_send.at[index], recv_sem=row_recv.at[index],
            device_id=device, device_id_type=MESH,
        )

    def put_row(index, row):
        row_src[index] = row[0:1, :]
        rows[index, me] = row[0:1, :]

    def send_rows(index, everywhere=False):
        (for_all if everywhere else for_near)(
            lambda device: row_copy(index, row_src.at[index], rows.at[index, me], device).start()
        )

    def wait_rows(index, everywhere=False):
        def wait_for(number):
            part = rows.at[index, pl.ds(0, number)]
            both = row_copy(index, part, part, other(1))
            both.wait_send()
            both.wait_recv()

        if everywhere:
            wait_for(count - 1)
        else:
            for number in near_counts:
                pl.when(near == number)(functools.partial(wait_for, number))
        return rows[index].reshape(count, LANES)

    def scalar(row, number):
        at = 2 * boxes + number
        return row[:, at : at + 1]

    def with_scalar(row, number, value):
        return jnp.where(lane == 2 * boxes + number, full(value), row)

    def edge_rows(values, z):
        result = zero
        for x in range(MAIN):
            result = jnp.where(sub == x, full(values[x][z : z + 1, :]), result)
        return result

    def halo_copies(ring, ext, cols, corner_src, corners):
        copies = []
        for do, dm in DIRECTIONS:
            if dm == 0:
                src = ext.at[MAIN - 1 if do == 1 else 0]
                dst = ext.at[XLO if do == 1 else XHI]
            elif do == 0:
                src = cols.at[1 if dm == 1 else 0]
                dst = ext.at[ZLO if dm == 1 else ZHI]
            else:
                at = 2 * (0 if do == 1 else 1) + (0 if dm == 1 else 1)
                src = corner_src.at[at]
                dst = corners.at[at]
            to_o, to_m = o + do, m + dm
            goes = (to_o >= 0) & (to_o < owners) & (to_m >= 0) & (to_m < members)
            copies.append(
                (
                    goes,
                    pltpu.make_async_remote_copy(
                        src_ref=src, dst_ref=dst,
                        send_sem=send_sems.at[ring], recv_sem=recv_sems.at[ring],
                        device_id={"coarse": to_o, "fine": to_m}, device_id_type=MESH,
                    ),
                )
            )
        return copies

    def pack_halo(fields, cols, corner_src):
        packs = [zero, zero, zero, zero]
        for f, values in enumerate(fields):
            cols[0, f] = edge_rows(values, 0)
            cols[1, f] = edge_rows(values, SUB - 1)
            for side_x in range(2):
                for side_z in range(2):
                    at = 2 * side_x + side_z
                    x = MAIN - 1 if side_x == 0 else 0
                    z = SUB - 1 if side_z == 0 else 0
                    packs[at] = jnp.where(sub == f, full(values[x][z : z + 1, :]), packs[at])
        for at in range(4):
            corner_src[at] = packs[at]

    def send_halo(ring, ext, cols, corner_src, corners):
        copies = halo_copies(ring, ext, cols, corner_src, corners)
        for goes, copy in copies:
            pl.when(goes)(copy.start)

    beside_o = (o > 0).astype(jnp.int32) + (o < owners - 1).astype(jnp.int32)
    beside_m = (m > 0).astype(jnp.int32) + (m < members - 1).astype(jnp.int32)

    def wait_halo(ring, fields):
        for number_o in range(3):
            for number_m in range(3):
                tiles = fields * (number_o + number_m) + number_o * number_m
                if tiles == 0:
                    continue

                @pl.when((beside_o == number_o) & (beside_m == number_m))
                def _(tiles=tiles):
                    part = rot.at[pl.ds(0, tiles)]
                    both = pltpu.make_async_remote_copy(
                        src_ref=part, dst_ref=part,
                        send_sem=send_sems.at[ring], recv_sem=recv_sems.at[ring],
                        device_id=other(1), device_id_type=MESH,
                    )
                    both.wait_send()
                    both.wait_recv()

    def corner_rows(corners, f):
        result = zero
        for at in range(4):
            result = jnp.where(sub == at, full(corners[at][f : f + 1, :]), result)
        return result

    def shifted(values, low, high):
        before = jnp.where(sub == 0, full(low), pltpu.roll(values, 1, 0))
        after = jnp.where(sub == SUB - 1, full(high), pltpu.roll(values, SUB - 1, 0))
        return values + 0.5 * (before + after)

    def smear(v):
        planes = [v[XLO]] + [v[x] for x in range(MAIN)] + [v[XHI]]
        corner = v[CORNER]
        low = shifted(v[ZLO], corner[0:1, :], corner[2:3, :])
        high = shifted(v[ZHI], corner[1:2, :], corner[3:4, :])
        result = []
        for x in range(MAIN):
            mid = planes[x + 1] + 0.5 * (planes[x] + planes[x + 2])
            mid = shifted(mid, low[x : x + 1, :], high[x : x + 1, :])
            before = jnp.where(lane == 0, 0.0, pltpu.roll(mid, 1, 1))
            after = jnp.where(lane == LANES - 1, 0.0, pltpu.roll(mid, LANES - 1, 1))
            result.append(mid + 0.5 * (before + after))
        return result

    node = lax.broadcasted_iota(jnp.int32, (count, LANES), 0)
    node_lane = lax.broadcasted_iota(jnp.int32, (count, LANES), 1)
    member = lax.rem(node, members)

    def coarse_solve(source, inverse):
        guess = omega * source * inverse
        for sweep in range(SWEEPS - 1):
            beside = pltpu.roll(guess, 1, 1) + pltpu.roll(guess, LANES - 1, 1)
            beside = beside + jnp.where(member == 0, 0.0, pltpu.roll(guess, 1, 0))
            beside = beside + jnp.where(
                member == members - 1, 0.0, pltpu.roll(guess, count - 1, 0)
            )
            beside = beside + jnp.where(node < members, 0.0, pltpu.roll(guess, members, 0))
            beside = beside + jnp.where(
                node >= count - members, 0.0, pltpu.roll(guess, count - members, 0)
            )
            guess = (1.0 - omega) * guess + omega * (source + beside) * inverse
        return guess

    def only_boxes(values):
        return jnp.where(node_lane < boxes, values, 0.0)

    def dot_of(left, right):
        total = zero
        for x in range(MAIN):
            total = total + left[x] * right[x]
        return total_of(total)

    start = [r_ref[x] for x in range(MAIN)]
    spread = full(small[1, 0:1, :])
    spread = jnp.where(lane < boxes, 1.0 / jnp.where(lane < boxes, 6.0 + spread, 1.0), 0.0)
    spread = pltpu.roll(spread, boxes, 1)
    first_row = restrict(start) + spread
    pick(start, picks)
    put_row(0, first_row)
    kappas = [first_ext[x, 0] for x in range(MAIN)]
    maps = [first_ext[x, 1] for x in range(MAIN)]
    pack_halo([kappas, maps], first_cols, first_corner_src)

    def open_up():
        pl.semaphore_wait(barrier, near)
        send_rows(0)
        send_halo(0, first_ext, first_cols, first_corner_src, first_corners)

    late = (o >= owners - max(1, owners // 4)) & (m >= members // 2)
    pl.when(late)(open_up)
    w = block_apply(lambda g: picks[g], None, True)
    for x in range(MAIN):
        w_ext[x, 0] = w[x]
    pack_halo([w], w_cols, w_corner_src)
    pl.when(jnp.logical_not(late))(open_up)
    send_halo(1, w_ext, w_cols, w_corner_src, w_corners)
    wait_halo(0, 2)
    for slot in range(SLOTS):
        if slot == CORNER:
            parts = [corner_rows(first_corners, f) for f in range(2)]
        else:
            parts = [first_ext[slot, f] for f in range(2)]
        kap[slot] = parts[0]
        if slot >= MAIN:
            amaps[slot] = (parts[1].astype(jnp.int32) + (LANES - 1)) & (LANES - 1)
    smeared = smear([kap[s] for s in range(SLOTS)])
    for x in range(MAIN):
        kt[x] = 8.0 * kap[x] + smeared[x]

    gathered = wait_rows(0)
    inverse = only_boxes(pltpu.roll(gathered, LANES - boxes, 1))
    guess = coarse_solve(only_boxes(gathered), inverse)

    def guess_rows(guess):
        picks = {}
        for do in (-1, 0, 1):
            for dm in (-1, 0, 1):
                wanted = me + do * members + dm
                picks[(do, dm)] = full(
                    jnp.sum(jnp.where(node == wanted, guess, 0.0), axis=0, keepdims=True)
                )
        return picks

    def coarse_parts(guess):
        picks_of = guess_rows(guess)
        result = []
        for x in range(MAIN):
            result.append(take(picks_of[(0, 0)], amaps[x]))
        for slot, way in ((XLO, (-1, 0)), (XHI, (1, 0)), (ZLO, (0, -1)), (ZHI, (0, 1))):
            result.append(take(picks_of[way], amaps[slot]))
        corner = zero
        for at, way in enumerate(((-1, -1), (-1, 1), (1, -1), (1, 1))):
            corner = jnp.where(sub == at, take(picks_of[way], amaps[CORNER]), corner)
        result.append(corner)
        return result

    def arrived(ring, ext, corners):
        wait_halo(ring, 1)
        return [ext[s, 0] for s in range(CORNER)] + [corner_rows(corners, 0)]

    def fine_operate(field, result):
        flat = smear(field)
        steep = smear([field[s] * kap[s] for s in range(SLOTS)])
        for x in range(MAIN):
            result[x] = field[x] * kt[x] - kap[x] * flat[x] - steep[x]

    coarse = coarse_parts(guess)
    z = [a + b for a, b in zip(arrived(1, w_ext, w_corners), coarse)]
    for slot in range(SLOTS):
        p_ext[slot] = z[slot]
    fine_operate(z, q_cur)
    image = [q_cur[x] for x in range(MAIN)]
    image_row = restrict(image)

    def send_image():
        put_row(1, image_row)
        send_rows(1)

    bq = solve(image, None, 0, send_image)
    for x in range(MAIN):
        b_ext[x, 0] = bq[x]
    pack_halo([bq], b_cols, b_corner_src)
    send_halo(2, b_ext, b_cols, b_corner_src, b_corners)
    r_dot_p = dot_of(r_ref, p_ext)
    p_dot_q = dot_of(p_ext, q_cur)
    coarse = coarse_parts(coarse_solve(only_boxes(wait_rows(1)), inverse))
    u = [a + b for a, b in zip(arrived(2, b_ext, b_corners), coarse)]
    for x in range(MAIN):
        u_ext[x] = u[x]
    fine_operate(u, v_cur)
    image = [v_cur[x] for x in range(MAIN)]
    row = restrict(image) + spread
    row = with_scalar(row, 0, r_dot_p)
    row = with_scalar(row, 1, p_dot_q)
    row = with_scalar(row, 2, dot_of(q_cur, u_ext))
    row = with_scalar(row, 3, dot_of(u_ext, v_cur))

    def send_moments():
        put_row(2, row)
        send_rows(2, True)

    def send_last(dot):
        put_row(3, full(dot))
        send_rows(3, True)

    bv = solve(image, send_last, groups // 2 - 1, send_moments)
    gathered = wait_rows(2, True)
    sums = jnp.sum(gathered, axis=0, keepdims=True)
    inverse = only_boxes(pltpu.roll(gathered, LANES - boxes, 1))
    source = only_boxes(gathered)
    guess = coarse_solve(source, inverse)
    coarse_part = full(total_of(source * guess) * (1.0 / restrict_scale))
    mu = [full(scalar(sums, number)) for number in range(4)]
    turn = 1.0 / mu[1]
    alpha0 = mu[0] * turn
    grow = alpha0 * mu[2] * turn
    curve = 1.0 / (alpha0 * alpha0 * mu[3] - grow * grow * mu[1])
    alpha1 = mu[0] * (grow - 1.0) * curve
    part = grow * grow * mu[2] - 2.0 * grow * alpha0 * mu[3] + alpha0 * alpha0 * coarse_part
    scale = alpha1 * curve
    own = full(jnp.sum(jnp.where(node == me, guess, 0.0), axis=0, keepdims=True))
    ahead, onward = [], []
    for x in range(MAIN):
        p0, q0, u0, v0 = p_ext[x], q_cur[x], u_ext[x], v_cur[x]
        t0 = bv[x] + take(own, amaps[x])
        p1 = grow * p0 - alpha0 * u0
        q1 = grow * q0 - alpha0 * v0
        x_out[x] = alpha0 * p0 + alpha1 * p1
        r_out[x] = r_ref[x] - alpha0 * q0 - alpha1 * q1
        ahead.append(p0 - alpha0 * u0 - alpha1 * (grow * u0 - alpha0 * t0))
        onward.append(p1)
    last = full(jnp.sum(wait_rows(3, True), axis=0, keepdims=True))
    beta1 = scale * (part + alpha0 * alpha0 * last) - 1.0
    for x in range(MAIN):
        p_out[x] = ahead[x] + beta1 * onward[x]


def emit(x_ref, r_ref, p_ref, x_out, r_out, p_out, sems):
    pairs = ((x_ref, x_out), (r_ref, r_out), (p_ref, p_out))
    copies = [pltpu.make_async_copy(a, b, sems.at[i]) for i, (a, b) in enumerate(pairs)]
    for copy in copies:
        copy.start()
    for copy in copies:
        copy.wait()


def shards(
    owners, members, right_side, coefficient_index, material_coefficients, block_cells,
    block_inverses, aggregate_map, coarse_diagonal,
):
    blocks, side = block_cells.shape[2], block_cells.shape[3]
    assert right_side.shape == (SUB, SUB, LANES) and side == LANES and blocks == SUB * SUB
    count = owners * members
    groups = blocks // SUB
    field = jax.ShapeDtypeStruct(right_side.shape, jnp.float32)
    vmem = pl.BlockSpec(memory_space=pltpu.VMEM)
    f32, i32 = jnp.float32, jnp.int32
    tile = (SUB, LANES)
    hbm = pl.BlockSpec(memory_space=pltpu.HBM)
    results = pl.pallas_call(
        functools.partial(kernel, owners, members),
        out_shape=(field, field, field),
        in_specs=[hbm] * 7,
        out_specs=(vmem, vmem, vmem),
        scratch_shapes=[
            pltpu.VMEM(right_side.shape, f32),
            pltpu.VMEM(right_side.shape, i32),
            pltpu.VMEM((1,) + material_coefficients.shape, f32),
            pltpu.VMEM((groups,) + tile, i32),
            pltpu.VMEM(right_side.shape, i32),
            pltpu.VMEM(coarse_diagonal.shape, f32),
            pltpu.SemaphoreType.DMA((6,)),
            pltpu.VMEM((blocks, side, side), f32),
            pltpu.VMEM((blocks // 2, 2 * side, side), jnp.bfloat16),
            pltpu.VMEM((blocks // 2, 2 * side, side), jnp.bfloat16),
            pltpu.VMEM((blocks,) + tile, f32),
            pltpu.VMEM((groups,) + tile, i32),
            pltpu.VMEM((groups,) + tile, i32),
            pltpu.VMEM((groups,) + tile, i32),
            pltpu.VMEM((groups,) + tile, i32),
            pltpu.VMEM((groups,) + tile, f32),
            pltpu.VMEM((CORNER, 2) + tile, f32),
            pltpu.VMEM((2, 2) + tile, f32),
            pltpu.VMEM((4,) + tile, f32),
            pltpu.VMEM((4,) + tile, f32),
            pltpu.VMEM((CORNER, 1) + tile, f32),
            pltpu.VMEM((2, 1) + tile, f32),
            pltpu.VMEM((4,) + tile, f32),
            pltpu.VMEM((4,) + tile, f32),
            pltpu.VMEM((CORNER, 1) + tile, f32),
            pltpu.VMEM((2, 1) + tile, f32),
            pltpu.VMEM((4,) + tile, f32),
            pltpu.VMEM((4,) + tile, f32),
            pltpu.VMEM((SLOTS,) + tile, f32),
            pltpu.VMEM((SLOTS,) + tile, i32),
            pltpu.VMEM((SLOTS,) + tile, f32),
            pltpu.VMEM((MAIN,) + tile, f32),
            pltpu.VMEM((MAIN,) + tile, f32),
            pltpu.VMEM((MAIN,) + tile, f32),
            pltpu.VMEM((MAIN,) + tile, f32),
            pltpu.VMEM((2,) + tile, f32),
            pltpu.VMEM((ROUNDS, 1, LANES), f32),
            pltpu.VMEM((ROUNDS, count, 1, LANES), f32),
            pltpu.VMEM((groups,) + tile, f32),
            pltpu.SemaphoreType.DMA((groups,)),
            pltpu.SemaphoreType.DMA((RINGS,)),
            pltpu.SemaphoreType.DMA((RINGS,)),
            pltpu.SemaphoreType.DMA((ROUNDS,)),
            pltpu.SemaphoreType.DMA((ROUNDS,)),
        ],
        compiler_params=pltpu.CompilerParams(
            collective_id=0, has_side_effects=True, vmem_limit_bytes=32 << 20
        ),
    )(
        *(pltpu.with_memory_space_constraint(a, pltpu.HBM) for a in (
        right_side,
        coefficient_index,
        material_coefficients.reshape(1, -1),
        block_cells.reshape(groups, SUB, LANES),
        block_inverses.reshape(blocks, side, side),
        aggregate_map,
        coarse_diagonal,
        ))
    )
    return pl.pallas_call(
        emit,
        out_shape=(field, field, field),
        in_specs=[vmem] * 3,
        out_specs=(hbm,) * 3,
        scratch_shapes=[pltpu.SemaphoreType.DMA((3,))],
        compiler_params=pltpu.CompilerParams(vmem_limit_bytes=1 << 20),
    )(*results)


def solution(mesh):
    three = P("coarse", "fine", None)
    return jax.shard_map(
        functools.partial(shards, mesh.shape["coarse"], mesh.shape["fine"]),
        mesh=mesh,
        in_specs=(
            three,
            three,
            P(),
            P("coarse", "fine", None, None),
            P("coarse", "fine", None, None, None),
            three,
            three,
        ),
        out_specs=(three, three, three),
        check_vma=False,
    )
```

```python
import functools

import jax
import jax.numpy as jnp
from jax import lax
from jax.experimental import pallas as pl
from jax.experimental.pallas import tpu as pltpu
from jax.sharding import PartitionSpec as P

RINGS = 3
ROUNDS = 4
UNROLLED = 64
WORD = 32
SWEEPS = 4
omega = 0.8
restrict_scale = 0.25
MESH = pl.DeviceIdType.MESH
SUB = 8
LANES = 128
MAIN = 8
XLO, XHI, ZLO, ZHI, CORNER = 8, 9, 10, 11, 12
SLOTS = 13
DIRECTIONS = ((-1, 0), (1, 0), (0, -1), (0, 1), (-1, -1), (-1, 1), (1, -1), (1, 1))


def take(values, lanes):
    return jnp.take_along_axis(values, lanes, axis=1, mode="promise_in_bounds")


def full(row):
    return jnp.broadcast_to(row, (SUB, LANES))


def total_of(values):
    return jnp.sum(jnp.sum(values, axis=0, keepdims=True), axis=1, keepdims=True)


def kernel(
    owners, members, r_hbm, cidx_hbm, table_hbm, cells_hbm, inv_ref, amap_hbm, diag_hbm,
    x_out, r_out, p_out,
    r_ref, cidx_ref, table_ref, cells_ref, amap_ref, diag_ref, in_sems,
    mats, highs, lows, rot, key_in, lane_in, key_out, lane_out, moved,
    first_ext, first_cols, first_corner_src, first_corners,
    w_ext, w_cols, w_corner_src, w_corners,
    b_ext, b_cols, b_corner_src, b_corners,
    kap, amaps, p_ext, u_ext, q_cur, v_cur, kt, small,
    row_src, rows, picks,
    mat_sems, send_sems, recv_sems, row_send, row_recv,
):
    count = owners * members
    o = lax.axis_index("coarse")
    m = lax.axis_index("fine")
    me = o * members + m
    groups = cells_ref.shape[0]
    sub = lax.broadcasted_iota(jnp.int32, (SUB, LANES), 0)
    lane = lax.broadcasted_iota(jnp.int32, (SUB, LANES), 1)
    zero = jnp.zeros((SUB, LANES), jnp.float32)

    in_copies = [
        pltpu.make_async_copy(src, dst, in_sems.at[at])
        for at, (src, dst) in enumerate(
            (
                (cells_hbm, cells_ref),
                (r_hbm, r_ref),
                (amap_hbm, amap_ref),
                (cidx_hbm, cidx_ref),
                (table_hbm, table_ref),
                (diag_hbm, diag_ref),
            )
        )
    ]
    for copy in in_copies:
        copy.start()
    def mat_copy(u):
        part = pl.ds(u * SUB, SUB)
        return pltpu.make_async_copy(inv_ref.at[part], mats.at[part], mat_sems.at[u])

    for slot in range(MAIN, CORNER):
        for f in range(2):
            first_ext[slot, f] = zero
        w_ext[slot, 0] = zero
        b_ext[slot, 0] = zero
    for c in range(4):
        first_corners[c] = zero
        w_corners[c] = zero
        b_corners[c] = zero
    rows[...] = jnp.zeros(rows.shape, jnp.float32)

    barrier = pltpu.get_barrier_semaphore()
    step_o, step_m = -(-(owners - 1) // 3), -(-(members - 1) // 3)
    reach = max(SWEEPS - 1, max(step_o - 1, 0) + max(step_m - 1, 0))

    def height(away):
        return reach - max(abs(away) - 1, 0) + 1

    columns = [b for b in range(1 - members, members) if height(b) > 0]

    def near_of(o, m, least, most):
        total = -1
        for b in columns:
            size = most(o - height(b), 0, least(o + height(b), owners - 1))
            total = total + size * ((m + b >= 0) & (m + b < members))
        return total

    near = near_of(
        o, m, jnp.minimum, lambda low, zero, high: high - jnp.maximum(low, zero) + 1
    )
    near_counts = sorted(
        {
            near_of(at_o, at_m, min, lambda low, zero, high: high - max(low, zero) + 1)
            for at_o in range(owners)
            for at_m in range(members)
        }
    )

    def other(d):
        if count & (count - 1) or members & (members - 1):
            t = lax.rem(me + d, count)
            return {"coarse": lax.div(t, members), "fine": lax.rem(t, members)}
        t = (me + d) & (count - 1)
        return {
            "coarse": lax.shift_right_logical(t, members.bit_length() - 1),
            "fine": t & (members - 1),
        }

    def for_all(act):
        def one(t):
            device = {"coarse": t // members, "fine": t % members}
            pl.when(me != t)(functools.partial(act, device))

        if count <= UNROLLED:
            for t in range(count):
                one(t)
        else:

            def step(t, carry):
                one(t)
                return carry

            lax.fori_loop(0, count, step, 0)

    inside_m = {b: (m + b >= 0) & (m + b < members) for b in columns}

    def greet_near(midway):
        highest = min(reach + 1, owners - 1)
        for a in range(-highest, highest + 1):
            if a == 0:
                midway()
            inside_o = (o + a >= 0) & (o + a < owners)
            for b in columns:
                if (a or b) and abs(a) <= height(b):

                    @pl.when(inside_o & inside_m[b])
                    def _(a=a, b=b):
                        pl.semaphore_signal(
                            barrier, inc=1, device_id={"coarse": o + a, "fine": m + b},
                            device_id_type=MESH,
                        )

    def is_near(device):
        away_o, away_m = jnp.abs(device["coarse"] - o), jnp.abs(device["fine"] - m)
        return jnp.maximum(away_o - 1, 0) + jnp.maximum(away_m - 1, 0) <= reach

    def for_near(act):
        if count <= WORD:
            for d in range(1, count):
                pl.when((mask & (1 << (d - 1))) != 0)(functools.partial(act, other(d)))
        else:
            for_all(lambda device: pl.when(is_near(device))(functools.partial(act, device)))

    def load_matrices():
        for u in range(groups):
            mat_copy(u).start()

    greet_near(load_matrices)
    mask = jnp.int32(0)
    if count <= WORD:
        for d in range(1, count):
            mask = mask | (is_near(other(d)).astype(jnp.int32) << (d - 1))

    for copy in in_copies:
        copy.wait()

    def keys_of(source):
        row = lax.shift_right_logical(source, 7)
        turn = (jnp.bitwise_and(row, 7) - sub) & 7
        return jnp.bitwise_and(row, ~7) + turn, jnp.bitwise_and(source, 127)

    for g in range(groups):
        key, lanes = keys_of(cells_ref[g])
        key_in[g] = key
        lane_in[g] = lanes

    def load_turns(values):
        for g in range(len(values)):
            for turn in range(SUB):
                rot[g * SUB + turn] = (
                    values[g] if turn == 0 else pltpu.roll(values[g], SUB - turn, 0)
                )

    def permuted(key, lanes):
        parts = [zero, zero]
        for k in range(groups * SUB):
            parts[k % 2] = jnp.where(key == k, take(rot[k], lanes), parts[k % 2])
        return parts[0] + parts[1]

    both_lanes = 2 * LANES
    tall = lax.broadcasted_iota(jnp.int32, (groups * SUB, both_lanes), 0)
    taller = lax.broadcasted_iota(jnp.int32, (LANES, both_lanes), 0)
    place = lax.broadcasted_iota(jnp.int32, (groups * SUB, both_lanes), 1)
    second = jnp.where(place >= LANES, 1.0, 0.0)

    def narrow(values):
        return values.astype(jnp.float32).astype(jnp.bfloat16)

    tall, taller, place = narrow(tall), narrow(taller), narrow(place & (LANES - 1))
    one, nothing = jnp.bfloat16(1), jnp.bfloat16(0)
    parts = [jnp.zeros((2 * groups * SUB, LANES), jnp.float32)] * 2
    for g in range(groups):
        block = cells_ref[g]
        for b in range(0, SUB, 2):
            source = jnp.concatenate([block[b : b + 1, :], block[b + 1 : b + 2, :]], axis=1)
            row = narrow(lax.shift_right_logical(source, 7))
            hit = tall == jnp.broadcast_to(row, tall.shape)
            number = (second + (g * SUB + b)).astype(jnp.bfloat16)
            left = jnp.concatenate(
                [jnp.where(hit, number, nothing), jnp.where(hit, place, nothing)], axis=0
            )
            column = narrow(jnp.bitwise_and(source, LANES - 1))
            right = jnp.where(taller == jnp.broadcast_to(column, taller.shape), one, nothing)
            at = (b // 2) % 2
            parts[at] = parts[at] + lax.dot_general(
                left, right, (((1,), (1,)), ((), ())), preferred_element_type=jnp.float32
            )
    found = jnp.maximum(parts[0], parts[1]).astype(jnp.int32)
    for g in range(groups):
        block = found[g * SUB : (g + 1) * SUB]
        spot = found[(groups + g) * SUB : (groups + g + 1) * SUB]
        key, lanes = keys_of(block * LANES + spot)
        key_out[g] = key
        lane_out[g] = lanes

    small[...] = jnp.zeros(small.shape, jnp.float32)
    small[0, 0:1, 0 : table_ref.shape[1]] = table_ref[...]
    small[1, 0:1, 0 : diag_ref.shape[2]] = diag_ref[0]
    boxes = diag_ref.shape[2]
    table = full(small[0, 0:1, :])
    for x in range(MAIN):
        first_ext[x, 0] = take(table, cidx_ref[x])
        first_ext[x, 1] = (amap_ref[x] + 1).astype(jnp.float32)
        amaps[x] = amap_ref[x]

    def split(values):
        high = values.astype(jnp.bfloat16)
        low = (values - high.astype(jnp.float32)).astype(jnp.bfloat16)
        return high, low

    odd = (sub & 1) == 1

    def pick(values, keep):
        load_turns(values)
        for g in range(groups):
            keep[g] = permuted(key_in[g], lane_in[g])

    def block_apply(picked_of, done_with_dot, first=False, hook_at=None, hook=None):
        dot = zero
        picked = picked_of(0)
        for u in range(groups):
            if first and u % (groups // 2) == 0:
                for at in range(u, u + groups // 2):
                    mat_copy(at).wait()
            if first:
                for b in range(SUB):
                    high, low = split(mats[u * SUB + b])
                    pair, part = (u * SUB + b) // 2, pl.ds((b % 2) * LANES, LANES)
                    highs[pair, part] = high
                    lows[pair, part] = low
            upcoming = picked_of(u + 1) if u + 1 < groups else None
            if u == hook_at:
                hook()
            sides = []
            for keep_odd in (False, True):
                side = jnp.where(odd == keep_odd, picked, 0.0)
                sides.append(jnp.concatenate(split(side), axis=0))
            left = jnp.concatenate(sides, axis=1)
            product = zero
            for j in range(SUB // 2):
                pair = u * SUB // 2 + j
                right = jnp.concatenate([highs[pair], lows[pair]], axis=1)
                both = jnp.dot(left, right, preferred_element_type=jnp.float32)
                line = both[:SUB, :LANES] + (both[SUB:, :LANES] + both[:SUB, LANES:])
                line = line + both[SUB:, LANES:]
                product = jnp.where(lax.shift_right_logical(sub, 1) == j, line, product)
            moved[u] = product
            if done_with_dot is not None:
                dot = dot + picked * product
            picked = upcoming
        if done_with_dot is not None:
            done_with_dot(total_of(dot))
        load_turns([moved[g] for g in range(groups)])
        for g in range(groups):
            moved[g] = permuted(key_out[g], lane_out[g])
        return [moved[g] for g in range(groups)]

    def solve(values, done_with_dot, hook_at, hook):
        load_turns(values)
        return block_apply(
            lambda g: permuted(key_in[g], lane_in[g]), done_with_dot, False, hook_at, hook
        )

    base = lax.shift_right_logical(lane, 3)

    def restrict(values):
        sums = []
        for move in (-1, 0, 1):
            total = zero
            for x in range(MAIN):
                total = total + jnp.where(amaps[x] - base == move, values[x], 0.0)
            sums.append(total)
        total = pltpu.roll(sums[0], LANES - SUB, 1) + sums[1] + pltpu.roll(sums[2], SUB, 1)
        total = full(jnp.sum(total, axis=0, keepdims=True))
        for step in (1, 2, 4):
            total = total + pltpu.roll(total, LANES - step, 1)
        return jnp.where(lane < boxes, restrict_scale * take(total, (lane * SUB) & 127), 0.0)

    def row_copy(index, src, dst, device):
        return pltpu.make_async_remote_copy(
            src_ref=src, dst_ref=dst, send_sem=row_send.at[index], recv_sem=row_recv.at[index],
            device_id=device, device_id_type=MESH,
        )

    def put_row(index, row):
        row_src[index] = row[0:1, :]
        rows[index, me] = row[0:1, :]

    def send_rows(index, everywhere=False):
        (for_all if everywhere else for_near)(
            lambda device: row_copy(index, row_src.at[index], rows.at[index, me], device).start()
        )

    def wait_rows(index, everywhere=False):
        def wait_for(number):
            part = rows.at[index, pl.ds(0, number)]
            both = row_copy(index, part, part, other(1))
            both.wait_send()
            both.wait_recv()

        if everywhere:
            wait_for(count - 1)
        else:
            for number in near_counts:
                pl.when(near == number)(functools.partial(wait_for, number))
        return rows[index].reshape(count, LANES)

    def scalar(row, number):
        at = 2 * boxes + number
        return row[:, at : at + 1]

    def with_scalar(row, number, value):
        return jnp.where(lane == 2 * boxes + number, full(value), row)

    def edge_rows(values, z):
        result = zero
        for x in range(MAIN):
            result = jnp.where(sub == x, full(values[x][z : z + 1, :]), result)
        return result

    def halo_copies(ring, ext, cols, corner_src, corners):
        copies = []
        for do, dm in DIRECTIONS:
            if dm == 0:
                src = ext.at[MAIN - 1 if do == 1 else 0]
                dst = ext.at[XLO if do == 1 else XHI]
            elif do == 0:
                src = cols.at[1 if dm == 1 else 0]
                dst = ext.at[ZLO if dm == 1 else ZHI]
            else:
                at = 2 * (0 if do == 1 else 1) + (0 if dm == 1 else 1)
                src = corner_src.at[at]
                dst = corners.at[at]
            to_o, to_m = o + do, m + dm
            goes = (to_o >= 0) & (to_o < owners) & (to_m >= 0) & (to_m < members)
            copies.append(
                (
                    goes,
                    pltpu.make_async_remote_copy(
                        src_ref=src, dst_ref=dst,
                        send_sem=send_sems.at[ring], recv_sem=recv_sems.at[ring],
                        device_id={"coarse": to_o, "fine": to_m}, device_id_type=MESH,
                    ),
                )
            )
        return copies

    def pack_halo(fields, cols, corner_src):
        packs = [zero, zero, zero, zero]
        for f, values in enumerate(fields):
            cols[0, f] = edge_rows(values, 0)
            cols[1, f] = edge_rows(values, SUB - 1)
            for side_x in range(2):
                for side_z in range(2):
                    at = 2 * side_x + side_z
                    x = MAIN - 1 if side_x == 0 else 0
                    z = SUB - 1 if side_z == 0 else 0
                    packs[at] = jnp.where(sub == f, full(values[x][z : z + 1, :]), packs[at])
        for at in range(4):
            corner_src[at] = packs[at]

    def send_halo(ring, ext, cols, corner_src, corners):
        copies = halo_copies(ring, ext, cols, corner_src, corners)
        for goes, copy in copies:
            pl.when(goes)(copy.start)

    beside_o = (o > 0).astype(jnp.int32) + (o < owners - 1).astype(jnp.int32)
    beside_m = (m > 0).astype(jnp.int32) + (m < members - 1).astype(jnp.int32)

    def wait_halo(ring, fields):
        for number_o in range(3):
            for number_m in range(3):
                tiles = fields * (number_o + number_m) + number_o * number_m
                if tiles == 0:
                    continue

                @pl.when((beside_o == number_o) & (beside_m == number_m))
                def _(tiles=tiles):
                    part = rot.at[pl.ds(0, tiles)]
                    both = pltpu.make_async_remote_copy(
                        src_ref=part, dst_ref=part,
                        send_sem=send_sems.at[ring], recv_sem=recv_sems.at[ring],
                        device_id=other(1), device_id_type=MESH,
                    )
                    both.wait_send()
                    both.wait_recv()

    def corner_rows(corners, f):
        result = zero
        for at in range(4):
            result = jnp.where(sub == at, full(corners[at][f : f + 1, :]), result)
        return result

    def shifted(values, low, high):
        before = jnp.where(sub == 0, full(low), pltpu.roll(values, 1, 0))
        after = jnp.where(sub == SUB - 1, full(high), pltpu.roll(values, SUB - 1, 0))
        return values + 0.5 * (before + after)

    def smear(v):
        planes = [v[XLO]] + [v[x] for x in range(MAIN)] + [v[XHI]]
        corner = v[CORNER]
        low = shifted(v[ZLO], corner[0:1, :], corner[2:3, :])
        high = shifted(v[ZHI], corner[1:2, :], corner[3:4, :])
        result = []
        for x in range(MAIN):
            mid = planes[x + 1] + 0.5 * (planes[x] + planes[x + 2])
            mid = shifted(mid, low[x : x + 1, :], high[x : x + 1, :])
            before = jnp.where(lane == 0, 0.0, pltpu.roll(mid, 1, 1))
            after = jnp.where(lane == LANES - 1, 0.0, pltpu.roll(mid, LANES - 1, 1))
            result.append(mid + 0.5 * (before + after))
        return result

    node = lax.broadcasted_iota(jnp.int32, (count, LANES), 0)
    node_lane = lax.broadcasted_iota(jnp.int32, (count, LANES), 1)
    member = lax.rem(node, members)

    def coarse_solve(source, inverse):
        pull = omega * inverse
        push = source * pull
        guess = push
        for sweep in range(SWEEPS - 1):
            sides = pltpu.roll(guess, 1, 1) + pltpu.roll(guess, LANES - 1, 1)
            left = jnp.where(member == 0, 0.0, pltpu.roll(guess, 1, 0))
            right = jnp.where(member == members - 1, 0.0, pltpu.roll(guess, count - 1, 0))
            low = jnp.where(node < members, 0.0, pltpu.roll(guess, members, 0))
            high = jnp.where(
                node >= count - members, 0.0, pltpu.roll(guess, count - members, 0)
            )
            beside = sides + ((left + right) + (low + high))
            guess = ((1.0 - omega) * guess + push) + pull * beside
        return guess

    def only_boxes(values):
        return jnp.where(node_lane < boxes, values, 0.0)

    def dot_of(left, right):
        total = zero
        for x in range(MAIN):
            total = total + left[x] * right[x]
        return total_of(total)

    start = [r_ref[x] for x in range(MAIN)]
    spread = full(small[1, 0:1, :])
    spread = jnp.where(lane < boxes, 1.0 / jnp.where(lane < boxes, 6.0 + spread, 1.0), 0.0)
    spread = pltpu.roll(spread, boxes, 1)
    first_row = restrict(start) + spread
    pick(start, picks)
    put_row(0, first_row)
    kappas = [first_ext[x, 0] for x in range(MAIN)]
    maps = [first_ext[x, 1] for x in range(MAIN)]
    pack_halo([kappas, maps], first_cols, first_corner_src)

    def open_up():
        pl.semaphore_wait(barrier, near)
        send_rows(0)
        send_halo(0, first_ext, first_cols, first_corner_src, first_corners)

    late = (o >= owners - max(1, owners // 4)) & (m >= members // 2)
    pl.when(late)(open_up)
    w = block_apply(lambda g: picks[g], None, True)
    for x in range(MAIN):
        w_ext[x, 0] = w[x]
    pack_halo([w], w_cols, w_corner_src)
    pl.when(jnp.logical_not(late))(open_up)
    send_halo(1, w_ext, w_cols, w_corner_src, w_corners)
    wait_halo(0, 2)
    for slot in range(SLOTS):
        if slot == CORNER:
            parts = [corner_rows(first_corners, f) for f in range(2)]
        else:
            parts = [first_ext[slot, f] for f in range(2)]
        kap[slot] = parts[0]
        if slot >= MAIN:
            amaps[slot] = (parts[1].astype(jnp.int32) + (LANES - 1)) & (LANES - 1)
    smeared = smear([kap[s] for s in range(SLOTS)])
    for x in range(MAIN):
        kt[x] = 8.0 * kap[x] + smeared[x]

    gathered = wait_rows(0)
    inverse = only_boxes(pltpu.roll(gathered, LANES - boxes, 1))
    guess = coarse_solve(only_boxes(gathered), inverse)

    def guess_rows(guess):
        picks = {}
        for do in (-1, 0, 1):
            for dm in (-1, 0, 1):
                wanted = me + do * members + dm
                picks[(do, dm)] = full(
                    jnp.sum(jnp.where(node == wanted, guess, 0.0), axis=0, keepdims=True)
                )
        return picks

    def coarse_parts(guess):
        picks_of = guess_rows(guess)
        result = []
        for x in range(MAIN):
            result.append(take(picks_of[(0, 0)], amaps[x]))
        for slot, way in ((XLO, (-1, 0)), (XHI, (1, 0)), (ZLO, (0, -1)), (ZHI, (0, 1))):
            result.append(take(picks_of[way], amaps[slot]))
        corner = zero
        for at, way in enumerate(((-1, -1), (-1, 1), (1, -1), (1, 1))):
            corner = jnp.where(sub == at, take(picks_of[way], amaps[CORNER]), corner)
        result.append(corner)
        return result

    def arrived(ring, ext, corners):
        wait_halo(ring, 1)
        return [ext[s, 0] for s in range(CORNER)] + [corner_rows(corners, 0)]

    def fine_operate(field, result):
        flat = smear(field)
        steep = smear([field[s] * kap[s] for s in range(SLOTS)])
        for x in range(MAIN):
            result[x] = field[x] * kt[x] - kap[x] * flat[x] - steep[x]

    coarse = coarse_parts(guess)
    z = [a + b for a, b in zip(arrived(1, w_ext, w_corners), coarse)]
    for slot in range(SLOTS):
        p_ext[slot] = z[slot]
    fine_operate(z, q_cur)
    image = [q_cur[x] for x in range(MAIN)]
    image_row = restrict(image)

    def send_image():
        put_row(1, image_row)
        send_rows(1)

    bq = solve(image, None, 0, send_image)
    for x in range(MAIN):
        b_ext[x, 0] = bq[x]
    pack_halo([bq], b_cols, b_corner_src)
    send_halo(2, b_ext, b_cols, b_corner_src, b_corners)
    r_dot_p = dot_of(r_ref, p_ext)
    p_dot_q = dot_of(p_ext, q_cur)
    coarse = coarse_parts(coarse_solve(only_boxes(wait_rows(1)), inverse))
    u = [a + b for a, b in zip(arrived(2, b_ext, b_corners), coarse)]
    for x in range(MAIN):
        u_ext[x] = u[x]
    fine_operate(u, v_cur)
    image = [v_cur[x] for x in range(MAIN)]
    row = restrict(image) + spread
    row = with_scalar(row, 0, r_dot_p)
    row = with_scalar(row, 1, p_dot_q)
    row = with_scalar(row, 2, dot_of(q_cur, u_ext))
    row = with_scalar(row, 3, dot_of(u_ext, v_cur))

    def send_moments():
        put_row(2, row)
        send_rows(2, True)

    def send_last(dot):
        put_row(3, full(dot))
        send_rows(3, True)

    bv = solve(image, send_last, groups // 4, send_moments)
    gathered = wait_rows(2, True)
    sums = jnp.sum(gathered, axis=0, keepdims=True)
    inverse = only_boxes(pltpu.roll(gathered, LANES - boxes, 1))
    source = only_boxes(gathered)
    guess = coarse_solve(source, inverse)
    coarse_part = full(total_of(source * guess) * (1.0 / restrict_scale))
    mu = [full(scalar(sums, number)) for number in range(4)]
    turn = 1.0 / mu[1]
    alpha0 = mu[0] * turn
    grow = alpha0 * mu[2] * turn
    curve = 1.0 / (alpha0 * alpha0 * mu[3] - grow * grow * mu[1])
    alpha1 = mu[0] * (grow - 1.0) * curve
    part = grow * grow * mu[2] - 2.0 * grow * alpha0 * mu[3] + alpha0 * alpha0 * coarse_part
    scale = alpha1 * curve
    own = full(jnp.sum(jnp.where(node == me, guess, 0.0), axis=0, keepdims=True))
    ahead, onward = [], []
    for x in range(MAIN):
        p0, q0, u0, v0 = p_ext[x], q_cur[x], u_ext[x], v_cur[x]
        t0 = bv[x] + take(own, amaps[x])
        p1 = grow * p0 - alpha0 * u0
        q1 = grow * q0 - alpha0 * v0
        x_out[x] = alpha0 * p0 + alpha1 * p1
        r_out[x] = r_ref[x] - alpha0 * q0 - alpha1 * q1
        ahead.append(p0 - alpha0 * u0 - alpha1 * (grow * u0 - alpha0 * t0))
        onward.append(p1)
    last = full(jnp.sum(wait_rows(3, True), axis=0, keepdims=True))
    beta1 = scale * (part + alpha0 * alpha0 * last) - 1.0
    for x in range(MAIN):
        p_out[x] = ahead[x] + beta1 * onward[x]


def emit(x_ref, r_ref, p_ref, x_out, r_out, p_out, sems):
    pairs = ((x_ref, x_out), (r_ref, r_out), (p_ref, p_out))
    copies = [pltpu.make_async_copy(a, b, sems.at[i]) for i, (a, b) in enumerate(pairs)]
    for copy in copies:
        copy.start()
    for copy in copies:
        copy.wait()


def shards(
    owners, members, right_side, coefficient_index, material_coefficients, block_cells,
    block_inverses, aggregate_map, coarse_diagonal,
):
    blocks, side = block_cells.shape[2], block_cells.shape[3]
    assert right_side.shape == (SUB, SUB, LANES) and side == LANES and blocks == SUB * SUB
    count = owners * members
    groups = blocks // SUB
    field = jax.ShapeDtypeStruct(right_side.shape, jnp.float32)
    vmem = pl.BlockSpec(memory_space=pltpu.VMEM)
    f32, i32 = jnp.float32, jnp.int32
    tile = (SUB, LANES)
    hbm = pl.BlockSpec(memory_space=pltpu.HBM)
    results = pl.pallas_call(
        functools.partial(kernel, owners, members),
        out_shape=(field, field, field),
        in_specs=[hbm] * 7,
        out_specs=(vmem, vmem, vmem),
        scratch_shapes=[
            pltpu.VMEM(right_side.shape, f32),
            pltpu.VMEM(right_side.shape, i32),
            pltpu.VMEM((1,) + material_coefficients.shape, f32),
            pltpu.VMEM((groups,) + tile, i32),
            pltpu.VMEM(right_side.shape, i32),
            pltpu.VMEM(coarse_diagonal.shape, f32),
            pltpu.SemaphoreType.DMA((6,)),
            pltpu.VMEM((blocks, side, side), f32),
            pltpu.VMEM((blocks // 2, 2 * side, side), jnp.bfloat16),
            pltpu.VMEM((blocks // 2, 2 * side, side), jnp.bfloat16),
            pltpu.VMEM((blocks,) + tile, f32),
            pltpu.VMEM((groups,) + tile, i32),
            pltpu.VMEM((groups,) + tile, i32),
            pltpu.VMEM((groups,) + tile, i32),
            pltpu.VMEM((groups,) + tile, i32),
            pltpu.VMEM((groups,) + tile, f32),
            pltpu.VMEM((CORNER, 2) + tile, f32),
            pltpu.VMEM((2, 2) + tile, f32),
            pltpu.VMEM((4,) + tile, f32),
            pltpu.VMEM((4,) + tile, f32),
            pltpu.VMEM((CORNER, 1) + tile, f32),
            pltpu.VMEM((2, 1) + tile, f32),
            pltpu.VMEM((4,) + tile, f32),
            pltpu.VMEM((4,) + tile, f32),
            pltpu.VMEM((CORNER, 1) + tile, f32),
            pltpu.VMEM((2, 1) + tile, f32),
            pltpu.VMEM((4,) + tile, f32),
            pltpu.VMEM((4,) + tile, f32),
            pltpu.VMEM((SLOTS,) + tile, f32),
            pltpu.VMEM((SLOTS,) + tile, i32),
            pltpu.VMEM((SLOTS,) + tile, f32),
            pltpu.VMEM((MAIN,) + tile, f32),
            pltpu.VMEM((MAIN,) + tile, f32),
            pltpu.VMEM((MAIN,) + tile, f32),
            pltpu.VMEM((MAIN,) + tile, f32),
            pltpu.VMEM((2,) + tile, f32),
            pltpu.VMEM((ROUNDS, 1, LANES), f32),
            pltpu.VMEM((ROUNDS, count, 1, LANES), f32),
            pltpu.VMEM((groups,) + tile, f32),
            pltpu.SemaphoreType.DMA((groups,)),
            pltpu.SemaphoreType.DMA((RINGS,)),
            pltpu.SemaphoreType.DMA((RINGS,)),
            pltpu.SemaphoreType.DMA((ROUNDS,)),
            pltpu.SemaphoreType.DMA((ROUNDS,)),
        ],
        compiler_params=pltpu.CompilerParams(
            collective_id=0, has_side_effects=True, vmem_limit_bytes=32 << 20,
        ),
    )(
        *(pltpu.with_memory_space_constraint(a, pltpu.HBM) for a in (
        right_side,
        coefficient_index,
        material_coefficients.reshape(1, -1),
        block_cells.reshape(groups, SUB, LANES),
        block_inverses.reshape(blocks, side, side),
        aggregate_map,
        coarse_diagonal,
        ))
    )
    return pl.pallas_call(
        emit,
        out_shape=(field, field, field),
        in_specs=[vmem] * 3,
        out_specs=(hbm,) * 3,
        scratch_shapes=[pltpu.SemaphoreType.DMA((3,))],
        compiler_params=pltpu.CompilerParams(vmem_limit_bytes=1 << 20),
    )(*results)


def solution(mesh):
    three = P("coarse", "fine", None)
    return jax.shard_map(
        functools.partial(shards, mesh.shape["coarse"], mesh.shape["fine"]),
        mesh=mesh,
        in_specs=(
            three,
            three,
            P(),
            P("coarse", "fine", None, None),
            P("coarse", "fine", None, None, None),
            three,
            three,
        ),
        out_specs=(three, three, three),
        check_vma=False,
    )
```

```python
import functools

import jax
import jax.numpy as jnp
from jax import lax
from jax.experimental import pallas as pl
from jax.experimental.pallas import tpu as pltpu
from jax.sharding import PartitionSpec as P

RINGS = 3
ROUNDS = 4
UNROLLED = 64
WORD = 32
SWEEPS = 4
omega = 0.8
restrict_scale = 0.25
MESH = pl.DeviceIdType.MESH
SUB = 8
LANES = 128
MAIN = 8
XLO, XHI, ZLO, ZHI, CORNER = 8, 9, 10, 11, 12
SLOTS = 13
DIRECTIONS = ((-1, 0), (1, 0), (0, -1), (0, 1), (-1, -1), (-1, 1), (1, -1), (1, 1))


def take(values, lanes):
    return jnp.take_along_axis(values, lanes, axis=1, mode="promise_in_bounds")


def full(row):
    return jnp.broadcast_to(row, (SUB, LANES))


def total_of(values):
    return jnp.sum(jnp.sum(values, axis=0, keepdims=True), axis=1, keepdims=True)


def kernel(
    owners, members, r_hbm, cidx_hbm, table_hbm, cells_hbm, inv_ref, amap_hbm, diag_hbm,
    x_out, r_out, p_out,
    r_ref, cidx_ref, table_ref, cells_ref, amap_ref, diag_ref, in_sems,
    mats, highs, lows, rot, key_in, lane_in, key_out, lane_out, moved,
    first_ext, first_cols, first_corner_src, first_corners,
    w_ext, w_cols, w_corner_src, w_corners,
    b_ext, b_cols, b_corner_src, b_corners,
    kap, amaps, p_ext, u_ext, q_cur, v_cur, kt, small,
    row_src, rows, picks,
    mat_sems, send_sems, recv_sems, row_send, row_recv,
):
    count = owners * members
    o = lax.axis_index("coarse")
    m = lax.axis_index("fine")
    me = o * members + m
    groups = cells_ref.shape[0]
    sub = lax.broadcasted_iota(jnp.int32, (SUB, LANES), 0)
    lane = lax.broadcasted_iota(jnp.int32, (SUB, LANES), 1)
    zero = jnp.zeros((SUB, LANES), jnp.float32)

    in_copies = [
        pltpu.make_async_copy(src, dst, in_sems.at[at])
        for at, (src, dst) in enumerate(
            (
                (cells_hbm, cells_ref),
                (r_hbm, r_ref),
                (amap_hbm, amap_ref),
                (cidx_hbm, cidx_ref),
                (table_hbm, table_ref),
                (diag_hbm, diag_ref),
            )
        )
    ]
    for copy in in_copies:
        copy.start()
    def mat_copy(u):
        part = pl.ds(u * SUB, SUB)
        return pltpu.make_async_copy(inv_ref.at[part], mats.at[part], mat_sems.at[u])

    for slot in range(MAIN, CORNER):
        for f in range(2):
            first_ext[slot, f] = zero
        w_ext[slot, 0] = zero
        b_ext[slot, 0] = zero
    for c in range(4):
        first_corners[c] = zero
        w_corners[c] = zero
        b_corners[c] = zero
    rows[...] = jnp.zeros(rows.shape, jnp.float32)

    barrier = pltpu.get_barrier_semaphore()
    step_o, step_m = -(-(owners - 1) // 3), -(-(members - 1) // 3)
    reach = max(SWEEPS - 1, max(step_o - 1, 0) + max(step_m - 1, 0))

    def height(away):
        return reach - max(abs(away) - 1, 0) + 1

    columns = [b for b in range(1 - members, members) if height(b) > 0]

    def near_of(o, m, least, most):
        total = -1
        for b in columns:
            size = most(o - height(b), 0, least(o + height(b), owners - 1))
            total = total + size * ((m + b >= 0) & (m + b < members))
        return total

    near = near_of(
        o, m, jnp.minimum, lambda low, zero, high: high - jnp.maximum(low, zero) + 1
    )
    near_counts = sorted(
        {
            near_of(at_o, at_m, min, lambda low, zero, high: high - max(low, zero) + 1)
            for at_o in range(owners)
            for at_m in range(members)
        }
    )

    def other(d):
        if count & (count - 1) or members & (members - 1):
            t = lax.rem(me + d, count)
            return {"coarse": lax.div(t, members), "fine": lax.rem(t, members)}
        t = (me + d) & (count - 1)
        return {
            "coarse": lax.shift_right_logical(t, members.bit_length() - 1),
            "fine": t & (members - 1),
        }

    def for_all(act):
        def one(t):
            device = {"coarse": t // members, "fine": t % members}
            pl.when(me != t)(functools.partial(act, device))

        if count <= UNROLLED:
            for t in range(count):
                one(t)
        else:

            def step(t, carry):
                one(t)
                return carry

            lax.fori_loop(0, count, step, 0)

    inside_m = {b: (m + b >= 0) & (m + b < members) for b in columns}

    def greet_near(midway):
        highest = min(reach + 1, owners - 1)
        for a in range(-highest, highest + 1):
            if a == 0:
                midway()
            inside_o = (o + a >= 0) & (o + a < owners)
            for b in columns:
                if (a or b) and abs(a) <= height(b):

                    @pl.when(inside_o & inside_m[b])
                    def _(a=a, b=b):
                        pl.semaphore_signal(
                            barrier, inc=1, device_id={"coarse": o + a, "fine": m + b},
                            device_id_type=MESH,
                        )

    def is_near(device):
        away_o, away_m = jnp.abs(device["coarse"] - o), jnp.abs(device["fine"] - m)
        return jnp.maximum(away_o - 1, 0) + jnp.maximum(away_m - 1, 0) <= reach

    def for_near(act):
        if count <= WORD:
            for d in range(1, count):
                pl.when((mask & (1 << (d - 1))) != 0)(functools.partial(act, other(d)))
        else:
            for_all(lambda device: pl.when(is_near(device))(functools.partial(act, device)))

    def load_matrices():
        for u in range(groups):
            mat_copy(u).start()

    greet_near(load_matrices)
    mask = jnp.int32(0)
    if count <= WORD:
        for d in range(1, count):
            mask = mask | (is_near(other(d)).astype(jnp.int32) << (d - 1))

    for copy in in_copies:
        copy.wait()

    def keys_of(source):
        row = lax.shift_right_logical(source, 7)
        turn = (jnp.bitwise_and(row, 7) - sub) & 7
        return jnp.bitwise_and(row, ~7) + turn, jnp.bitwise_and(source, 127)

    for g in range(groups):
        key, lanes = keys_of(cells_ref[g])
        key_in[g] = key
        lane_in[g] = lanes

    def load_turns(values):
        for g in range(len(values)):
            for turn in range(SUB):
                rot[g * SUB + turn] = (
                    values[g] if turn == 0 else pltpu.roll(values[g], SUB - turn, 0)
                )

    def permuted(key, lanes):
        parts = [zero, zero]
        for k in range(groups * SUB):
            parts[k % 2] = jnp.where(key == k, take(rot[k], lanes), parts[k % 2])
        return parts[0] + parts[1]

    both_lanes = 2 * LANES
    tall = lax.broadcasted_iota(jnp.int32, (groups * SUB, both_lanes), 0)
    taller = lax.broadcasted_iota(jnp.int32, (LANES, both_lanes), 0)
    place = lax.broadcasted_iota(jnp.int32, (groups * SUB, both_lanes), 1)
    second = jnp.where(place >= LANES, 1.0, 0.0)

    def narrow(values):
        return values.astype(jnp.float32).astype(jnp.bfloat16)

    tall, taller, place = narrow(tall), narrow(taller), narrow(place & (LANES - 1))
    one, nothing = jnp.bfloat16(1), jnp.bfloat16(0)
    parts = [jnp.zeros((2 * groups * SUB, LANES), jnp.float32)] * 2
    for g in range(groups):
        block = cells_ref[g]
        for b in range(0, SUB, 2):
            source = jnp.concatenate([block[b : b + 1, :], block[b + 1 : b + 2, :]], axis=1)
            row = narrow(lax.shift_right_logical(source, 7))
            hit = tall == jnp.broadcast_to(row, tall.shape)
            number = (second + (g * SUB + b)).astype(jnp.bfloat16)
            left = jnp.concatenate(
                [jnp.where(hit, number, nothing), jnp.where(hit, place, nothing)], axis=0
            )
            column = narrow(jnp.bitwise_and(source, LANES - 1))
            right = jnp.where(taller == jnp.broadcast_to(column, taller.shape), one, nothing)
            at = (b // 2) % 2
            parts[at] = parts[at] + lax.dot_general(
                left, right, (((1,), (1,)), ((), ())), preferred_element_type=jnp.float32
            )
    found = jnp.maximum(parts[0], parts[1]).astype(jnp.int32)
    for g in range(groups):
        block = found[g * SUB : (g + 1) * SUB]
        spot = found[(groups + g) * SUB : (groups + g + 1) * SUB]
        key, lanes = keys_of(block * LANES + spot)
        key_out[g] = key
        lane_out[g] = lanes

    small[...] = jnp.zeros(small.shape, jnp.float32)
    small[0, 0:1, 0 : table_ref.shape[1]] = table_ref[...]
    small[1, 0:1, 0 : diag_ref.shape[2]] = diag_ref[0]
    boxes = diag_ref.shape[2]
    table = full(small[0, 0:1, :])
    for x in range(MAIN):
        first_ext[x, 0] = take(table, cidx_ref[x])
        first_ext[x, 1] = (amap_ref[x] + 1).astype(jnp.float32)
        amaps[x] = amap_ref[x]

    def split(values):
        high = values.astype(jnp.bfloat16)
        low = (values - high.astype(jnp.float32)).astype(jnp.bfloat16)
        return high, low

    odd = (sub & 1) == 1

    def pick(values, keep):
        load_turns(values)
        for g in range(groups):
            keep[g] = permuted(key_in[g], lane_in[g])

    def block_apply(picked_of, done_with_dot, first=False, hook_at=None, hook=None):
        dot = zero
        picked = picked_of(0)
        for u in range(groups):
            if first and u % (groups // 2) == 0:
                for at in range(u, u + groups // 2):
                    mat_copy(at).wait()
            if first:
                for b in range(SUB):
                    high, low = split(mats[u * SUB + b])
                    pair, part = (u * SUB + b) // 2, pl.ds((b % 2) * LANES, LANES)
                    highs[pair, part] = high
                    lows[pair, part] = low
            upcoming = picked_of(u + 1) if u + 1 < groups else None
            if u == hook_at:
                hook()
            sides = []
            for keep_odd in (False, True):
                side = jnp.where(odd == keep_odd, picked, 0.0)
                sides.append(jnp.concatenate(split(side), axis=0))
            left = jnp.concatenate(sides, axis=1)
            product = zero
            for j in range(SUB // 2):
                pair = u * SUB // 2 + j
                right = jnp.concatenate([highs[pair], lows[pair]], axis=1)
                both = jnp.dot(left, right, preferred_element_type=jnp.float32)
                line = both[:SUB, :LANES] + (both[SUB:, :LANES] + both[:SUB, LANES:])
                line = line + both[SUB:, LANES:]
                product = jnp.where(lax.shift_right_logical(sub, 1) == j, line, product)
            moved[u] = product
            if done_with_dot is not None:
                dot = dot + picked * product
            picked = upcoming
        if done_with_dot is not None:
            done_with_dot(total_of(dot))
        load_turns([moved[g] for g in range(groups)])
        for g in range(groups):
            moved[g] = permuted(key_out[g], lane_out[g])
        return [moved[g] for g in range(groups)]

    def solve(values, done_with_dot, hook_at, hook):
        load_turns(values)
        return block_apply(
            lambda g: permuted(key_in[g], lane_in[g]), done_with_dot, False, hook_at, hook
        )

    base = lax.shift_right_logical(lane, 3)

    def restrict(values):
        sums = []
        for move in (-1, 0, 1):
            total = zero
            for x in range(MAIN):
                total = total + jnp.where(amaps[x] - base == move, values[x], 0.0)
            sums.append(total)
        total = pltpu.roll(sums[0], LANES - SUB, 1) + sums[1] + pltpu.roll(sums[2], SUB, 1)
        total = full(jnp.sum(total, axis=0, keepdims=True))
        for step in (1, 2, 4):
            total = total + pltpu.roll(total, LANES - step, 1)
        return jnp.where(lane < boxes, restrict_scale * take(total, (lane * SUB) & 127), 0.0)

    def row_copy(index, src, dst, device):
        return pltpu.make_async_remote_copy(
            src_ref=src, dst_ref=dst, send_sem=row_send.at[index], recv_sem=row_recv.at[index],
            device_id=device, device_id_type=MESH,
        )

    def put_row(index, row):
        row_src[index] = row[0:1, :]
        rows[index, me] = row[0:1, :]

    def send_rows(index, everywhere=False):
        (for_all if everywhere else for_near)(
            lambda device: row_copy(index, row_src.at[index], rows.at[index, me], device).start()
        )

    def wait_rows(index, everywhere=False):
        def wait_for(number):
            part = rows.at[index, pl.ds(0, number)]
            both = row_copy(index, part, part, other(1))
            both.wait_send()
            both.wait_recv()

        if everywhere:
            wait_for(count - 1)
        else:
            for number in near_counts:
                pl.when(near == number)(functools.partial(wait_for, number))
        return rows[index].reshape(count, LANES)

    def scalar(row, number):
        at = 2 * boxes + number
        return row[:, at : at + 1]

    def with_scalar(row, number, value):
        return jnp.where(lane == 2 * boxes + number, full(value), row)

    def edge_rows(values, z):
        result = zero
        for x in range(MAIN):
            result = jnp.where(sub == x, full(values[x][z : z + 1, :]), result)
        return result

    def halo_copies(ring, ext, cols, corner_src, corners):
        copies = []
        for do, dm in DIRECTIONS:
            if dm == 0:
                src = ext.at[MAIN - 1 if do == 1 else 0]
                dst = ext.at[XLO if do == 1 else XHI]
            elif do == 0:
                src = cols.at[1 if dm == 1 else 0]
                dst = ext.at[ZLO if dm == 1 else ZHI]
            else:
                at = 2 * (0 if do == 1 else 1) + (0 if dm == 1 else 1)
                src = corner_src.at[at]
                dst = corners.at[at]
            to_o, to_m = o + do, m + dm
            goes = (to_o >= 0) & (to_o < owners) & (to_m >= 0) & (to_m < members)
            copies.append(
                (
                    goes,
                    pltpu.make_async_remote_copy(
                        src_ref=src, dst_ref=dst,
                        send_sem=send_sems.at[ring], recv_sem=recv_sems.at[ring],
                        device_id={"coarse": to_o, "fine": to_m}, device_id_type=MESH,
                    ),
                )
            )
        return copies

    def pack_halo(fields, cols, corner_src):
        packs = [zero, zero, zero, zero]
        for f, values in enumerate(fields):
            cols[0, f] = edge_rows(values, 0)
            cols[1, f] = edge_rows(values, SUB - 1)
            for side_x in range(2):
                for side_z in range(2):
                    at = 2 * side_x + side_z
                    x = MAIN - 1 if side_x == 0 else 0
                    z = SUB - 1 if side_z == 0 else 0
                    packs[at] = jnp.where(sub == f, full(values[x][z : z + 1, :]), packs[at])
        for at in range(4):
            corner_src[at] = packs[at]

    def send_halo(ring, ext, cols, corner_src, corners):
        copies = halo_copies(ring, ext, cols, corner_src, corners)
        for goes, copy in copies:
            pl.when(goes)(copy.start)

    beside_o = (o > 0).astype(jnp.int32) + (o < owners - 1).astype(jnp.int32)
    beside_m = (m > 0).astype(jnp.int32) + (m < members - 1).astype(jnp.int32)

    def wait_halo(ring, fields):
        for number_o in range(3):
            for number_m in range(3):
                tiles = fields * (number_o + number_m) + number_o * number_m
                if tiles == 0:
                    continue

                @pl.when((beside_o == number_o) & (beside_m == number_m))
                def _(tiles=tiles):
                    part = rot.at[pl.ds(0, tiles)]
                    both = pltpu.make_async_remote_copy(
                        src_ref=part, dst_ref=part,
                        send_sem=send_sems.at[ring], recv_sem=recv_sems.at[ring],
                        device_id=other(1), device_id_type=MESH,
                    )
                    both.wait_send()
                    both.wait_recv()

    def corner_rows(corners, f):
        result = zero
        for at in range(4):
            result = jnp.where(sub == at, full(corners[at][f : f + 1, :]), result)
        return result

    def shifted(values, low, high):
        before = jnp.where(sub == 0, full(low), pltpu.roll(values, 1, 0))
        after = jnp.where(sub == SUB - 1, full(high), pltpu.roll(values, SUB - 1, 0))
        return values + 0.5 * (before + after)

    def smear(v):
        planes = [v[XLO]] + [v[x] for x in range(MAIN)] + [v[XHI]]
        corner = v[CORNER]
        low = shifted(v[ZLO], corner[0:1, :], corner[2:3, :])
        high = shifted(v[ZHI], corner[1:2, :], corner[3:4, :])
        result = []
        for x in range(MAIN):
            mid = planes[x + 1] + 0.5 * (planes[x] + planes[x + 2])
            mid = shifted(mid, low[x : x + 1, :], high[x : x + 1, :])
            before = jnp.where(lane == 0, 0.0, pltpu.roll(mid, 1, 1))
            after = jnp.where(lane == LANES - 1, 0.0, pltpu.roll(mid, LANES - 1, 1))
            result.append(mid + 0.5 * (before + after))
        return result

    node = lax.broadcasted_iota(jnp.int32, (count, LANES), 0)
    node_lane = lax.broadcasted_iota(jnp.int32, (count, LANES), 1)
    member = lax.rem(node, members)

    def coarse_solve(source, inverse):
        pull = omega * inverse
        push = source * pull
        guess = push
        for sweep in range(SWEEPS - 1):
            sides = pltpu.roll(guess, 1, 1) + pltpu.roll(guess, LANES - 1, 1)
            left = jnp.where(member == 0, 0.0, pltpu.roll(guess, 1, 0))
            right = jnp.where(member == members - 1, 0.0, pltpu.roll(guess, count - 1, 0))
            low = jnp.where(node < members, 0.0, pltpu.roll(guess, members, 0))
            high = jnp.where(
                node >= count - members, 0.0, pltpu.roll(guess, count - members, 0)
            )
            beside = sides + ((left + right) + (low + high))
            guess = ((1.0 - omega) * guess + push) + pull * beside
        return guess

    def only_boxes(values):
        return jnp.where(node_lane < boxes, values, 0.0)

    def dot_of(left, right):
        total = zero
        for x in range(MAIN):
            total = total + left[x] * right[x]
        return total_of(total)

    start = [r_ref[x] for x in range(MAIN)]
    spread = full(small[1, 0:1, :])
    spread = jnp.where(lane < boxes, 1.0 / jnp.where(lane < boxes, 6.0 + spread, 1.0), 0.0)
    spread = pltpu.roll(spread, boxes, 1)
    first_row = restrict(start) + spread
    pick(start, picks)
    put_row(0, first_row)
    kappas = [first_ext[x, 0] for x in range(MAIN)]
    maps = [first_ext[x, 1] for x in range(MAIN)]
    pack_halo([kappas, maps], first_cols, first_corner_src)

    def open_up():
        pl.semaphore_wait(barrier, near)
        send_rows(0)
        send_halo(0, first_ext, first_cols, first_corner_src, first_corners)

    late = o >= owners - max(1, owners // 4)
    pl.when(late)(open_up)
    w = block_apply(lambda g: picks[g], None, True)
    for x in range(MAIN):
        w_ext[x, 0] = w[x]
    pack_halo([w], w_cols, w_corner_src)
    pl.when(jnp.logical_not(late))(open_up)
    send_halo(1, w_ext, w_cols, w_corner_src, w_corners)
    wait_halo(0, 2)
    for slot in range(SLOTS):
        if slot == CORNER:
            parts = [corner_rows(first_corners, f) for f in range(2)]
        else:
            parts = [first_ext[slot, f] for f in range(2)]
        kap[slot] = parts[0]
        if slot >= MAIN:
            amaps[slot] = (parts[1].astype(jnp.int32) + (LANES - 1)) & (LANES - 1)
    smeared = smear([kap[s] for s in range(SLOTS)])
    for x in range(MAIN):
        kt[x] = 8.0 * kap[x] + smeared[x]

    gathered = wait_rows(0)
    inverse = only_boxes(pltpu.roll(gathered, LANES - boxes, 1))
    guess = coarse_solve(only_boxes(gathered), inverse)

    def guess_rows(guess):
        picks = {}
        for do in (-1, 0, 1):
            for dm in (-1, 0, 1):
                wanted = me + do * members + dm
                picks[(do, dm)] = full(
                    jnp.sum(jnp.where(node == wanted, guess, 0.0), axis=0, keepdims=True)
                )
        return picks

    def coarse_parts(guess):
        picks_of = guess_rows(guess)
        result = []
        for x in range(MAIN):
            result.append(take(picks_of[(0, 0)], amaps[x]))
        for slot, way in ((XLO, (-1, 0)), (XHI, (1, 0)), (ZLO, (0, -1)), (ZHI, (0, 1))):
            result.append(take(picks_of[way], amaps[slot]))
        corner = zero
        for at, way in enumerate(((-1, -1), (-1, 1), (1, -1), (1, 1))):
            corner = jnp.where(sub == at, take(picks_of[way], amaps[CORNER]), corner)
        result.append(corner)
        return result

    def arrived(ring, ext, corners):
        wait_halo(ring, 1)
        return [ext[s, 0] for s in range(CORNER)] + [corner_rows(corners, 0)]

    def fine_operate(field, result):
        flat = smear(field)
        steep = smear([field[s] * kap[s] for s in range(SLOTS)])
        for x in range(MAIN):
            result[x] = field[x] * kt[x] - kap[x] * flat[x] - steep[x]

    coarse = coarse_parts(guess)
    z = [a + b for a, b in zip(arrived(1, w_ext, w_corners), coarse)]
    for slot in range(SLOTS):
        p_ext[slot] = z[slot]
    fine_operate(z, q_cur)
    image = [q_cur[x] for x in range(MAIN)]
    image_row = restrict(image)

    def send_image():
        put_row(1, image_row)
        send_rows(1)

    bq = solve(image, None, 0, send_image)
    for x in range(MAIN):
        b_ext[x, 0] = bq[x]
    pack_halo([bq], b_cols, b_corner_src)
    send_halo(2, b_ext, b_cols, b_corner_src, b_corners)
    r_dot_p = dot_of(r_ref, p_ext)
    p_dot_q = dot_of(p_ext, q_cur)
    coarse = coarse_parts(coarse_solve(only_boxes(wait_rows(1)), inverse))
    u = [a + b for a, b in zip(arrived(2, b_ext, b_corners), coarse)]
    for x in range(MAIN):
        u_ext[x] = u[x]
    fine_operate(u, v_cur)
    image = [v_cur[x] for x in range(MAIN)]
    row = restrict(image) + spread
    row = with_scalar(row, 0, r_dot_p)
    row = with_scalar(row, 1, p_dot_q)
    row = with_scalar(row, 2, dot_of(q_cur, u_ext))
    row = with_scalar(row, 3, dot_of(u_ext, v_cur))

    def send_moments():
        put_row(2, row)
        send_rows(2, True)

    def send_last(dot):
        put_row(3, full(dot))
        send_rows(3, True)

    bv = solve(image, send_last, groups // 4, send_moments)
    gathered = wait_rows(2, True)
    sums = jnp.sum(gathered, axis=0, keepdims=True)
    inverse = only_boxes(pltpu.roll(gathered, LANES - boxes, 1))
    source = only_boxes(gathered)
    guess = coarse_solve(source, inverse)
    coarse_part = full(total_of(source * guess) * (1.0 / restrict_scale))
    mu = [full(scalar(sums, number)) for number in range(4)]
    turn = 1.0 / mu[1]
    alpha0 = mu[0] * turn
    grow = alpha0 * mu[2] * turn
    curve = 1.0 / (alpha0 * alpha0 * mu[3] - grow * grow * mu[1])
    alpha1 = mu[0] * (grow - 1.0) * curve
    part = grow * grow * mu[2] - 2.0 * grow * alpha0 * mu[3] + alpha0 * alpha0 * coarse_part
    scale = alpha1 * curve
    own = full(jnp.sum(jnp.where(node == me, guess, 0.0), axis=0, keepdims=True))
    ahead, onward = [], []
    for x in range(MAIN):
        p0, q0, u0, v0 = p_ext[x], q_cur[x], u_ext[x], v_cur[x]
        t0 = bv[x] + take(own, amaps[x])
        p1 = grow * p0 - alpha0 * u0
        q1 = grow * q0 - alpha0 * v0
        x_out[x] = alpha0 * p0 + alpha1 * p1
        r_out[x] = r_ref[x] - alpha0 * q0 - alpha1 * q1
        ahead.append(p0 - alpha0 * u0 - alpha1 * (grow * u0 - alpha0 * t0))
        onward.append(p1)
    last = full(jnp.sum(wait_rows(3, True), axis=0, keepdims=True))
    beta1 = scale * (part + alpha0 * alpha0 * last) - 1.0
    for x in range(MAIN):
        p_out[x] = ahead[x] + beta1 * onward[x]


def emit(x_ref, r_ref, p_ref, x_out, r_out, p_out, sems):
    pairs = ((x_ref, x_out), (r_ref, r_out), (p_ref, p_out))
    copies = [pltpu.make_async_copy(a, b, sems.at[i]) for i, (a, b) in enumerate(pairs)]
    for copy in copies:
        copy.start()
    for copy in copies:
        copy.wait()


def shards(
    owners, members, right_side, coefficient_index, material_coefficients, block_cells,
    block_inverses, aggregate_map, coarse_diagonal,
):
    blocks, side = block_cells.shape[2], block_cells.shape[3]
    assert right_side.shape == (SUB, SUB, LANES) and side == LANES and blocks == SUB * SUB
    count = owners * members
    groups = blocks // SUB
    field = jax.ShapeDtypeStruct(right_side.shape, jnp.float32)
    vmem = pl.BlockSpec(memory_space=pltpu.VMEM)
    f32, i32 = jnp.float32, jnp.int32
    tile = (SUB, LANES)
    hbm = pl.BlockSpec(memory_space=pltpu.HBM)
    results = pl.pallas_call(
        functools.partial(kernel, owners, members),
        out_shape=(field, field, field),
        in_specs=[hbm] * 7,
        out_specs=(vmem, vmem, vmem),
        scratch_shapes=[
            pltpu.VMEM(right_side.shape, f32),
            pltpu.VMEM(right_side.shape, i32),
            pltpu.VMEM((1,) + material_coefficients.shape, f32),
            pltpu.VMEM((groups,) + tile, i32),
            pltpu.VMEM(right_side.shape, i32),
            pltpu.VMEM(coarse_diagonal.shape, f32),
            pltpu.SemaphoreType.DMA((6,)),
            pltpu.VMEM((blocks, side, side), f32),
            pltpu.VMEM((blocks // 2, 2 * side, side), jnp.bfloat16),
            pltpu.VMEM((blocks // 2, 2 * side, side), jnp.bfloat16),
            pltpu.VMEM((blocks,) + tile, f32),
            pltpu.VMEM((groups,) + tile, i32),
            pltpu.VMEM((groups,) + tile, i32),
            pltpu.VMEM((groups,) + tile, i32),
            pltpu.VMEM((groups,) + tile, i32),
            pltpu.VMEM((groups,) + tile, f32),
            pltpu.VMEM((CORNER, 2) + tile, f32),
            pltpu.VMEM((2, 2) + tile, f32),
            pltpu.VMEM((4,) + tile, f32),
            pltpu.VMEM((4,) + tile, f32),
            pltpu.VMEM((CORNER, 1) + tile, f32),
            pltpu.VMEM((2, 1) + tile, f32),
            pltpu.VMEM((4,) + tile, f32),
            pltpu.VMEM((4,) + tile, f32),
            pltpu.VMEM((CORNER, 1) + tile, f32),
            pltpu.VMEM((2, 1) + tile, f32),
            pltpu.VMEM((4,) + tile, f32),
            pltpu.VMEM((4,) + tile, f32),
            pltpu.VMEM((SLOTS,) + tile, f32),
            pltpu.VMEM((SLOTS,) + tile, i32),
            pltpu.VMEM((SLOTS,) + tile, f32),
            pltpu.VMEM((MAIN,) + tile, f32),
            pltpu.VMEM((MAIN,) + tile, f32),
            pltpu.VMEM((MAIN,) + tile, f32),
            pltpu.VMEM((MAIN,) + tile, f32),
            pltpu.VMEM((2,) + tile, f32),
            pltpu.VMEM((ROUNDS, 1, LANES), f32),
            pltpu.VMEM((ROUNDS, count, 1, LANES), f32),
            pltpu.VMEM((groups,) + tile, f32),
            pltpu.SemaphoreType.DMA((groups,)),
            pltpu.SemaphoreType.DMA((RINGS,)),
            pltpu.SemaphoreType.DMA((RINGS,)),
            pltpu.SemaphoreType.DMA((ROUNDS,)),
            pltpu.SemaphoreType.DMA((ROUNDS,)),
        ],
        compiler_params=pltpu.CompilerParams(
            collective_id=0, has_side_effects=True, vmem_limit_bytes=32 << 20,
        ),
    )(
        *(pltpu.with_memory_space_constraint(a, pltpu.HBM) for a in (
        right_side,
        coefficient_index,
        material_coefficients.reshape(1, -1),
        block_cells.reshape(groups, SUB, LANES),
        block_inverses.reshape(blocks, side, side),
        aggregate_map,
        coarse_diagonal,
        ))
    )
    return pl.pallas_call(
        emit,
        out_shape=(field, field, field),
        in_specs=[vmem] * 3,
        out_specs=(hbm,) * 3,
        scratch_shapes=[pltpu.SemaphoreType.DMA((3,))],
        compiler_params=pltpu.CompilerParams(vmem_limit_bytes=1 << 20),
    )(*results)


def solution(mesh):
    three = P("coarse", "fine", None)
    return jax.shard_map(
        functools.partial(shards, mesh.shape["coarse"], mesh.shape["fine"]),
        mesh=mesh,
        in_specs=(
            three,
            three,
            P(),
            P("coarse", "fine", None, None),
            P("coarse", "fine", None, None, None),
            three,
            three,
        ),
        out_specs=(three, three, three),
        check_vma=False,
    )
```
